32 devices in a mesh: dp: 4 (over x, core), ctx: 8 (over z, y).
Axes of the slice: x: 2, y: 2, z: 4, core: 2. Of those that a mesh axis runs over, the one named last changes fastest.
Arguments:
- hidden_rows: bfloat16 [4096, 4096], P(('dp', 'ctx')), may hold values from -6 to 6
- query_rows: bfloat16 [4096, 2048], P(('dp', 'ctx')), may hold values from -17 to 17
- out_grad: bfloat16 [4096, 2048], P(('dp', 'ctx')), may hold values from -6 to 6
- projection: bfloat16 [1024, 4096], replicated, may hold values from -0.09375 to 0.09375
- packing_plan: int32 [32, 128], P(('dp', 'ctx')), may hold values from 0 to 127, each once within a row
- document_ids: int32 [4, 1024], P('dp'), may hold values from 0 to 7, never falling along the last dimension, each value on 1 to 768 neighbouring positions
Outputs:
- attended: bfloat16 [4096, 2048], P(('dp', 'ctx'))
- query_grad: bfloat16 [4096, 2048], P(('dp', 'ctx'))
- hidden_grad: bfloat16 [4096, 4096], P(('dp', 'ctx'))
- weight_grad: float32 [1024, 4096], P('dp', 'ctx')
The draws below stay inside these ranges and needn't reach their ends.
Inputs may be any that keep to these rules, and one draw needn't show every extreme that they name: `packing_plan`: each row holds every value once, so each device sends exactly 32 rows to each packed sequence. `document_ids`: never falling along a sequence; a document spans at most 768 positions, and some document exactly that many.
All inputs are finite; a program needn't handle non-finite values.
Results may differ from the reference program's by a relative error of at most 0.017.
The reference program's roundings to bfloat16 on the way (of `rounded`, `grad_score` and `projected_grad`) count: a program that leaves them out, or rounds other values in their place, can miss the bound.
Values may be sent and summed in bfloat16 or wider, within the bound.
No kernel may reach another device: no remote copies, remote signals or barrier semaphores. Data moves between devices by JAX's collectives and lax.ppermute only.
A program may use at most 64 MiB of HBM per device.

```python
import math
import jax
import jax.numpy as jnp
import numpy as np
from jax import lax

D = 4096
HEADS = 16
KV_HEADS = 4
HEAD_DIM = 128
S_DEV = 128
DOCS = 8
SEQS = 4
SPLIT = 8
SEQ_LEN = 1024
TOKENS = 4096
SEND = 32
KV_WIDTH = 1024


def draw_query_rows(key, part):
    array_shape = (TOKENS, HEADS * HEAD_DIM)
    normal = jax.random.normal(jax.random.fold_in(key, 23), array_shape, jnp.float32)
    return (jnp.clip(normal, -6.0, 6.0) * 2.0).astype(jnp.bfloat16)


def block_levels(own_key, extent, cuts, low, top_value):
    loudness, own = 1.0, jax.random.fold_in(own_key, 6)
    for position, shards_of in cuts:
        steps = jnp.exp(jax.random.uniform(jax.random.fold_in(own, position), (shards_of,), jnp.float32, low / len(cuts), top_value / len(cuts)))
        loudness = loudness * jnp.repeat(steps, extent[position] // shards_of).reshape([-1 if axis == position else 1 for axis in range(len(extent))])
    return loudness


def profile(count, total, limit, lean):
    weights = [(1 << 20) // math.isqrt(standing ** lean) + 1 for standing in range(2, count + 1)]
    rest, counts = total - limit - (count - 1), [1] * (count - 1)
    while rest > 0:
        free = [i for i in range(count - 1) if counts[i] < limit]
        mass, budget = sum([weights[i] for i in free]), rest
        for i in free:
            addition = min(limit - counts[i], max(1, budget * weights[i] // mass), rest)
            counts[i] = counts[i] + addition
            rest = rest - addition
    return np.array([limit] + counts)


def ragged(key, number_of, total, most, slope):
    if number_of == 2:
        one = jax.random.randint(key, (), max(1, total - most), min(most, total - 1) + 1)
        return jnp.stack([one, total - one])
    tallies = jnp.asarray(profile(number_of, total, most, slope), jnp.int32)
    twos = (number_of - 1) // 2
    giver, sink = tallies[1:1 + 2 * twos:2], tallies[2:2 + 2 * twos:2]
    slack = jnp.minimum(giver - 1, most - sink)
    passed = jax.random.randint(jax.random.fold_in(key, 1), (twos,), 0, 1 << 20) % (slack + 1)
    tallies = tallies.at[1:1 + 2 * twos:2].set(giver - passed).at[2:2 + 2 * twos:2].set(sink + passed)
    return tallies[jax.random.permutation(jax.random.fold_in(key, 2), number_of)]


def scatter_about(stream_key, shape, scale, reach, split=(), held_as=jnp.bfloat16):
    array = scale * jax.random.normal(stream_key, shape, jnp.float32)
    if split:
        array = array * block_levels(stream_key, shape, split, -0.22, 0.18)
    return jnp.clip(array, -reach, reach).astype(held_as)


def setup_inputs(seed: int = 0) -> dict:
    keys = jax.random.split(jax.random.key(seed), 7)
    hidden_rows = scatter_about(keys[0], (TOKENS, D), 1.0, 6.0, ((0, 32),))
    query_rows = draw_query_rows(jax.random.fold_in(keys[6], 71), 0)
    out_grad = scatter_about(keys[2], (TOKENS, HEADS * HEAD_DIM), 1.0, 6.0, ((0, 32),))
    projection = scatter_about(keys[3], (KV_WIDTH, D), D ** -0.5, 0.09375)
    packing_plan = jax.vmap(lambda own: jax.random.permutation(own, S_DEV))(jax.random.split(keys[4], (SEQS * SPLIT))).reshape((SEQS * SPLIT, S_DEV)).astype(jnp.int32)
    document_ids = jax.vmap(lambda own: jnp.searchsorted(jnp.cumsum(ragged(own, DOCS, SEQ_LEN, SEQ_LEN * 3 // 4, 2)), jnp.arange(SEQ_LEN), side="right"))(jax.random.split(keys[5], SEQS)).reshape((SEQS, SEQ_LEN)).astype(jnp.int32)
    return dict(hidden_rows=hidden_rows, query_rows=query_rows, out_grad=out_grad, projection=projection, packing_plan=packing_plan, document_ids=document_ids)


ROPE_BASE = 500000.0
MASK_VALUE = -1e30


def rotary_tables(positions, head_width):
    half_width = head_width // 2
    exponent = jnp.arange(half_width, dtype=jnp.float32) * (-2.0 * math.log(ROPE_BASE) / head_width)
    angles = positions.astype(jnp.float32)[:, None] * jnp.exp(exponent)[None, :]
    return jnp.cos(angles), jnp.sin(angles)


def rotate_forward(head_rows, cosine_table, sine_table):
    half_width = head_rows.shape[-1] // 2
    first_half = head_rows[..., :half_width]
    second_half = head_rows[..., half_width:]
    cosine_part = cosine_table[:, None, :]
    sine_part = sine_table[:, None, :]
    return jnp.concatenate([first_half * cosine_part - second_half * sine_part, second_half * cosine_part + first_half * sine_part], axis=-1)


def rotate_adjoint(head_grads, cosine_table, sine_table):
    half_width = head_grads.shape[-1] // 2
    first_half = head_grads[..., :half_width]
    second_half = head_grads[..., half_width:]
    cosine_part = cosine_table[:, None, :]
    sine_part = sine_table[:, None, :]
    return jnp.concatenate([first_half * cosine_part + second_half * sine_part, second_half * cosine_part - first_half * sine_part], axis=-1)


def inner_rows(left_side, right_side):
    return lax.dot_general(left_side, right_side, (((1,), (1,)), ((), ())), preferred_element_type=jnp.float32)


def outer_rows(left_side, right_side):
    return lax.dot_general(left_side, right_side, (((0,), (0,)), ((), ())), preferred_element_type=jnp.float32)


def block_terms(query_block, grad_block, key_rows, value_rows, query_index, query_document, key_document):
    score_scale = key_rows.shape[1] ** -0.5
    scores = inner_rows(query_block, key_rows) * score_scale
    key_index = jnp.arange(key_rows.shape[0], dtype=jnp.int32)
    allowed = (key_index[None, :] <= query_index[:, None]) & (key_document[None, :] == query_document[:, None])
    scores = jnp.where(allowed, scores, MASK_VALUE)
    row_max = jnp.max(scores, axis=1, keepdims=True)
    exponent = jnp.exp(scores - row_max)
    probability = exponent / jnp.sum(exponent, axis=1, keepdims=True)
    rounded = probability.astype(jnp.bfloat16)
    attended = jnp.dot(rounded, value_rows, preferred_element_type=jnp.float32).astype(jnp.bfloat16)
    grad_prob = inner_rows(grad_block, value_rows)
    delta_sum = jnp.sum(probability * grad_prob, axis=1, keepdims=True)
    grad_score = (probability * (grad_prob - delta_sum)).astype(jnp.bfloat16)
    query_grad = (jnp.dot(grad_score, key_rows, preferred_element_type=jnp.float32) * score_scale).astype(jnp.bfloat16)
    key_part = outer_rows(grad_score, query_block) * score_scale
    value_part = outer_rows(rounded, grad_block)
    return attended, query_grad, key_part, value_part


def reference(hidden_rows, query_rows, out_grad, projection, packing_plan, document_ids):
    block_ids = jnp.arange(SEQS * SPLIT, dtype=jnp.int32)
    sequence_of = (block_ids // SPLIT)[:, None]
    part_of = (block_ids % SPLIT)[:, None]
    targets = (packing_plan // SEND) * SEQ_LEN + part_of * S_DEV + sequence_of * SEND + packing_plan % SEND
    targets = targets.reshape(-1).astype(jnp.int32)
    packed_hidden = jnp.zeros_like(hidden_rows).at[targets].set(hidden_rows)
    packed_query = jnp.zeros_like(query_rows).at[targets].set(query_rows)
    projected = inner_rows(packed_hidden, projection)
    positions = jnp.arange(TOKENS, dtype=jnp.int32) % SEQ_LEN
    cosine_table, sine_table = rotary_tables(positions, HEAD_DIM)
    key_width = KV_HEADS * HEAD_DIM
    key_heads = rotate_forward(projected[:, :key_width].reshape(TOKENS, KV_HEADS, HEAD_DIM), cosine_table, sine_table).astype(jnp.bfloat16)
    values = projected[:, key_width:].reshape(TOKENS, KV_HEADS, HEAD_DIM).astype(jnp.bfloat16)
    query_heads = packed_query.reshape(SEQS, SEQ_LEN, HEADS, HEAD_DIM).transpose(0, 2, 1, 3).reshape(SEQS * HEADS, SEQ_LEN, HEAD_DIM)
    grad_heads = out_grad.reshape(SEQS, SEQ_LEN, HEADS, HEAD_DIM).transpose(0, 2, 1, 3).reshape(SEQS * HEADS, SEQ_LEN, HEAD_DIM)
    key_major = key_heads.reshape(SEQS, SEQ_LEN, KV_HEADS, HEAD_DIM).transpose(0, 2, 1, 3)
    value_major = values.reshape(SEQS, SEQ_LEN, KV_HEADS, HEAD_DIM).transpose(0, 2, 1, 3)
    group_size = HEADS // KV_HEADS
    query_index = jnp.arange(SEQ_LEN, dtype=jnp.int32)

    def one_head(pair_index):
        sequence = pair_index // HEADS
        group_index = (pair_index % HEADS) // group_size
        documents = document_ids[sequence]
        return block_terms(query_heads[pair_index], grad_heads[pair_index], key_major[sequence, group_index], value_major[sequence, group_index], query_index, documents, documents)

    attended_heads, query_grad_heads, key_parts, value_parts = lax.map(one_head, jnp.arange(SEQS * HEADS, dtype=jnp.int32))

    def to_rows(head_major):
        return head_major.reshape(SEQS, HEADS, SEQ_LEN, HEAD_DIM).transpose(0, 2, 1, 3).reshape(TOKENS, HEADS * HEAD_DIM)

    attended = to_rows(attended_heads)
    query_grad = to_rows(query_grad_heads)
    key_grad = key_parts.reshape(SEQS, KV_HEADS, group_size, SEQ_LEN, HEAD_DIM).sum(axis=2).astype(jnp.bfloat16)
    value_grad = value_parts.reshape(SEQS, KV_HEADS, group_size, SEQ_LEN, HEAD_DIM).sum(axis=2).astype(jnp.bfloat16)
    key_grad = key_grad.transpose(0, 2, 1, 3).reshape(TOKENS, KV_HEADS, HEAD_DIM)
    value_grad = value_grad.transpose(0, 2, 1, 3).reshape(TOKENS, key_width)
    key_back = rotate_adjoint(key_grad.astype(jnp.float32), cosine_table, sine_table).reshape(TOKENS, key_width)
    projected_grad = jnp.concatenate([key_back, value_grad.astype(jnp.float32)], axis=1).astype(jnp.bfloat16)
    hidden_grad = jnp.dot(projected_grad, projection, preferred_element_type=jnp.float32).astype(jnp.bfloat16)
    block_count = SEQS * SPLIT
    grad_blocks = projected_grad.reshape(block_count, S_DEV, KV_WIDTH)
    hidden_blocks = packed_hidden.reshape(block_count, S_DEV, D)

    def add_block(running_sum, block_pair):
        block_term = outer_rows(block_pair[0], block_pair[1]).astype(jnp.bfloat16)
        block_term = lax.optimization_barrier(block_term)
        return running_sum + block_term.astype(jnp.float32), None

    running_sum, unused = lax.scan(add_block, jnp.zeros((KV_WIDTH, D), jnp.float32), (grad_blocks, hidden_blocks))
    weight_grad = running_sum / SEQS
    return attended, query_grad, hidden_grad, weight_grad
```

```python
import functools
import math


import jax
import jax.numpy as jnp
from jax import lax
from jax.experimental import pallas as pl
from jax.experimental.pallas import tpu as pltpu
from jax.sharding import PartitionSpec as P

KV_HEADS = 4
HEAD_DIM = 128


ROPE_BASE = 500000.0
MASK_VALUE = -1e30


def rotary_tables(positions, head_width):
    half_width = head_width // 2
    exponent = jnp.arange(half_width, dtype=jnp.float32) * (-2.0 * math.log(ROPE_BASE) / head_width)
    angles = positions.astype(jnp.float32)[:, None] * jnp.exp(exponent)[None, :]
    return (jnp.cos(angles), jnp.sin(angles))


def rotate_forward(head_rows, cosine_table, sine_table):
    half_width = head_rows.shape[-1] // 2
    first_half = head_rows[..., :half_width]
    second_half = head_rows[..., half_width:]
    cosine_part = cosine_table[:, None, :]
    sine_part = sine_table[:, None, :]
    return jnp.concatenate(
        [
            first_half * cosine_part - second_half * sine_part,
            second_half * cosine_part + first_half * sine_part,
        ],
        axis=-1,
    )


def rotate_adjoint(head_grads, cosine_table, sine_table):
    half_width = head_grads.shape[-1] // 2
    first_half = head_grads[..., :half_width]
    second_half = head_grads[..., half_width:]
    cosine_part = cosine_table[:, None, :]
    sine_part = sine_table[:, None, :]
    return jnp.concatenate(
        [
            first_half * cosine_part + second_half * sine_part,
            second_half * cosine_part - first_half * sine_part,
        ],
        axis=-1,
    )


def inner_rows(left_side, right_side):
    return lax.dot_general(
        left_side, right_side, (((1,), (1,)), ((), ())), preferred_element_type=jnp.float32
    )


def outer_rows(left_side, right_side):
    return lax.dot_general(
        left_side, right_side, (((0,), (0,)), ((), ())), preferred_element_type=jnp.float32
    )


def block_terms(
    query_block, grad_block, key_rows, value_rows, query_index, query_document, key_document
):
    score_scale = key_rows.shape[1] ** (-0.5)
    scores = inner_rows(query_block, key_rows) * score_scale
    key_index = jnp.arange(key_rows.shape[0], dtype=jnp.int32)
    allowed = (key_index[None, :] <= query_index[:, None]) & (
        key_document[None, :] == query_document[:, None]
    )
    scores = jnp.where(allowed, scores, MASK_VALUE)
    row_max = jnp.max(scores, axis=1, keepdims=True)
    exponent = jnp.exp(scores - row_max)
    probability = exponent / jnp.sum(exponent, axis=1, keepdims=True)
    rounded = probability.astype(jnp.bfloat16)
    attended = jnp.dot(rounded, value_rows, preferred_element_type=jnp.float32).astype(jnp.bfloat16)
    grad_prob = inner_rows(grad_block, value_rows)
    delta_sum = jnp.sum(probability * grad_prob, axis=1, keepdims=True)
    grad_score = (probability * (grad_prob - delta_sum)).astype(jnp.bfloat16)
    query_grad = (
        jnp.dot(grad_score, key_rows, preferred_element_type=jnp.float32) * score_scale
    ).astype(jnp.bfloat16)
    key_part = outer_rows(grad_score, query_block) * score_scale
    value_part = outer_rows(rounded, grad_block)
    return (attended, query_grad, key_part, value_part)


def general_body(hidden_rows, query_rows, out_grad, projection, packing_plan, document_ids):
    row_count = hidden_rows.shape[0]
    split_size = lax.axis_size("ctx")
    part_index = lax.axis_index("ctx")
    sequences = lax.axis_size("dp")
    order_rows = jnp.argsort(packing_plan[0])
    send_hidden = jnp.take(hidden_rows, order_rows, axis=0)
    send_query = jnp.take(query_rows, order_rows, axis=0)
    packed_hidden, packed_query = (
        lax.all_to_all(send_hidden, "dp", split_axis=0, concat_axis=0, tiled=True),
        lax.all_to_all(send_query, "dp", split_axis=0, concat_axis=0, tiled=True),
    )
    projected = inner_rows(packed_hidden, projection)
    positions = part_index * row_count + jnp.arange(row_count, dtype=jnp.int32)
    cosine_table, sine_table = rotary_tables(positions, HEAD_DIM)
    key_width = KV_HEADS * HEAD_DIM
    key_heads = rotate_forward(
        projected[:, :key_width].reshape(row_count, KV_HEADS, HEAD_DIM), cosine_table, sine_table
    ).astype(jnp.bfloat16)
    values = projected[:, key_width:].reshape(row_count, KV_HEADS, HEAD_DIM).astype(jnp.bfloat16)
    repeats = split_size // KV_HEADS
    key_slots = jnp.repeat(key_heads, repeats, axis=1).reshape(row_count, split_size * HEAD_DIM)
    value_slots = jnp.repeat(values, repeats, axis=1).reshape(row_count, split_size * HEAD_DIM)
    local_query, local_keys, local_values = (
        lax.all_to_all(packed_query, "ctx", split_axis=1, concat_axis=0, tiled=True),
        lax.all_to_all(key_slots, "ctx", split_axis=1, concat_axis=0, tiled=True),
        lax.all_to_all(value_slots, "ctx", split_axis=1, concat_axis=0, tiled=True),
    )
    local_grad = lax.all_to_all(out_grad, "ctx", split_axis=1, concat_axis=0, tiled=True)
    length = local_query.shape[0]
    block_rows = math.gcd(length, 512)
    block_count = length // block_rows
    documents = document_ids[0]
    head_count = local_query.shape[1] // HEAD_DIM
    starts = jnp.arange(block_count, dtype=jnp.int32) * block_rows
    key_total = jnp.zeros((length, HEAD_DIM), jnp.float32)
    value_total = jnp.zeros((length, HEAD_DIM), jnp.float32)
    attended_parts = []
    query_parts = []
    for head_index in range(head_count):
        query_blocks = local_query[:, head_index * HEAD_DIM : (head_index + 1) * HEAD_DIM].reshape(
            block_count, block_rows, HEAD_DIM
        )
        grad_blocks = local_grad[:, head_index * HEAD_DIM : (head_index + 1) * HEAD_DIM].reshape(
            block_count, block_rows, HEAD_DIM
        )

        def block_step(carry_pair, inputs):
            query_block, grad_block, block_start = inputs
            query_index = block_start + jnp.arange(block_rows, dtype=jnp.int32)
            query_document = lax.dynamic_slice_in_dim(documents, block_start, block_rows)
            attended_block, query_block_grad, key_part, value_part = block_terms(
                query_block,
                grad_block,
                local_keys,
                local_values,
                query_index,
                query_document,
                documents,
            )
            return (
                (carry_pair[0] + key_part, carry_pair[1] + value_part),
                (attended_block, query_block_grad),
            )

        (key_total, value_total), (attended_blocks, query_grad_blocks) = lax.scan(
            block_step, (key_total, value_total), (query_blocks, grad_blocks, starts)
        )
        attended_parts.append(attended_blocks.reshape(length, HEAD_DIM))
        query_parts.append(query_grad_blocks.reshape(length, HEAD_DIM))
    local_attended = jnp.concatenate(attended_parts, axis=1)
    local_query_grad = jnp.concatenate(query_parts, axis=1)
    attended = lax.all_to_all(local_attended, "ctx", split_axis=0, concat_axis=1, tiled=True)
    query_grad = lax.all_to_all(local_query_grad, "ctx", split_axis=0, concat_axis=1, tiled=True)
    key_slots_grad, value_slots_grad = (
        lax.all_to_all(key_total, "ctx", split_axis=0, concat_axis=1, tiled=True),
        lax.all_to_all(value_total, "ctx", split_axis=0, concat_axis=1, tiled=True),
    )
    key_grad = (
        key_slots_grad.reshape(row_count, KV_HEADS, repeats, HEAD_DIM)
        .sum(axis=2)
        .astype(jnp.bfloat16)
    )
    value_grad = (
        value_slots_grad.reshape(row_count, KV_HEADS, repeats, HEAD_DIM)
        .sum(axis=2)
        .astype(jnp.bfloat16)
    )
    key_back = rotate_adjoint(key_grad.astype(jnp.float32), cosine_table, sine_table).reshape(
        row_count, key_width
    )
    projected_grad = jnp.concatenate(
        [key_back, value_grad.reshape(row_count, key_width).astype(jnp.float32)], axis=1
    ).astype(jnp.bfloat16)
    hidden_grad = jnp.dot(projected_grad, projection, preferred_element_type=jnp.float32).astype(
        jnp.bfloat16
    )
    block_term = outer_rows(projected_grad, packed_hidden)
    partial_sum = lax.psum_scatter(
        block_term.astype(jnp.bfloat16), "ctx", scatter_dimension=1, tiled=True
    ).astype(jnp.float32)
    weight_grad = lax.psum_scatter(partial_sum, "dp", scatter_dimension=0, tiled=True)
    weight_grad = weight_grad / sequences
    return (attended, query_grad, hidden_grad, weight_grad)


VMEM = pltpu.VMEM
SMEM = pltpu.SMEM


def vmem_specs(count):
    return [pl.BlockSpec(memory_space=VMEM)] * count


def pack_kernel(dp, ctx, plan_ref, hidden_ref, query_ref, cos_ref, sin_ref, proj_ref, qkv_ref, hid_ref, sorted_ref):
    step = pl.program_id(0)
    rows, width = hidden_ref.shape
    send = rows // dp
    pair = query_ref.shape[1] // ctx
    eighth = width // ctx

    @pl.when(step == 0)
    def _():
        slot = lax.broadcasted_iota(jnp.int32, (rows, rows), 0)
        select = (plan_ref[...] == slot).astype(jnp.bfloat16)
        for col in range(ctx):
            window = pl.ds(col * eighth, eighth)
            part = jnp.dot(select, hidden_ref[:, window], preferred_element_type=jnp.float32).astype(jnp.bfloat16)
            sorted_ref[:, window] = part
            for a in range(dp):
                hid_ref[a * ctx + col] = part[a * send : (a + 1) * send]
            part = jnp.dot(
                select, query_ref[:, pl.ds(col * pair, pair)], preferred_element_type=jnp.float32
            ).astype(jnp.bfloat16)
            for a in range(dp):
                qkv_ref[a * ctx + col, :, 0:pair] = part[a * send : (a + 1) * send]

    block = inner_rows(sorted_ref[...], proj_ref[...])
    heads = block.shape[1] // HEAD_DIM
    for which in range(2 * KV_HEADS // heads):

        @pl.when(step == which)
        def _(which=which):
            for t in range(heads):
                head = which * heads + t
                is_value, group = head // KV_HEADS, head % KV_HEADS
                start = pair + is_value * HEAD_DIM
                for a in range(dp):
                    x = block[a * send : (a + 1) * send, t * HEAD_DIM : (t + 1) * HEAD_DIM]
                    if not is_value:
                        x = x * cos_ref[...] + pltpu.roll(x, HEAD_DIM // 2, 1) * sin_ref[...]
                    x = x.astype(jnp.bfloat16)
                    for h in range(ctx // KV_HEADS):
                        qkv_ref[a * ctx + group * (ctx // KV_HEADS) + h, :, start : start + HEAD_DIM] = x


def pack_rows(dp, ctx, plan, hidden, query, cosine, sine, projection):
    rows, width = hidden.shape
    send = rows // dp
    pair = query.shape[1] // ctx
    proj_rows = 2 * HEAD_DIM
    steps = projection.shape[0] // proj_rows
    full = lambda shape: pl.BlockSpec(shape, lambda i: (0,) * len(shape))
    qkv_shape = (dp * ctx, send, pair + 2 * HEAD_DIM)
    hid_shape = (dp * ctx, send, width // ctx)
    return pl.pallas_call(
        functools.partial(pack_kernel, dp, ctx),
        grid=(steps,),
        in_specs=[
            full(plan.shape),
            full(hidden.shape),
            full(query.shape),
            full(cosine.shape),
            full(sine.shape),
            pl.BlockSpec((proj_rows, width), lambda i: (i, 0)),
        ],
        out_specs=[full(qkv_shape), full(hid_shape)],
        out_shape=[
            jax.ShapeDtypeStruct(qkv_shape, jnp.bfloat16),
            jax.ShapeDtypeStruct(hid_shape, jnp.bfloat16),
        ],
        scratch_shapes=[VMEM((rows, width), jnp.bfloat16)],
        cost_estimate=pl.CostEstimate(
            flops=2 * rows * width * projection.shape[0],
            bytes_accessed=2 * (projection.size + 2 * hidden.size + 2 * query.size),
            transcendentals=0,
        ),
        name="pack_rows",
    )(plan, hidden, query, cosine, sine, projection)


def attend_kernel(dp, ctx, which_ref, qkv_ref, grad_ref, row_doc_ref, col_doc_ref, out_ref, keep_ref, send_ref,
                  key_s, value_s, query_s, dk_s, dv_s):
    send = qkv_ref.shape[1]
    rows = grad_ref.shape[1]
    length = ctx * rows
    pair = grad_ref.shape[2]
    score_scale = HEAD_DIM ** (-0.5)
    power = score_scale * math.log2(math.e)
    for c in range(ctx):
        for s in range(dp):
            at = c * rows + s * send
            piece = s * ctx + c
            query_s[at : at + send, :] = qkv_ref[piece, :, 0:pair]
            key_s[at : at + send, :] = qkv_ref[piece, :, pair : pair + HEAD_DIM]
            value_s[at : at + send, :] = qkv_ref[piece, :, pair + HEAD_DIM : pair + 2 * HEAD_DIM]
    dk_s[...] = jnp.zeros_like(dk_s)
    dv_s[...] = jnp.zeros_like(dv_s)
    block = math.gcd(length, 2 * rows)
    per = block // rows
    for i in range(length // block):
        lo, hi = i * block, (i + 1) * block
        keys = key_s[0:hi, :]
        values = value_s[0:hi, :]
        key_index = lax.broadcasted_iota(jnp.int32, (block, hi), 1)
        query_index = lax.broadcasted_iota(jnp.int32, (block, hi), 0) + lo
        allowed = (key_index <= query_index) & (row_doc_ref[:, 0:hi] == col_doc_ref[lo:hi, :])
        for head in range(pair // HEAD_DIM):
            cols = slice(head * HEAD_DIM, (head + 1) * HEAD_DIM)
            query = query_s[lo:hi, cols]
            grad = jnp.concatenate([grad_ref[i * per + t, :, cols] for t in range(per)], axis=0)
            scores = jnp.where(allowed, inner_rows(query, keys), MASK_VALUE)
            row_max = jnp.max(scores, axis=1, keepdims=True)
            exponent = jnp.exp2((scores - row_max) * power)
            inverse = 1.0 / jnp.sum(exponent, axis=1, keepdims=True)
            probability = exponent * inverse
            rounded = probability.astype(jnp.bfloat16)
            attended = jnp.dot(rounded, values, preferred_element_type=jnp.float32).astype(jnp.bfloat16)
            weighted = inner_rows(grad, values) * probability
            delta = jnp.sum(weighted, axis=1, keepdims=True)
            grad_score = (weighted - probability * delta).astype(jnp.bfloat16)
            query_grad = (
                jnp.dot(grad_score, keys, preferred_element_type=jnp.float32) * score_scale
            ).astype(jnp.bfloat16)
            dk_s[0:hi, :] += outer_rows(grad_score, query)
            dv_s[0:hi, :] += outer_rows(rounded, grad)
            for t in range(per):
                out_ref[i * per + t, :, cols] = attended[t * rows : (t + 1) * rows]
                out_ref[i * per + t, :, pair + head * HEAD_DIM : pair + (head + 1) * HEAD_DIM] = query_grad[
                    t * rows : (t + 1) * rows
                ]
    which = which_ref[0]

    @pl.when(which == 0)
    def _():
        keep_ref[...] = dk_s[...] * score_scale
        send_ref[...] = dv_s[...].astype(send_ref.dtype)

    @pl.when(which != 0)
    def _():
        keep_ref[...] = dv_s[...]
        send_ref[...] = (dk_s[...] * score_scale).astype(send_ref.dtype)


def attend(dp, ctx, which, qkv, grad, documents):
    length = ctx * grad.shape[1]
    pair = grad.shape[2]
    out_shape = (ctx, grad.shape[1], 2 * pair)
    pairs = pair // HEAD_DIM * length * length // 2
    return pl.pallas_call(
        functools.partial(attend_kernel, dp, ctx),
        in_specs=[pl.BlockSpec(memory_space=SMEM)] + vmem_specs(4),
        out_specs=vmem_specs(3),
        out_shape=[
            jax.ShapeDtypeStruct(out_shape, jnp.bfloat16),
            jax.ShapeDtypeStruct((length, HEAD_DIM), jnp.float32),
            jax.ShapeDtypeStruct((length, HEAD_DIM), jnp.bfloat16),
        ],
        scratch_shapes=[
            VMEM((length, HEAD_DIM), jnp.bfloat16),
            VMEM((length, HEAD_DIM), jnp.bfloat16),
            VMEM((length, pair), jnp.bfloat16),
            VMEM((length, HEAD_DIM), jnp.float32),
            VMEM((length, HEAD_DIM), jnp.float32),
        ],
        cost_estimate=pl.CostEstimate(
            flops=10 * pairs * HEAD_DIM, bytes_accessed=2 * (qkv.size + 3 * grad.size), transcendentals=pairs
        ),
        name="attend",
    )(which, qkv, grad, documents, documents.reshape(length, 1))


def combine_kernel(dp, ctx, keep_ref, recv_ref, cos_ref, sin_ref, out_ref):
    length = keep_ref.shape[0]
    send = length // (dp * ctx)
    total = (keep_ref[...] + recv_ref[...].astype(jnp.float32)).astype(jnp.bfloat16).astype(jnp.float32)
    back = total * cos_ref[...] + pltpu.roll(total, HEAD_DIM // 2, 1) * sin_ref[...]
    back = back.astype(jnp.bfloat16)
    for c in range(ctx):
        for s in range(dp):
            at = (c * dp + s) * send
            to = (s * ctx + c) * send
            out_ref[to : to + send, :] = back[at : at + send]


def combine(dp, ctx, keep, recv, cosine, sine):
    return pl.pallas_call(
        functools.partial(combine_kernel, dp, ctx),
        in_specs=vmem_specs(4),
        out_specs=pl.BlockSpec(memory_space=VMEM),
        out_shape=jax.ShapeDtypeStruct(keep.shape, jnp.bfloat16),
        cost_estimate=pl.CostEstimate(flops=4 * keep.size, bytes_accessed=16 * keep.size, transcendentals=0),
        name="combine",
    )(keep, recv, cosine, sine)


def product_kernel(dp, ctx, index_ref, *refs):
    group, block_id, high = index_ref[0], index_ref[1], index_ref[2]
    grads = refs[:KV_HEADS]
    hid_refs = refs[KV_HEADS : KV_HEADS + 2]
    out_refs = refs[KV_HEADS + 2 : KV_HEADS + 2 + dp]
    own_ref, other_ref, heads_s = refs[KV_HEADS + 2 + dp :]
    length = grads[0].shape[0]
    send = length // (dp * ctx)
    for e in range(KV_HEADS):
        heads_s[jnp.bitwise_xor(group, e)] = grads[e][...]
    for s in range(dp):
        own = pl.ds(pl.multiple_of(s * ctx * send + block_id * send, send), send)
        other = pl.ds(pl.multiple_of(s * ctx * send + jnp.bitwise_xor(block_id, 1) * send, send), send)
        for head in range(KV_HEADS):
            cols = slice(head * HEAD_DIM, (head + 1) * HEAD_DIM)
            own_ref[s * send : (s + 1) * send, cols] = heads_s[head, own, :]
            other_ref[s * send : (s + 1) * send, cols] = heads_s[head, other, :]
    halves = dp // 2
    per = KV_HEADS // halves
    for ek in range(halves):
        first = jnp.bitwise_xor(high, ek) * per
        for t in range(per):
            left = heads_s[first + t]
            for ey in range(2):
                part = outer_rows(left, hid_refs[ey][...])
                out_refs[ek * 2 + ey][t * HEAD_DIM : (t + 1) * HEAD_DIM, :] = part.astype(jnp.bfloat16)


def product(dp, ctx, index, grads, hid_own, hid_other):
    length = grads[0].shape[0]
    columns = hid_own.shape[1]
    rows = length // ctx
    block = (2 * KV_HEADS * HEAD_DIM // dp, columns)
    return pl.pallas_call(
        functools.partial(product_kernel, dp, ctx),
        in_specs=[pl.BlockSpec(memory_space=SMEM)] + vmem_specs(KV_HEADS + 2),
        out_specs=vmem_specs(dp + 2),
        out_shape=[jax.ShapeDtypeStruct(block, jnp.bfloat16)] * dp
        + [jax.ShapeDtypeStruct((rows, KV_HEADS * HEAD_DIM), jnp.bfloat16)] * 2,
        scratch_shapes=[VMEM((KV_HEADS, length, HEAD_DIM), jnp.bfloat16)],
        cost_estimate=pl.CostEstimate(
            flops=4 * length * KV_HEADS * HEAD_DIM * columns,
            bytes_accessed=2 * (2 * length * columns + length * KV_HEADS * HEAD_DIM + 4 * columns * HEAD_DIM * KV_HEADS),
            transcendentals=0,
        ),
        name="weight_product",
    )(index, *grads, hid_own, hid_other)


def paired_body(hidden_rows, query_rows, out_grad, projection, packing_plan, document_ids):
    rows, width = hidden_rows.shape
    dp, ctx = lax.axis_size("dp"), lax.axis_size("ctx")
    a, c = lax.axis_index("dp"), lax.axis_index("ctx")
    group, side = c // 2, c % 2
    everyone = ("dp", "ctx")
    send = rows // dp
    length = rows * ctx
    pair = query_rows.shape[1] // ctx
    which = jnp.bitwise_xor(side, a % 2)

    def route(target):
        moves = []
        for i in range(dp):
            for j in range(ctx):
                to_dp, to_ctx = target(i, j)
                moves.append((i * ctx + j, to_dp * ctx + to_ctx))
        return moves

    def move(value, target):
        return lax.ppermute(value, everyone, route(target))

    grad_pieces = out_grad.reshape(rows, ctx, pair).transpose(1, 0, 2)
    grad_heads = lax.all_to_all(grad_pieces, "ctx", split_axis=0, concat_axis=0, tiled=True)

    slot = c * rows + a * send + jnp.arange(send, dtype=jnp.int32)
    cosine, sine = rotary_tables(slot, HEAD_DIM)
    qkv_pieces, hid_pieces = pack_rows(
        dp, ctx, packing_plan, hidden_rows, query_rows,
        jnp.concatenate([cosine, cosine], axis=1), jnp.concatenate([-sine, sine], axis=1), projection,
    )
    qkv = lax.all_to_all(qkv_pieces, everyone, split_axis=0, concat_axis=0, tiled=True)
    hid = lax.all_to_all(hid_pieces, everyone, split_axis=0, concat_axis=0, tiled=True)
    hid_own = hid.reshape(length, width // ctx)
    hid_other = move(hid_own, lambda i, j: (i, j ^ 1))

    outputs, keep, give = attend(dp, ctx, which.reshape(1), qkv, grad_heads, document_ids)
    recv = move(give, lambda i, j: (i, j ^ 1))
    cosine, sine = rotary_tables(jnp.arange(length, dtype=jnp.int32), HEAD_DIM)
    cosine = jnp.where(which == 0, jnp.concatenate([cosine, cosine], axis=1), 1.0)
    sine = jnp.where(which == 0, jnp.concatenate([sine, -sine], axis=1), 0.0)
    piece = combine(dp, ctx, keep, recv, cosine, sine)
    grads = [piece] + [move(piece, lambda i, j, e=e: (i, j ^ (2 * e))) for e in range(1, KV_HEADS)]

    index = jnp.stack([group, c, a // 2]).astype(jnp.int32)
    products = product(dp, ctx, index, grads, hid_own, hid_other)
    blocks = []
    half = dp // 2
    for ek in range(half):
        for ey in range(2):
            blocks.append(
                move(
                    products[ek * 2 + ey],
                    lambda i, j, ek=ek, ey=ey: (((j % 2) ^ (i % 2)) * half + ((i // 2) ^ ek), j ^ ey),
                )
            )
    weight_grad = functools.reduce(jnp.add, [b.astype(jnp.float32) for b in blocks]) / dp

    own_rows, other_rows = products[dp], products[dp + 1]
    other_half = move(other_rows, lambda i, j: (i, j ^ 1))
    first = jnp.where(which == 0, own_rows, other_half)
    second = jnp.where(which == 0, other_half, own_rows)
    projected_grad = jnp.concatenate([first, second], axis=1)
    hidden_grad = jnp.dot(projected_grad, projection, preferred_element_type=jnp.float32).astype(jnp.bfloat16)

    back = lax.all_to_all(outputs, "ctx", split_axis=0, concat_axis=0, tiled=True)
    back = back.transpose(1, 0, 2)
    attended = back[:, :, :pair].reshape(rows, ctx * pair)
    query_grad = back[:, :, pair:].reshape(rows, ctx * pair)
    return (attended, query_grad, hidden_grad, weight_grad)


def body_for(mesh):
    dp, ctx = mesh.shape["dp"], mesh.shape["ctx"]
    if ctx == 2 * KV_HEADS and dp in (2, 4, 8):
        return paired_body
    return general_body


def solution(mesh):
    in_specs = (
        P(("dp", "ctx"), None),
        P(("dp", "ctx"), None),
        P(("dp", "ctx"), None),
        P(),
        P(("dp", "ctx"), None),
        P("dp", None),
    )
    out_specs = (
        P(("dp", "ctx"), None),
        P(("dp", "ctx"), None),
        P(("dp", "ctx"), None),
        P("dp", "ctx"),
    )
    return jax.shard_map(body_for(mesh), mesh=mesh, in_specs=in_specs, out_specs=out_specs, check_vma=False)
```

```python
import functools
import math


import jax
import jax.numpy as jnp
from jax import lax
from jax.experimental import pallas as pl
from jax.experimental.pallas import tpu as pltpu
from jax.sharding import PartitionSpec as P

KV_HEADS = 4
HEAD_DIM = 128


ROPE_BASE = 500000.0
MASK_VALUE = -1e30


def rotary_tables(positions, head_width):
    half_width = head_width // 2
    exponent = jnp.arange(half_width, dtype=jnp.float32) * (-2.0 * math.log(ROPE_BASE) / head_width)
    angles = positions.astype(jnp.float32)[:, None] * jnp.exp(exponent)[None, :]
    return (jnp.cos(angles), jnp.sin(angles))


def rotate_forward(head_rows, cosine_table, sine_table):
    half_width = head_rows.shape[-1] // 2
    first_half = head_rows[..., :half_width]
    second_half = head_rows[..., half_width:]
    cosine_part = cosine_table[:, None, :]
    sine_part = sine_table[:, None, :]
    return jnp.concatenate(
        [
            first_half * cosine_part - second_half * sine_part,
            second_half * cosine_part + first_half * sine_part,
        ],
        axis=-1,
    )


def rotate_adjoint(head_grads, cosine_table, sine_table):
    half_width = head_grads.shape[-1] // 2
    first_half = head_grads[..., :half_width]
    second_half = head_grads[..., half_width:]
    cosine_part = cosine_table[:, None, :]
    sine_part = sine_table[:, None, :]
    return jnp.concatenate(
        [
            first_half * cosine_part + second_half * sine_part,
            second_half * cosine_part - first_half * sine_part,
        ],
        axis=-1,
    )


def inner_rows(left_side, right_side):
    return lax.dot_general(
        left_side, right_side, (((1,), (1,)), ((), ())), preferred_element_type=jnp.float32
    )


def outer_rows(left_side, right_side):
    return lax.dot_general(
        left_side, right_side, (((0,), (0,)), ((), ())), preferred_element_type=jnp.float32
    )


def block_terms(
    query_block, grad_block, key_rows, value_rows, query_index, query_document, key_document
):
    score_scale = key_rows.shape[1] ** (-0.5)
    scores = inner_rows(query_block, key_rows) * score_scale
    key_index = jnp.arange(key_rows.shape[0], dtype=jnp.int32)
    allowed = (key_index[None, :] <= query_index[:, None]) & (
        key_document[None, :] == query_document[:, None]
    )
    scores = jnp.where(allowed, scores, MASK_VALUE)
    row_max = jnp.max(scores, axis=1, keepdims=True)
    exponent = jnp.exp(scores - row_max)
    probability = exponent / jnp.sum(exponent, axis=1, keepdims=True)
    rounded = probability.astype(jnp.bfloat16)
    attended = jnp.dot(rounded, value_rows, preferred_element_type=jnp.float32).astype(jnp.bfloat16)
    grad_prob = inner_rows(grad_block, value_rows)
    delta_sum = jnp.sum(probability * grad_prob, axis=1, keepdims=True)
    grad_score = (probability * (grad_prob - delta_sum)).astype(jnp.bfloat16)
    query_grad = (
        jnp.dot(grad_score, key_rows, preferred_element_type=jnp.float32) * score_scale
    ).astype(jnp.bfloat16)
    key_part = outer_rows(grad_score, query_block) * score_scale
    value_part = outer_rows(rounded, grad_block)
    return (attended, query_grad, key_part, value_part)


def general_body(hidden_rows, query_rows, out_grad, projection, packing_plan, document_ids):
    row_count = hidden_rows.shape[0]
    split_size = lax.axis_size("ctx")
    part_index = lax.axis_index("ctx")
    sequences = lax.axis_size("dp")
    order_rows = jnp.argsort(packing_plan[0])
    send_hidden = jnp.take(hidden_rows, order_rows, axis=0)
    send_query = jnp.take(query_rows, order_rows, axis=0)
    packed_hidden, packed_query = (
        lax.all_to_all(send_hidden, "dp", split_axis=0, concat_axis=0, tiled=True),
        lax.all_to_all(send_query, "dp", split_axis=0, concat_axis=0, tiled=True),
    )
    projected = inner_rows(packed_hidden, projection)
    positions = part_index * row_count + jnp.arange(row_count, dtype=jnp.int32)
    cosine_table, sine_table = rotary_tables(positions, HEAD_DIM)
    key_width = KV_HEADS * HEAD_DIM
    key_heads = rotate_forward(
        projected[:, :key_width].reshape(row_count, KV_HEADS, HEAD_DIM), cosine_table, sine_table
    ).astype(jnp.bfloat16)
    values = projected[:, key_width:].reshape(row_count, KV_HEADS, HEAD_DIM).astype(jnp.bfloat16)
    repeats = split_size // KV_HEADS
    key_slots = jnp.repeat(key_heads, repeats, axis=1).reshape(row_count, split_size * HEAD_DIM)
    value_slots = jnp.repeat(values, repeats, axis=1).reshape(row_count, split_size * HEAD_DIM)
    local_query, local_keys, local_values = (
        lax.all_to_all(packed_query, "ctx", split_axis=1, concat_axis=0, tiled=True),
        lax.all_to_all(key_slots, "ctx", split_axis=1, concat_axis=0, tiled=True),
        lax.all_to_all(value_slots, "ctx", split_axis=1, concat_axis=0, tiled=True),
    )
    local_grad = lax.all_to_all(out_grad, "ctx", split_axis=1, concat_axis=0, tiled=True)
    length = local_query.shape[0]
    block_rows = math.gcd(length, 512)
    block_count = length // block_rows
    documents = document_ids[0]
    head_count = local_query.shape[1] // HEAD_DIM
    starts = jnp.arange(block_count, dtype=jnp.int32) * block_rows
    key_total = jnp.zeros((length, HEAD_DIM), jnp.float32)
    value_total = jnp.zeros((length, HEAD_DIM), jnp.float32)
    attended_parts = []
    query_parts = []
    for head_index in range(head_count):
        query_blocks = local_query[:, head_index * HEAD_DIM : (head_index + 1) * HEAD_DIM].reshape(
            block_count, block_rows, HEAD_DIM
        )
        grad_blocks = local_grad[:, head_index * HEAD_DIM : (head_index + 1) * HEAD_DIM].reshape(
            block_count, block_rows, HEAD_DIM
        )

        def block_step(carry_pair, inputs):
            query_block, grad_block, block_start = inputs
            query_index = block_start + jnp.arange(block_rows, dtype=jnp.int32)
            query_document = lax.dynamic_slice_in_dim(documents, block_start, block_rows)
            attended_block, query_block_grad, key_part, value_part = block_terms(
                query_block,
                grad_block,
                local_keys,
                local_values,
                query_index,
                query_document,
                documents,
            )
            return (
                (carry_pair[0] + key_part, carry_pair[1] + value_part),
                (attended_block, query_block_grad),
            )

        (key_total, value_total), (attended_blocks, query_grad_blocks) = lax.scan(
            block_step, (key_total, value_total), (query_blocks, grad_blocks, starts)
        )
        attended_parts.append(attended_blocks.reshape(length, HEAD_DIM))
        query_parts.append(query_grad_blocks.reshape(length, HEAD_DIM))
    local_attended = jnp.concatenate(attended_parts, axis=1)
    local_query_grad = jnp.concatenate(query_parts, axis=1)
    attended = lax.all_to_all(local_attended, "ctx", split_axis=0, concat_axis=1, tiled=True)
    query_grad = lax.all_to_all(local_query_grad, "ctx", split_axis=0, concat_axis=1, tiled=True)
    key_slots_grad, value_slots_grad = (
        lax.all_to_all(key_total, "ctx", split_axis=0, concat_axis=1, tiled=True),
        lax.all_to_all(value_total, "ctx", split_axis=0, concat_axis=1, tiled=True),
    )
    key_grad = (
        key_slots_grad.reshape(row_count, KV_HEADS, repeats, HEAD_DIM)
        .sum(axis=2)
        .astype(jnp.bfloat16)
    )
    value_grad = (
        value_slots_grad.reshape(row_count, KV_HEADS, repeats, HEAD_DIM)
        .sum(axis=2)
        .astype(jnp.bfloat16)
    )
    key_back = rotate_adjoint(key_grad.astype(jnp.float32), cosine_table, sine_table).reshape(
        row_count, key_width
    )
    projected_grad = jnp.concatenate(
        [key_back, value_grad.reshape(row_count, key_width).astype(jnp.float32)], axis=1
    ).astype(jnp.bfloat16)
    hidden_grad = jnp.dot(projected_grad, projection, preferred_element_type=jnp.float32).astype(
        jnp.bfloat16
    )
    block_term = outer_rows(projected_grad, packed_hidden)
    partial_sum = lax.psum_scatter(
        block_term.astype(jnp.bfloat16), "ctx", scatter_dimension=1, tiled=True
    ).astype(jnp.float32)
    weight_grad = lax.psum_scatter(partial_sum, "dp", scatter_dimension=0, tiled=True)
    weight_grad = weight_grad / sequences
    return (attended, query_grad, hidden_grad, weight_grad)


VMEM = pltpu.VMEM
SMEM = pltpu.SMEM


def vmem_specs(count):
    return [pl.BlockSpec(memory_space=VMEM)] * count


def pack_kernel(dp, ctx, plan_ref, hidden_ref, query_ref, cos_ref, sin_ref, proj_ref, qkv_ref, hid_ref, sorted_ref):
    step = pl.program_id(0)
    rows, width = hidden_ref.shape
    send = rows // dp
    pair = query_ref.shape[1] // ctx
    eighth = width // ctx

    @pl.when(step == 0)
    def _():
        slot = lax.broadcasted_iota(jnp.int32, (rows, rows), 0)
        select = (plan_ref[...] == slot).astype(jnp.bfloat16)
        for col in range(ctx):
            window = pl.ds(col * eighth, eighth)
            part = jnp.dot(select, hidden_ref[:, window], preferred_element_type=jnp.float32).astype(jnp.bfloat16)
            sorted_ref[:, window] = part
            for a in range(dp):
                hid_ref[a * ctx + col] = part[a * send : (a + 1) * send]
            part = jnp.dot(
                select, query_ref[:, pl.ds(col * pair, pair)], preferred_element_type=jnp.float32
            ).astype(jnp.bfloat16)
            for a in range(dp):
                qkv_ref[a * ctx + col, :, 0:pair] = part[a * send : (a + 1) * send]

    block = inner_rows(sorted_ref[...], proj_ref[...])
    heads = block.shape[1] // HEAD_DIM
    for which in range(2 * KV_HEADS // heads):

        @pl.when(step == which)
        def _(which=which):
            for t in range(heads):
                head = which * heads + t
                is_value, group = head // KV_HEADS, head % KV_HEADS
                start = pair + is_value * HEAD_DIM
                for a in range(dp):
                    x = block[a * send : (a + 1) * send, t * HEAD_DIM : (t + 1) * HEAD_DIM]
                    if not is_value:
                        x = x * cos_ref[...] + pltpu.roll(x, HEAD_DIM // 2, 1) * sin_ref[...]
                    x = x.astype(jnp.bfloat16)
                    for h in range(ctx // KV_HEADS):
                        qkv_ref[a * ctx + group * (ctx // KV_HEADS) + h, :, start : start + HEAD_DIM] = x


def pack_rows(dp, ctx, plan, hidden, query, cosine, sine, projection):
    rows, width = hidden.shape
    send = rows // dp
    pair = query.shape[1] // ctx
    proj_rows = 2 * HEAD_DIM
    steps = projection.shape[0] // proj_rows
    full = lambda shape: pl.BlockSpec(shape, lambda i: (0,) * len(shape))
    qkv_shape = (dp * ctx, send, pair + 2 * HEAD_DIM)
    hid_shape = (dp * ctx, send, width // ctx)
    return pl.pallas_call(
        functools.partial(pack_kernel, dp, ctx),
        grid=(steps,),
        in_specs=[
            full(plan.shape),
            full(hidden.shape),
            full(query.shape),
            full(cosine.shape),
            full(sine.shape),
            pl.BlockSpec((proj_rows, width), lambda i: (i, 0)),
        ],
        out_specs=[full(qkv_shape), full(hid_shape)],
        out_shape=[
            jax.ShapeDtypeStruct(qkv_shape, jnp.bfloat16),
            jax.ShapeDtypeStruct(hid_shape, jnp.bfloat16),
        ],
        scratch_shapes=[VMEM((rows, width), jnp.bfloat16)],
        cost_estimate=pl.CostEstimate(
            flops=2 * rows * width * projection.shape[0],
            bytes_accessed=2 * (projection.size + 2 * hidden.size + 2 * query.size),
            transcendentals=0,
        ),
        name="pack_rows",
    )(plan, hidden, query, cosine, sine, projection)


def attend_kernel(dp, ctx, which_ref, qkv_ref, grad_ref, row_doc_ref, col_doc_ref, out_ref, keep_ref, send_ref,
                  key_s, value_s, query_s, dk_s, dv_s):
    send = qkv_ref.shape[1]
    rows = grad_ref.shape[1]
    length = ctx * rows
    pair = grad_ref.shape[2]
    score_scale = HEAD_DIM ** (-0.5)
    power = score_scale * math.log2(math.e)
    for c in range(ctx):
        for s in range(dp):
            at = c * rows + s * send
            piece = s * ctx + c
            query_s[at : at + send, :] = qkv_ref[piece, :, 0:pair]
            key_s[at : at + send, :] = qkv_ref[piece, :, pair : pair + HEAD_DIM]
            value_s[at : at + send, :] = qkv_ref[piece, :, pair + HEAD_DIM : pair + 2 * HEAD_DIM]
    dk_s[...] = jnp.zeros_like(dk_s)
    dv_s[...] = jnp.zeros_like(dv_s)
    block = math.gcd(length, 2 * rows)
    per = block // rows
    for i in range(length // block):
        lo, hi = i * block, (i + 1) * block
        keys = key_s[0:hi, :]
        values = value_s[0:hi, :]
        key_index = lax.broadcasted_iota(jnp.int32, (block, hi), 1)
        query_index = lax.broadcasted_iota(jnp.int32, (block, hi), 0) + lo
        allowed = (key_index <= query_index) & (row_doc_ref[:, 0:hi] == col_doc_ref[lo:hi, :])
        for head in range(pair // HEAD_DIM):
            cols = slice(head * HEAD_DIM, (head + 1) * HEAD_DIM)
            query = query_s[lo:hi, cols]
            grad = jnp.concatenate([grad_ref[i * per + t, :, cols] for t in range(per)], axis=0)
            scores = jnp.where(allowed, inner_rows(query, keys), MASK_VALUE)
            row_max = jnp.max(scores, axis=1, keepdims=True)
            exponent = jnp.exp2((scores - row_max) * power)
            inverse = 1.0 / jnp.sum(exponent, axis=1, keepdims=True)
            probability = exponent * inverse
            rounded = probability.astype(jnp.bfloat16)
            attended = jnp.dot(rounded, values, preferred_element_type=jnp.float32).astype(jnp.bfloat16)
            weighted = inner_rows(grad, values) * probability
            delta = jnp.sum(weighted, axis=1, keepdims=True)
            grad_score = (weighted - probability * delta).astype(jnp.bfloat16)
            query_grad = (
                jnp.dot(grad_score, keys, preferred_element_type=jnp.float32) * score_scale
            ).astype(jnp.bfloat16)
            dk_s[0:hi, :] += outer_rows(grad_score, query)
            dv_s[0:hi, :] += outer_rows(rounded, grad)
            for t in range(per):
                out_ref[i * per + t, :, cols] = attended[t * rows : (t + 1) * rows]
                out_ref[i * per + t, :, pair + head * HEAD_DIM : pair + (head + 1) * HEAD_DIM] = query_grad[
                    t * rows : (t + 1) * rows
                ]
    which = which_ref[0]

    @pl.when(which == 0)
    def _():
        keep_ref[...] = dk_s[...] * score_scale
        send_ref[...] = dv_s[...].astype(send_ref.dtype)

    @pl.when(which != 0)
    def _():
        keep_ref[...] = dv_s[...]
        send_ref[...] = (dk_s[...] * score_scale).astype(send_ref.dtype)


def attend(dp, ctx, which, qkv, grad, documents):
    length = ctx * grad.shape[1]
    pair = grad.shape[2]
    out_shape = (ctx, grad.shape[1], 2 * pair)
    pairs = pair // HEAD_DIM * length * length // 2
    return pl.pallas_call(
        functools.partial(attend_kernel, dp, ctx),
        in_specs=[pl.BlockSpec(memory_space=SMEM)] + vmem_specs(4),
        out_specs=vmem_specs(3),
        out_shape=[
            jax.ShapeDtypeStruct(out_shape, jnp.bfloat16),
            jax.ShapeDtypeStruct((length, HEAD_DIM), jnp.float32),
            jax.ShapeDtypeStruct((length, HEAD_DIM), jnp.bfloat16),
        ],
        scratch_shapes=[
            VMEM((length, HEAD_DIM), jnp.bfloat16),
            VMEM((length, HEAD_DIM), jnp.bfloat16),
            VMEM((length, pair), jnp.bfloat16),
            VMEM((length, HEAD_DIM), jnp.float32),
            VMEM((length, HEAD_DIM), jnp.float32),
        ],
        cost_estimate=pl.CostEstimate(
            flops=10 * pairs * HEAD_DIM, bytes_accessed=2 * (qkv.size + 3 * grad.size), transcendentals=pairs
        ),
        name="attend",
    )(which, qkv, grad, documents, documents.reshape(length, 1))


def combine_kernel(dp, ctx, keep_ref, recv_ref, cos_ref, sin_ref, out_ref):
    length = keep_ref.shape[0]
    send = length // (dp * ctx)
    total = (keep_ref[...] + recv_ref[...].astype(jnp.float32)).astype(jnp.bfloat16).astype(jnp.float32)
    back = total * cos_ref[...] + pltpu.roll(total, HEAD_DIM // 2, 1) * sin_ref[...]
    back = back.astype(jnp.bfloat16)
    for c in range(ctx):
        for s in range(dp):
            at = (c * dp + s) * send
            to = (s * ctx + c) * send
            out_ref[to : to + send, :] = back[at : at + send]


def combine(dp, ctx, keep, recv, cosine, sine):
    return pl.pallas_call(
        functools.partial(combine_kernel, dp, ctx),
        in_specs=vmem_specs(4),
        out_specs=pl.BlockSpec(memory_space=VMEM),
        out_shape=jax.ShapeDtypeStruct(keep.shape, jnp.bfloat16),
        cost_estimate=pl.CostEstimate(flops=4 * keep.size, bytes_accessed=16 * keep.size, transcendentals=0),
        name="combine",
    )(keep, recv, cosine, sine)


def product_kernel(dp, ctx, index_ref, *refs):
    group, block_id, high = index_ref[0], index_ref[1], index_ref[2]
    grads = refs[:KV_HEADS]
    hid_refs = refs[KV_HEADS : KV_HEADS + 2]
    out_refs = refs[KV_HEADS + 2 : KV_HEADS + 2 + dp]
    own_ref, other_ref, heads_s = refs[KV_HEADS + 2 + dp :]
    length = grads[0].shape[0]
    send = length // (dp * ctx)
    for e in range(KV_HEADS):
        heads_s[jnp.bitwise_xor(group, e)] = grads[e][...]
    for s in range(dp):
        own = pl.ds(pl.multiple_of(s * ctx * send + block_id * send, send), send)
        other = pl.ds(pl.multiple_of(s * ctx * send + jnp.bitwise_xor(block_id, 1) * send, send), send)
        for head in range(KV_HEADS):
            cols = slice(head * HEAD_DIM, (head + 1) * HEAD_DIM)
            own_ref[s * send : (s + 1) * send, cols] = heads_s[head, own, :]
            other_ref[s * send : (s + 1) * send, cols] = heads_s[head, other, :]
    halves = dp // 2
    per = KV_HEADS // halves
    for ek in range(halves):
        first = jnp.bitwise_xor(high, ek) * per
        for t in range(per):
            left = heads_s[first + t]
            for ey in range(2):
                part = outer_rows(left, hid_refs[ey][...])
                out_refs[ek * 2 + ey][t * HEAD_DIM : (t + 1) * HEAD_DIM, :] = part.astype(jnp.bfloat16)


def product(dp, ctx, index, grads, hid_own, hid_other):
    length = grads[0].shape[0]
    columns = hid_own.shape[1]
    rows = length // ctx
    block = (2 * KV_HEADS * HEAD_DIM // dp, columns)
    return pl.pallas_call(
        functools.partial(product_kernel, dp, ctx),
        in_specs=[pl.BlockSpec(memory_space=SMEM)] + vmem_specs(KV_HEADS + 2),
        out_specs=vmem_specs(dp + 2),
        out_shape=[jax.ShapeDtypeStruct(block, jnp.bfloat16)] * dp
        + [jax.ShapeDtypeStruct((rows, KV_HEADS * HEAD_DIM), jnp.bfloat16)] * 2,
        scratch_shapes=[VMEM((KV_HEADS, length, HEAD_DIM), jnp.bfloat16)],
        cost_estimate=pl.CostEstimate(
            flops=4 * length * KV_HEADS * HEAD_DIM * columns,
            bytes_accessed=2 * (2 * length * columns + length * KV_HEADS * HEAD_DIM + 4 * columns * HEAD_DIM * KV_HEADS),
            transcendentals=0,
        ),
        name="weight_product",
    )(index, *grads, hid_own, hid_other)


def split_kernel(in_ref, out_ref):
    width = out_ref.shape[2]
    for j in range(out_ref.shape[0]):
        out_ref[j] = in_ref[:, j * width : (j + 1) * width]


def split_columns(array, parts):
    rows, width = array.shape
    return pl.pallas_call(
        split_kernel,
        in_specs=vmem_specs(1),
        out_specs=pl.BlockSpec(memory_space=VMEM),
        out_shape=jax.ShapeDtypeStruct((parts, rows, width // parts), array.dtype),
        cost_estimate=pl.CostEstimate(flops=0, bytes_accessed=4 * array.size, transcendentals=0),
        name="split_columns",
    )(array)


def join_kernel(in_ref, *out_refs):
    width = in_ref.shape[2] // len(out_refs)
    for j in range(in_ref.shape[0]):
        for k, out_ref in enumerate(out_refs):
            out_ref[:, j * width : (j + 1) * width] = in_ref[j, :, k * width : (k + 1) * width]


def join_columns(array, outs):
    parts, rows, width = array.shape
    return pl.pallas_call(
        join_kernel,
        in_specs=vmem_specs(1),
        out_specs=vmem_specs(outs),
        out_shape=[jax.ShapeDtypeStruct((rows, parts * width // outs), array.dtype)] * outs,
        cost_estimate=pl.CostEstimate(flops=0, bytes_accessed=4 * array.size, transcendentals=0),
        name="join_columns",
    )(array)


def paired_body(hidden_rows, query_rows, out_grad, projection, packing_plan, document_ids):
    rows, width = hidden_rows.shape
    dp, ctx = lax.axis_size("dp"), lax.axis_size("ctx")
    a, c = lax.axis_index("dp"), lax.axis_index("ctx")
    group, side = c // 2, c % 2
    everyone = ("dp", "ctx")
    send = rows // dp
    length = rows * ctx
    pair = query_rows.shape[1] // ctx
    which = jnp.bitwise_xor(side, a % 2)

    def route(target):
        moves = []
        for i in range(dp):
            for j in range(ctx):
                to_dp, to_ctx = target(i, j)
                moves.append((i * ctx + j, to_dp * ctx + to_ctx))
        return moves

    def move(value, target):
        return lax.ppermute(value, everyone, route(target))

    grad_pieces = split_columns(out_grad, ctx)
    grad_heads = lax.all_to_all(grad_pieces, "ctx", split_axis=0, concat_axis=0, tiled=True)

    slot = c * rows + a * send + jnp.arange(send, dtype=jnp.int32)
    cosine, sine = rotary_tables(slot, HEAD_DIM)
    qkv_pieces, hid_pieces = pack_rows(
        dp, ctx, packing_plan, hidden_rows, query_rows,
        jnp.concatenate([cosine, cosine], axis=1), jnp.concatenate([-sine, sine], axis=1), projection,
    )
    grad_heads, qkv_pieces = lax.optimization_barrier((grad_heads, qkv_pieces))
    qkv = lax.all_to_all(qkv_pieces, everyone, split_axis=0, concat_axis=0, tiled=True)
    qkv, hid_pieces = lax.optimization_barrier((qkv, hid_pieces))
    hid = lax.all_to_all(hid_pieces, everyone, split_axis=0, concat_axis=0, tiled=True)

    outputs, keep, give = attend(dp, ctx, which.reshape(1), qkv, grad_heads, document_ids)
    recv = move(give, lambda i, j: (i, j ^ 1))
    cosine, sine = rotary_tables(jnp.arange(length, dtype=jnp.int32), HEAD_DIM)
    cosine = jnp.where(which == 0, jnp.concatenate([cosine, cosine], axis=1), 1.0)
    sine = jnp.where(which == 0, jnp.concatenate([sine, -sine], axis=1), 0.0)
    piece = combine(dp, ctx, keep, recv, cosine, sine)
    piece, hid = lax.optimization_barrier((piece, hid))
    hid_own = hid.reshape(length, width // ctx)
    hid_other = move(hid_own, lambda i, j: (i, j ^ 1))
    grads = [piece] + [move(piece, lambda i, j, e=e: (i, j ^ (2 * e))) for e in range(1, KV_HEADS)]

    outputs, *grads = lax.optimization_barrier((outputs, *grads))
    back = lax.all_to_all(outputs, "ctx", split_axis=0, concat_axis=0, tiled=True)
    index = jnp.stack([group, c, a // 2]).astype(jnp.int32)
    products = product(dp, ctx, index, grads, hid_own, hid_other)
    blocks = []
    half = dp // 2
    for ek in range(half):
        for ey in range(2):
            blocks.append(
                move(
                    products[ek * 2 + ey],
                    lambda i, j, ek=ek, ey=ey: (((j % 2) ^ (i % 2)) * half + ((i // 2) ^ ek), j ^ ey),
                )
            )
    weight_grad = functools.reduce(jnp.add, [b.astype(jnp.float32) for b in blocks]) / dp

    own_rows, other_rows = products[dp], products[dp + 1]
    other_half = move(other_rows, lambda i, j: (i, j ^ 1))
    first = jnp.where(which == 0, own_rows, other_half)
    second = jnp.where(which == 0, other_half, own_rows)
    projected_grad = jnp.concatenate([first, second], axis=1)
    hidden_grad = jnp.dot(projected_grad, projection, preferred_element_type=jnp.float32).astype(jnp.bfloat16)

    back, hidden_grad = lax.optimization_barrier((back, hidden_grad))
    attended, query_grad = join_columns(back, 2)
    return (attended, query_grad, hidden_grad, weight_grad)


def body_for(mesh):
    dp, ctx = mesh.shape["dp"], mesh.shape["ctx"]
    if ctx == 2 * KV_HEADS and dp in (2, 4, 8):
        return paired_body
    return general_body


def solution(mesh):
    in_specs = (
        P(("dp", "ctx"), None),
        P(("dp", "ctx"), None),
        P(("dp", "ctx"), None),
        P(),
        P(("dp", "ctx"), None),
        P("dp", None),
    )
    out_specs = (
        P(("dp", "ctx"), None),
        P(("dp", "ctx"), None),
        P(("dp", "ctx"), None),
        P("dp", "ctx"),
    )
    return jax.shard_map(body_for(mesh), mesh=mesh, in_specs=in_specs, out_specs=out_specs, check_vma=False)
```

```python
import functools
import math

import jax
import jax.numpy as jnp
from jax import lax
from jax.experimental import pallas as pl
from jax.experimental.pallas import tpu as pltpu
from jax.sharding import Mesh, PartitionSpec as P

KV_HEADS = 4
HEAD_DIM = 128


ROPE_BASE = 500000.0
MASK_VALUE = -1e30


def rotary_tables(positions, head_width):
    half_width = head_width // 2
    exponent = jnp.arange(half_width, dtype=jnp.float32) * (-2.0 * math.log(ROPE_BASE) / head_width)
    angles = positions.astype(jnp.float32)[:, None] * jnp.exp(exponent)[None, :]
    return (jnp.cos(angles), jnp.sin(angles))


def rotate_forward(head_rows, cosine_table, sine_table):
    half_width = head_rows.shape[-1] // 2
    first_half = head_rows[..., :half_width]
    second_half = head_rows[..., half_width:]
    cosine_part = cosine_table[:, None, :]
    sine_part = sine_table[:, None, :]
    return jnp.concatenate(
        [
            first_half * cosine_part - second_half * sine_part,
            second_half * cosine_part + first_half * sine_part,
        ],
        axis=-1,
    )


def rotate_adjoint(head_grads, cosine_table, sine_table):
    half_width = head_grads.shape[-1] // 2
    first_half = head_grads[..., :half_width]
    second_half = head_grads[..., half_width:]
    cosine_part = cosine_table[:, None, :]
    sine_part = sine_table[:, None, :]
    return jnp.concatenate(
        [
            first_half * cosine_part + second_half * sine_part,
            second_half * cosine_part - first_half * sine_part,
        ],
        axis=-1,
    )


def inner_rows(left_side, right_side):
    return lax.dot_general(
        left_side, right_side, (((1,), (1,)), ((), ())), preferred_element_type=jnp.float32
    )


def outer_rows(left_side, right_side):
    return lax.dot_general(
        left_side, right_side, (((0,), (0,)), ((), ())), preferred_element_type=jnp.float32
    )


def block_terms(
    query_block, grad_block, key_rows, value_rows, query_index, query_document, key_document
):
    score_scale = key_rows.shape[1] ** (-0.5)
    scores = inner_rows(query_block, key_rows) * score_scale
    key_index = jnp.arange(key_rows.shape[0], dtype=jnp.int32)
    allowed = (key_index[None, :] <= query_index[:, None]) & (
        key_document[None, :] == query_document[:, None]
    )
    scores = jnp.where(allowed, scores, MASK_VALUE)
    row_max = jnp.max(scores, axis=1, keepdims=True)
    exponent = jnp.exp(scores - row_max)
    probability = exponent / jnp.sum(exponent, axis=1, keepdims=True)
    rounded = probability.astype(jnp.bfloat16)
    attended = jnp.dot(rounded, value_rows, preferred_element_type=jnp.float32).astype(jnp.bfloat16)
    grad_prob = inner_rows(grad_block, value_rows)
    delta_sum = jnp.sum(probability * grad_prob, axis=1, keepdims=True)
    grad_score = (probability * (grad_prob - delta_sum)).astype(jnp.bfloat16)
    query_grad = (
        jnp.dot(grad_score, key_rows, preferred_element_type=jnp.float32) * score_scale
    ).astype(jnp.bfloat16)
    key_part = outer_rows(grad_score, query_block) * score_scale
    value_part = outer_rows(rounded, grad_block)
    return (attended, query_grad, key_part, value_part)


def general_body(hidden_rows, query_rows, out_grad, projection, packing_plan, document_ids):
    row_count = hidden_rows.shape[0]
    split_size = lax.axis_size("ctx")
    part_index = lax.axis_index("ctx")
    sequences = lax.axis_size("dp")
    order_rows = jnp.argsort(packing_plan[0])
    send_hidden = jnp.take(hidden_rows, order_rows, axis=0)
    send_query = jnp.take(query_rows, order_rows, axis=0)
    packed_hidden, packed_query = (
        lax.all_to_all(send_hidden, "dp", split_axis=0, concat_axis=0, tiled=True),
        lax.all_to_all(send_query, "dp", split_axis=0, concat_axis=0, tiled=True),
    )
    projected = inner_rows(packed_hidden, projection)
    positions = part_index * row_count + jnp.arange(row_count, dtype=jnp.int32)
    cosine_table, sine_table = rotary_tables(positions, HEAD_DIM)
    key_width = KV_HEADS * HEAD_DIM
    key_heads = rotate_forward(
        projected[:, :key_width].reshape(row_count, KV_HEADS, HEAD_DIM), cosine_table, sine_table
    ).astype(jnp.bfloat16)
    values = projected[:, key_width:].reshape(row_count, KV_HEADS, HEAD_DIM).astype(jnp.bfloat16)
    repeats = split_size // KV_HEADS
    key_slots = jnp.repeat(key_heads, repeats, axis=1).reshape(row_count, split_size * HEAD_DIM)
    value_slots = jnp.repeat(values, repeats, axis=1).reshape(row_count, split_size * HEAD_DIM)
    local_query, local_keys, local_values = (
        lax.all_to_all(packed_query, "ctx", split_axis=1, concat_axis=0, tiled=True),
        lax.all_to_all(key_slots, "ctx", split_axis=1, concat_axis=0, tiled=True),
        lax.all_to_all(value_slots, "ctx", split_axis=1, concat_axis=0, tiled=True),
    )
    local_grad = lax.all_to_all(out_grad, "ctx", split_axis=1, concat_axis=0, tiled=True)
    length = local_query.shape[0]
    block_rows = math.gcd(length, 512)
    block_count = length // block_rows
    documents = document_ids[0]
    head_count = local_query.shape[1] // HEAD_DIM
    starts = jnp.arange(block_count, dtype=jnp.int32) * block_rows
    key_total = jnp.zeros((length, HEAD_DIM), jnp.float32)
    value_total = jnp.zeros((length, HEAD_DIM), jnp.float32)
    attended_parts = []
    query_parts = []
    for head_index in range(head_count):
        query_blocks = local_query[:, head_index * HEAD_DIM : (head_index + 1) * HEAD_DIM].reshape(
            block_count, block_rows, HEAD_DIM
        )
        grad_blocks = local_grad[:, head_index * HEAD_DIM : (head_index + 1) * HEAD_DIM].reshape(
            block_count, block_rows, HEAD_DIM
        )

        def block_step(carry_pair, inputs):
            query_block, grad_block, block_start = inputs
            query_index = block_start + jnp.arange(block_rows, dtype=jnp.int32)
            query_document = lax.dynamic_slice_in_dim(documents, block_start, block_rows)
            attended_block, query_block_grad, key_part, value_part = block_terms(
                query_block,
                grad_block,
                local_keys,
                local_values,
                query_index,
                query_document,
                documents,
            )
            return (
                (carry_pair[0] + key_part, carry_pair[1] + value_part),
                (attended_block, query_block_grad),
            )

        (key_total, value_total), (attended_blocks, query_grad_blocks) = lax.scan(
            block_step, (key_total, value_total), (query_blocks, grad_blocks, starts)
        )
        attended_parts.append(attended_blocks.reshape(length, HEAD_DIM))
        query_parts.append(query_grad_blocks.reshape(length, HEAD_DIM))
    local_attended = jnp.concatenate(attended_parts, axis=1)
    local_query_grad = jnp.concatenate(query_parts, axis=1)
    attended = lax.all_to_all(local_attended, "ctx", split_axis=0, concat_axis=1, tiled=True)
    query_grad = lax.all_to_all(local_query_grad, "ctx", split_axis=0, concat_axis=1, tiled=True)
    key_slots_grad, value_slots_grad = (
        lax.all_to_all(key_total, "ctx", split_axis=0, concat_axis=1, tiled=True),
        lax.all_to_all(value_total, "ctx", split_axis=0, concat_axis=1, tiled=True),
    )
    key_grad = (
        key_slots_grad.reshape(row_count, KV_HEADS, repeats, HEAD_DIM)
        .sum(axis=2)
        .astype(jnp.bfloat16)
    )
    value_grad = (
        value_slots_grad.reshape(row_count, KV_HEADS, repeats, HEAD_DIM)
        .sum(axis=2)
        .astype(jnp.bfloat16)
    )
    key_back = rotate_adjoint(key_grad.astype(jnp.float32), cosine_table, sine_table).reshape(
        row_count, key_width
    )
    projected_grad = jnp.concatenate(
        [key_back, value_grad.reshape(row_count, key_width).astype(jnp.float32)], axis=1
    ).astype(jnp.bfloat16)
    hidden_grad = jnp.dot(projected_grad, projection, preferred_element_type=jnp.float32).astype(
        jnp.bfloat16
    )
    block_term = outer_rows(projected_grad, packed_hidden)
    partial_sum = lax.psum_scatter(
        block_term.astype(jnp.bfloat16), "ctx", scatter_dimension=1, tiled=True
    ).astype(jnp.float32)
    weight_grad = lax.psum_scatter(partial_sum, "dp", scatter_dimension=0, tiled=True)
    weight_grad = weight_grad / sequences
    return (attended, query_grad, hidden_grad, weight_grad)


VMEM = pltpu.VMEM
SMEM = pltpu.SMEM
SIDES = 2


def vmem_specs(count):
    return [pl.BlockSpec(memory_space=VMEM)] * count


def struct(shape, dtype=jnp.bfloat16):
    return jax.ShapeDtypeStruct(shape, dtype)


def cost(flops, count, transcendentals=0):
    return pl.CostEstimate(flops=flops, bytes_accessed=count, transcendentals=transcendentals)


def sort_matrix(plan_ref, rows):
    slot = lax.broadcasted_iota(jnp.int32, (rows, rows), 0)
    return (plan_ref[...] == slot).astype(jnp.bfloat16)


def pack_query_kernel(dp, plan_ref, query_ref, out_ref):
    rows, width = query_ref.shape
    send, part_width = rows // dp, width // KV_HEADS
    select = sort_matrix(plan_ref, rows)
    for group in range(KV_HEADS):
        part = jnp.dot(
            select,
            query_ref[:, group * part_width : (group + 1) * part_width],
            preferred_element_type=jnp.float32,
        ).astype(jnp.bfloat16)
        for a in range(dp):
            out_ref[a * KV_HEADS + group] = part[a * send : (a + 1) * send]


def pack_query(dp, plan, query):
    rows, width = query.shape
    return pl.pallas_call(
        functools.partial(pack_query_kernel, dp),
        in_specs=vmem_specs(2),
        out_specs=pl.BlockSpec(memory_space=VMEM),
        out_shape=struct((dp * KV_HEADS, rows // dp, width // KV_HEADS)),
        cost_estimate=cost(2 * rows * rows * width, 4 * query.size),
        name="pack_query",
    )(plan, query)


def pack_rows_kernel(dp, plan_ref, hidden_ref, cos_ref, sin_ref, proj_ref, kv_ref, hid_ref, sorted_ref):
    step = pl.program_id(0)
    rows, width = hidden_ref.shape
    send = rows // dp
    ctx = KV_HEADS * SIDES
    eighth = width // ctx

    @pl.when(step == 0)
    def _():
        select = sort_matrix(plan_ref, rows)
        for col in range(ctx):
            window = pl.ds(col * eighth, eighth)
            part = jnp.dot(select, hidden_ref[:, window], preferred_element_type=jnp.float32).astype(jnp.bfloat16)
            sorted_ref[:, window] = part
            for a in range(dp):
                hid_ref[a * ctx + col] = part[a * send : (a + 1) * send]

    block = inner_rows(sorted_ref[...], proj_ref[...])
    heads = block.shape[1] // HEAD_DIM
    for which in range(2 * KV_HEADS // heads):

        @pl.when(step == which)
        def _(which=which):
            for t in range(heads):
                head = which * heads + t
                is_value, group = head // KV_HEADS, head % KV_HEADS
                start = is_value * HEAD_DIM
                for a in range(dp):
                    x = block[a * send : (a + 1) * send, t * HEAD_DIM : (t + 1) * HEAD_DIM]
                    if not is_value:
                        x = x * cos_ref[...] + pltpu.roll(x, HEAD_DIM // 2, 1) * sin_ref[...]
                    x = x.astype(jnp.bfloat16)
                    for side in range(SIDES):
                        kv_ref[a * ctx + group * SIDES + side, :, start : start + HEAD_DIM] = x


def pack_rows(dp, plan, hidden, cosine, sine, projection):
    rows, width = hidden.shape
    send = rows // dp
    ctx = KV_HEADS * SIDES
    proj_rows = 2 * HEAD_DIM
    steps = projection.shape[0] // proj_rows
    full = lambda shape: pl.BlockSpec(shape, lambda i: (0,) * len(shape))
    kv_shape = (dp * ctx, send, 2 * HEAD_DIM)
    hid_shape = (dp * ctx, send, width // ctx)
    return pl.pallas_call(
        functools.partial(pack_rows_kernel, dp),
        grid=(steps,),
        in_specs=[
            full(plan.shape),
            full(hidden.shape),
            full(cosine.shape),
            full(sine.shape),
            pl.BlockSpec((proj_rows, width), lambda i: (i, 0)),
        ],
        out_specs=[full(kv_shape), full(hid_shape)],
        out_shape=[struct(kv_shape), struct(hid_shape)],
        scratch_shapes=[VMEM((rows, width), jnp.bfloat16)],
        cost_estimate=cost(2 * rows * width * projection.shape[0], 2 * (projection.size + 3 * hidden.size)),
        name="pack_rows",
    )(plan, hidden, cosine, sine, projection)


def split_kernel(group_ref, in_ref, *out_refs):
    width = out_refs[0].shape[1]
    for e, out_ref in enumerate(out_refs):
        at = jnp.bitwise_xor(group_ref[0], e) * width
        out_ref[...] = in_ref[:, pl.ds(pl.multiple_of(at, width), width)]


def split_columns(group, array):
    rows, width = array.shape
    return pl.pallas_call(
        split_kernel,
        in_specs=[pl.BlockSpec(memory_space=SMEM)] + vmem_specs(1),
        out_specs=vmem_specs(KV_HEADS),
        out_shape=[struct((rows, width // KV_HEADS))] * KV_HEADS,
        cost_estimate=cost(0, 4 * array.size),
        name="split_columns",
    )(group, array)


def join_kernel(group_ref, *refs):
    pieces, outs = refs[:KV_HEADS], refs[KV_HEADS:]
    width = pieces[0].shape[1] // len(outs)
    for e, piece in enumerate(pieces):
        at = pl.multiple_of(jnp.bitwise_xor(group_ref[0], e) * width, width)
        for k, out_ref in enumerate(outs):
            out_ref[:, pl.ds(at, width)] = piece[:, k * width : (k + 1) * width]


def join_columns(group, pieces, outs):
    rows, width = pieces[0].shape
    return pl.pallas_call(
        join_kernel,
        in_specs=[pl.BlockSpec(memory_space=SMEM)] + vmem_specs(KV_HEADS),
        out_specs=vmem_specs(outs),
        out_shape=[struct((rows, KV_HEADS * width // outs))] * outs,
        cost_estimate=cost(0, 4 * KV_HEADS * rows * width),
        name="join_columns",
    )(group, *pieces)


def attend_kernel(dp, index_ref, query_ref, kv_ref, *refs):
    grads = refs[:KV_HEADS]
    row_doc_ref, col_doc_ref = refs[KV_HEADS : KV_HEADS + 2]
    outs = refs[KV_HEADS + 2 : 2 * KV_HEADS + 2]
    keep_ref, send_ref, key_s, value_s, query_s, grad_s, dk_s, dv_s = refs[2 * KV_HEADS + 2 :]
    which, group, side = index_ref[0], index_ref[1], index_ref[2]
    send = query_ref.shape[1]
    rows = dp * send
    width = query_ref.shape[2]
    heads = width // HEAD_DIM
    ctx = KV_HEADS * SIDES
    score_scale = HEAD_DIM ** (-0.5)
    power = score_scale * math.log2(math.e)
    for c in range(ctx):
        for s in range(dp):
            at = c * rows + s * send
            key_s[at : at + send, :] = kv_ref[s * ctx + c, :, 0:HEAD_DIM]
            value_s[at : at + send, :] = kv_ref[s * ctx + c, :, HEAD_DIM : 2 * HEAD_DIM]
    for e in range(KV_HEADS):
        zone = jnp.bitwise_xor(group, e)
        for head in range(heads):
            grad_s[zone, head * rows : (head + 1) * rows, :] = grads[e][:, head * HEAD_DIM : (head + 1) * HEAD_DIM]
            for s in range(dp):
                query_s[e, head * rows + s * send : head * rows + (s + 1) * send, :] = query_ref[
                    s * KV_HEADS + e, :, head * HEAD_DIM : (head + 1) * HEAD_DIM
                ]
    for zone in reversed(range(KV_HEADS)):
        hi = (zone + 1) * SIDES * rows
        start = pl.multiple_of((zone * SIDES + side) * rows, rows)
        keys = key_s[0:hi, :]
        values = value_s[0:hi, :]
        key_index = lax.broadcasted_iota(jnp.int32, (rows, hi), 1)
        query_index = lax.broadcasted_iota(jnp.int32, (rows, hi), 0) + start
        allowed = (key_index <= query_index) & (row_doc_ref[:, 0:hi] == col_doc_ref[pl.ds(start, rows), :])
        bias = jnp.where(allowed, 0.0, MASK_VALUE)
        query = query_s[zone]
        grad = grad_s[zone]
        scores = inner_rows(query, keys)
        scores = (scores.reshape(heads, rows, hi) + bias[None]).reshape(heads * rows, hi)
        row_max = jnp.max(scores, axis=1, keepdims=True)
        exponent = jnp.exp2((scores - row_max) * power)
        inverse = 1.0 / jnp.sum(exponent, axis=1, keepdims=True)
        probability = exponent * inverse
        rounded = probability.astype(jnp.bfloat16)
        attended = jnp.dot(rounded, values, preferred_element_type=jnp.float32).astype(jnp.bfloat16)
        weighted = inner_rows(grad, values) * probability
        delta = jnp.sum(weighted, axis=1, keepdims=True)
        grad_score = (weighted - probability * delta).astype(jnp.bfloat16)
        query_grad = (jnp.dot(grad_score, keys, preferred_element_type=jnp.float32) * score_scale).astype(jnp.bfloat16)
        if zone == KV_HEADS - 1:
            dk_s[0:hi, :] = outer_rows(grad_score, query)
            dv_s[0:hi, :] = outer_rows(rounded, grad)
        else:
            dk_s[0:hi, :] += outer_rows(grad_score, query)
            dv_s[0:hi, :] += outer_rows(rounded, grad)
        for e in range(KV_HEADS):

            @pl.when(jnp.bitwise_xor(group, e) == zone)
            def _(e=e, attended=attended, query_grad=query_grad):
                for head in range(heads):
                    part = slice(head * rows, (head + 1) * rows)
                    outs[e][:, head * HEAD_DIM : (head + 1) * HEAD_DIM] = attended[part]
                    outs[e][:, width + head * HEAD_DIM : width + (head + 1) * HEAD_DIM] = query_grad[part]

    @pl.when(which == 0)
    def _():
        keep_ref[...] = dk_s[...] * score_scale
        send_ref[...] = dv_s[...].astype(send_ref.dtype)

    @pl.when(which != 0)
    def _():
        keep_ref[...] = dv_s[...]
        send_ref[...] = (dk_s[...] * score_scale).astype(send_ref.dtype)


def attend(dp, index, query, kv, grads, documents):
    rows, width = grads[0].shape
    heads = width // HEAD_DIM
    length = KV_HEADS * SIDES * rows
    pairs = heads * length * length // 4
    return pl.pallas_call(
        functools.partial(attend_kernel, dp),
        in_specs=[pl.BlockSpec(memory_space=SMEM)] + vmem_specs(KV_HEADS + 4),
        out_specs=vmem_specs(KV_HEADS + 2),
        out_shape=[struct((rows, 2 * width))] * KV_HEADS
        + [struct((length, HEAD_DIM), jnp.float32), struct((length, HEAD_DIM))],
        scratch_shapes=[
            VMEM((length, HEAD_DIM), jnp.bfloat16),
            VMEM((length, HEAD_DIM), jnp.bfloat16),
            VMEM((KV_HEADS, heads * rows, HEAD_DIM), jnp.bfloat16),
            VMEM((KV_HEADS, heads * rows, HEAD_DIM), jnp.bfloat16),
            VMEM((length, HEAD_DIM), jnp.float32),
            VMEM((length, HEAD_DIM), jnp.float32),
        ],
        cost_estimate=cost(10 * pairs * HEAD_DIM, 2 * (2 * kv.size + 4 * query.size), pairs),
        name="attend",
    )(index, query, kv, *grads, documents, documents.reshape(length, 1))


def combine_kernel(dp, keep_ref, recv_ref, cos_ref, sin_ref, out_ref):
    length = keep_ref.shape[0]
    ctx = KV_HEADS * SIDES
    send = length // (dp * ctx)
    total = (keep_ref[...] + recv_ref[...].astype(jnp.float32)).astype(jnp.bfloat16).astype(jnp.float32)
    back = total * cos_ref[...] + pltpu.roll(total, HEAD_DIM // 2, 1) * sin_ref[...]
    back = back.astype(jnp.bfloat16)
    for c in range(ctx):
        for s in range(dp):
            at = (c * dp + s) * send
            to = (s * ctx + c) * send
            out_ref[to : to + send, :] = back[at : at + send]


def combine(dp, keep, recv, cosine, sine):
    return pl.pallas_call(
        functools.partial(combine_kernel, dp),
        in_specs=vmem_specs(4),
        out_specs=pl.BlockSpec(memory_space=VMEM),
        out_shape=struct(keep.shape),
        cost_estimate=cost(4 * keep.size, 16 * keep.size),
        name="combine",
    )(keep, recv, cosine, sine)


def product_kernel(dp, index_ref, *refs):
    group, block_id, high = index_ref[1], index_ref[3], index_ref[4]
    grads = refs[:KV_HEADS]
    hid_refs = refs[KV_HEADS : KV_HEADS + SIDES]
    out_refs = refs[KV_HEADS + SIDES : KV_HEADS + SIDES + dp]
    own_ref, other_ref, heads_s = refs[KV_HEADS + SIDES + dp :]
    ctx = KV_HEADS * SIDES
    length = grads[0].shape[0]
    send = length // (dp * ctx)
    for e in range(KV_HEADS):
        heads_s[jnp.bitwise_xor(group, e)] = grads[e][...]
    for s in range(dp):
        own = pl.ds(pl.multiple_of(s * ctx * send + block_id * send, send), send)
        other = pl.ds(pl.multiple_of(s * ctx * send + jnp.bitwise_xor(block_id, 1) * send, send), send)
        for head in range(KV_HEADS):
            cols = slice(head * HEAD_DIM, (head + 1) * HEAD_DIM)
            own_ref[s * send : (s + 1) * send, cols] = heads_s[head, own, :]
            other_ref[s * send : (s + 1) * send, cols] = heads_s[head, other, :]
    halves = dp // SIDES
    per = KV_HEADS // halves
    for ek in range(halves):
        first = jnp.bitwise_xor(high, ek) * per
        for t in range(per):
            left = heads_s[first + t]
            for ey in range(SIDES):
                part = outer_rows(left, hid_refs[ey][...])
                out_refs[ek * SIDES + ey][t * HEAD_DIM : (t + 1) * HEAD_DIM, :] = part.astype(jnp.bfloat16)


def product(dp, index, grads, hid_own, hid_other):
    length = grads[0].shape[0]
    columns = hid_own.shape[1]
    rows = length // (KV_HEADS * SIDES)
    block = (2 * KV_HEADS * HEAD_DIM // dp, columns)
    return pl.pallas_call(
        functools.partial(product_kernel, dp),
        in_specs=[pl.BlockSpec(memory_space=SMEM)] + vmem_specs(KV_HEADS + SIDES),
        out_specs=vmem_specs(dp + 2),
        out_shape=[struct(block)] * dp + [struct((rows, KV_HEADS * HEAD_DIM))] * 2,
        scratch_shapes=[VMEM((KV_HEADS, length, HEAD_DIM), jnp.bfloat16)],
        cost_estimate=cost(
            4 * length * KV_HEADS * HEAD_DIM * columns,
            2 * (2 * length * columns + length * KV_HEADS * HEAD_DIM + 4 * columns * HEAD_DIM * KV_HEADS),
        ),
        name="weight_product",
    )(index, *grads, hid_own, hid_other)


AXES = ("dp", "group", "side")


def paired_body(hidden_rows, query_rows, out_grad, projection, packing_plan, document_ids):
    rows, width = hidden_rows.shape
    dp = lax.axis_size("dp")
    ctx = KV_HEADS * SIDES
    a, group, side = (lax.axis_index(name) for name in AXES)
    block_id = group * SIDES + side
    send = rows // dp
    length = rows * ctx
    which = jnp.bitwise_xor(side, a % SIDES)
    index = jnp.stack([which, group, side, block_id, a // SIDES]).astype(jnp.int32)
    group_index = group.reshape(1)

    def move(value, target):
        flat = lambda i, g, p: (i * KV_HEADS + g) * SIDES + p
        moves = [
            (flat(i, g, p), flat(*target(i, g, p)))
            for i in range(dp)
            for g in range(KV_HEADS)
            for p in range(SIDES)
        ]
        return lax.ppermute(value, AXES, moves)

    def spread(pieces):
        return [pieces[0]] + [move(pieces[e], lambda i, g, p, e=e: (i, g ^ e, p)) for e in range(1, KV_HEADS)]

    other_side = lambda i, g, p: (i, g, 1 - p)
    scatter = lambda value, axes: lax.all_to_all(value, axes, split_axis=0, concat_axis=0, tiled=True)

    query_pieces = pack_query(dp, packing_plan, query_rows)
    query = scatter(query_pieces, AXES[:2])
    out_grad, query_pieces = lax.optimization_barrier((out_grad, query_pieces))
    grads_in = spread(split_columns(group_index, out_grad))

    slot = block_id * rows + a * send + jnp.arange(send, dtype=jnp.int32)
    cosine, sine = rotary_tables(slot, HEAD_DIM)
    kv_pieces, hid_pieces = pack_rows(
        dp, packing_plan, hidden_rows,
        jnp.concatenate([cosine, cosine], axis=1), jnp.concatenate([-sine, sine], axis=1), projection,
    )
    query, grads_in, kv_pieces = lax.optimization_barrier((query, grads_in, kv_pieces))
    kv = scatter(kv_pieces, AXES)
    kv, hid_pieces = lax.optimization_barrier((kv, hid_pieces))
    hid = scatter(hid_pieces, AXES)

    *outputs, keep, give = attend(dp, index, query, kv, grads_in, document_ids)
    recv = move(give, other_side)
    cosine, sine = rotary_tables(jnp.arange(length, dtype=jnp.int32), HEAD_DIM)
    cosine = jnp.where(which == 0, jnp.concatenate([cosine, cosine], axis=1), 1.0)
    sine = jnp.where(which == 0, jnp.concatenate([sine, -sine], axis=1), 0.0)
    piece = combine(dp, keep, recv, cosine, sine)
    piece, hid = lax.optimization_barrier((piece, hid))
    hid_own = hid.reshape(length, width // ctx)
    hid_other = move(hid_own, other_side)
    grads = spread([piece] * KV_HEADS)

    outputs, grads = lax.optimization_barrier((outputs, grads))
    back = spread(outputs)
    products = product(dp, index, grads, hid_own, hid_other)
    half = dp // SIDES
    blocks = [
        move(
            products[ek * SIDES + ey],
            lambda i, g, p, ek=ek, ey=ey: ((p ^ (i % SIDES)) * half + ((i // SIDES) ^ ek), g, p ^ ey),
        )
        for ek in range(half)
        for ey in range(SIDES)
    ]

    own_rows, other_rows = products[dp], products[dp + 1]
    other_half = move(other_rows, other_side)
    first = jnp.where(which == 0, own_rows, other_half)
    second = jnp.where(which == 0, other_half, own_rows)
    projected_grad = jnp.concatenate([first, second], axis=1)
    hidden_grad = jnp.dot(projected_grad, projection, preferred_element_type=jnp.float32).astype(jnp.bfloat16)
    weight_grad = functools.reduce(jnp.add, [b.astype(jnp.float32) for b in blocks]) / dp

    back, hidden_grad = lax.optimization_barrier((back, hidden_grad))
    attended, query_grad = join_columns(group_index, back, 2)
    return (attended, query_grad, hidden_grad, weight_grad)


def paired(mesh):
    dp, ctx = mesh.shape["dp"], mesh.shape["ctx"]
    return ctx == KV_HEADS * SIDES and dp in (2, 4, 8)


def solution(mesh):
    if paired(mesh):
        body = paired_body
        inner = Mesh(mesh.devices.reshape(mesh.shape["dp"], KV_HEADS, SIDES), AXES)
        ctx = AXES[1:]
    else:
        body = general_body
        inner = mesh
        ctx = ("ctx",)
    rows = P(("dp", *ctx), None)
    step = jax.shard_map(
        body,
        mesh=inner,
        in_specs=(rows, rows, rows, P(), rows, P("dp", None)),
        out_specs=(rows, rows, rows, P("dp", ctx)),
        check_vma=False,
    )
    if body is general_body:
        return step

    return step
```

```python
import functools
import math

import jax
import jax.numpy as jnp
from jax import lax
from jax.experimental import pallas as pl
from jax.experimental.pallas import tpu as pltpu
from jax.sharding import Mesh, PartitionSpec as P

KV_HEADS = 4
HEAD_DIM = 128


ROPE_BASE = 500000.0
MASK_VALUE = -1e30


def rotary_tables(positions, head_width):
    half_width = head_width // 2
    exponent = jnp.arange(half_width, dtype=jnp.float32) * (-2.0 * math.log(ROPE_BASE) / head_width)
    angles = positions.astype(jnp.float32)[:, None] * jnp.exp(exponent)[None, :]
    return (jnp.cos(angles), jnp.sin(angles))


def rotate_forward(head_rows, cosine_table, sine_table):
    half_width = head_rows.shape[-1] // 2
    first_half = head_rows[..., :half_width]
    second_half = head_rows[..., half_width:]
    cosine_part = cosine_table[:, None, :]
    sine_part = sine_table[:, None, :]
    return jnp.concatenate(
        [
            first_half * cosine_part - second_half * sine_part,
            second_half * cosine_part + first_half * sine_part,
        ],
        axis=-1,
    )


def rotate_adjoint(head_grads, cosine_table, sine_table):
    half_width = head_grads.shape[-1] // 2
    first_half = head_grads[..., :half_width]
    second_half = head_grads[..., half_width:]
    cosine_part = cosine_table[:, None, :]
    sine_part = sine_table[:, None, :]
    return jnp.concatenate(
        [
            first_half * cosine_part + second_half * sine_part,
            second_half * cosine_part - first_half * sine_part,
        ],
        axis=-1,
    )


def inner_rows(left_side, right_side):
    return lax.dot_general(
        left_side, right_side, (((1,), (1,)), ((), ())), preferred_element_type=jnp.float32
    )


def outer_rows(left_side, right_side):
    return lax.dot_general(
        left_side, right_side, (((0,), (0,)), ((), ())), preferred_element_type=jnp.float32
    )


def block_terms(
    query_block, grad_block, key_rows, value_rows, query_index, query_document, key_document
):
    score_scale = key_rows.shape[1] ** (-0.5)
    scores = inner_rows(query_block, key_rows) * score_scale
    key_index = jnp.arange(key_rows.shape[0], dtype=jnp.int32)
    allowed = (key_index[None, :] <= query_index[:, None]) & (
        key_document[None, :] == query_document[:, None]
    )
    scores = jnp.where(allowed, scores, MASK_VALUE)
    row_max = jnp.max(scores, axis=1, keepdims=True)
    exponent = jnp.exp(scores - row_max)
    probability = exponent / jnp.sum(exponent, axis=1, keepdims=True)
    rounded = probability.astype(jnp.bfloat16)
    attended = jnp.dot(rounded, value_rows, preferred_element_type=jnp.float32).astype(jnp.bfloat16)
    grad_prob = inner_rows(grad_block, value_rows)
    delta_sum = jnp.sum(probability * grad_prob, axis=1, keepdims=True)
    grad_score = (probability * (grad_prob - delta_sum)).astype(jnp.bfloat16)
    query_grad = (
        jnp.dot(grad_score, key_rows, preferred_element_type=jnp.float32) * score_scale
    ).astype(jnp.bfloat16)
    key_part = outer_rows(grad_score, query_block) * score_scale
    value_part = outer_rows(rounded, grad_block)
    return (attended, query_grad, key_part, value_part)


def general_body(hidden_rows, query_rows, out_grad, projection, packing_plan, document_ids):
    row_count = hidden_rows.shape[0]
    split_size = lax.axis_size("ctx")
    part_index = lax.axis_index("ctx")
    sequences = lax.axis_size("dp")
    order_rows = jnp.argsort(packing_plan[0])
    send_hidden = jnp.take(hidden_rows, order_rows, axis=0)
    send_query = jnp.take(query_rows, order_rows, axis=0)
    packed_hidden, packed_query = (
        lax.all_to_all(send_hidden, "dp", split_axis=0, concat_axis=0, tiled=True),
        lax.all_to_all(send_query, "dp", split_axis=0, concat_axis=0, tiled=True),
    )
    projected = inner_rows(packed_hidden, projection)
    positions = part_index * row_count + jnp.arange(row_count, dtype=jnp.int32)
    cosine_table, sine_table = rotary_tables(positions, HEAD_DIM)
    key_width = KV_HEADS * HEAD_DIM
    key_heads = rotate_forward(
        projected[:, :key_width].reshape(row_count, KV_HEADS, HEAD_DIM), cosine_table, sine_table
    ).astype(jnp.bfloat16)
    values = projected[:, key_width:].reshape(row_count, KV_HEADS, HEAD_DIM).astype(jnp.bfloat16)
    repeats = split_size // KV_HEADS
    key_slots = jnp.repeat(key_heads, repeats, axis=1).reshape(row_count, split_size * HEAD_DIM)
    value_slots = jnp.repeat(values, repeats, axis=1).reshape(row_count, split_size * HEAD_DIM)
    local_query, local_keys, local_values = (
        lax.all_to_all(packed_query, "ctx", split_axis=1, concat_axis=0, tiled=True),
        lax.all_to_all(key_slots, "ctx", split_axis=1, concat_axis=0, tiled=True),
        lax.all_to_all(value_slots, "ctx", split_axis=1, concat_axis=0, tiled=True),
    )
    local_grad = lax.all_to_all(out_grad, "ctx", split_axis=1, concat_axis=0, tiled=True)
    length = local_query.shape[0]
    block_rows = math.gcd(length, 512)
    block_count = length // block_rows
    documents = document_ids[0]
    head_count = local_query.shape[1] // HEAD_DIM
    starts = jnp.arange(block_count, dtype=jnp.int32) * block_rows
    key_total = jnp.zeros((length, HEAD_DIM), jnp.float32)
    value_total = jnp.zeros((length, HEAD_DIM), jnp.float32)
    attended_parts = []
    query_parts = []
    for head_index in range(head_count):
        query_blocks = local_query[:, head_index * HEAD_DIM : (head_index + 1) * HEAD_DIM].reshape(
            block_count, block_rows, HEAD_DIM
        )
        grad_blocks = local_grad[:, head_index * HEAD_DIM : (head_index + 1) * HEAD_DIM].reshape(
            block_count, block_rows, HEAD_DIM
        )

        def block_step(carry_pair, inputs):
            query_block, grad_block, block_start = inputs
            query_index = block_start + jnp.arange(block_rows, dtype=jnp.int32)
            query_document = lax.dynamic_slice_in_dim(documents, block_start, block_rows)
            attended_block, query_block_grad, key_part, value_part = block_terms(
                query_block,
                grad_block,
                local_keys,
                local_values,
                query_index,
                query_document,
                documents,
            )
            return (
                (carry_pair[0] + key_part, carry_pair[1] + value_part),
                (attended_block, query_block_grad),
            )

        (key_total, value_total), (attended_blocks, query_grad_blocks) = lax.scan(
            block_step, (key_total, value_total), (query_blocks, grad_blocks, starts)
        )
        attended_parts.append(attended_blocks.reshape(length, HEAD_DIM))
        query_parts.append(query_grad_blocks.reshape(length, HEAD_DIM))
    local_attended = jnp.concatenate(attended_parts, axis=1)
    local_query_grad = jnp.concatenate(query_parts, axis=1)
    attended = lax.all_to_all(local_attended, "ctx", split_axis=0, concat_axis=1, tiled=True)
    query_grad = lax.all_to_all(local_query_grad, "ctx", split_axis=0, concat_axis=1, tiled=True)
    key_slots_grad, value_slots_grad = (
        lax.all_to_all(key_total, "ctx", split_axis=0, concat_axis=1, tiled=True),
        lax.all_to_all(value_total, "ctx", split_axis=0, concat_axis=1, tiled=True),
    )
    key_grad = (
        key_slots_grad.reshape(row_count, KV_HEADS, repeats, HEAD_DIM)
        .sum(axis=2)
        .astype(jnp.bfloat16)
    )
    value_grad = (
        value_slots_grad.reshape(row_count, KV_HEADS, repeats, HEAD_DIM)
        .sum(axis=2)
        .astype(jnp.bfloat16)
    )
    key_back = rotate_adjoint(key_grad.astype(jnp.float32), cosine_table, sine_table).reshape(
        row_count, key_width
    )
    projected_grad = jnp.concatenate(
        [key_back, value_grad.reshape(row_count, key_width).astype(jnp.float32)], axis=1
    ).astype(jnp.bfloat16)
    hidden_grad = jnp.dot(projected_grad, projection, preferred_element_type=jnp.float32).astype(
        jnp.bfloat16
    )
    block_term = outer_rows(projected_grad, packed_hidden)
    partial_sum = lax.psum_scatter(
        block_term.astype(jnp.bfloat16), "ctx", scatter_dimension=1, tiled=True
    ).astype(jnp.float32)
    weight_grad = lax.psum_scatter(partial_sum, "dp", scatter_dimension=0, tiled=True)
    weight_grad = weight_grad / sequences
    return (attended, query_grad, hidden_grad, weight_grad)


VMEM = pltpu.VMEM
SMEM = pltpu.SMEM
SIDES = 2


def vmem_specs(count):
    return [pl.BlockSpec(memory_space=VMEM)] * count


def struct(shape, dtype=jnp.bfloat16):
    return jax.ShapeDtypeStruct(shape, dtype)


def cost(flops, count, transcendentals=0):
    return pl.CostEstimate(flops=flops, bytes_accessed=count, transcendentals=transcendentals)


def sort_matrix(plan_ref, rows):
    slot = lax.broadcasted_iota(jnp.int32, (rows, rows), 0)
    return (plan_ref[...] == slot).astype(jnp.bfloat16)


def pack_query_kernel(dp, plan_ref, query_ref, out_ref):
    rows, width = query_ref.shape
    send, part_width = rows // dp, width // KV_HEADS
    select = sort_matrix(plan_ref, rows)
    for group in range(KV_HEADS):
        part = jnp.dot(
            select,
            query_ref[:, group * part_width : (group + 1) * part_width],
            preferred_element_type=jnp.float32,
        ).astype(jnp.bfloat16)
        for a in range(dp):
            out_ref[a * KV_HEADS + group] = part[a * send : (a + 1) * send]


def pack_query(dp, plan, query):
    rows, width = query.shape
    return pl.pallas_call(
        functools.partial(pack_query_kernel, dp),
        in_specs=vmem_specs(2),
        out_specs=pl.BlockSpec(memory_space=VMEM),
        out_shape=struct((dp * KV_HEADS, rows // dp, width // KV_HEADS)),
        cost_estimate=cost(2 * rows * rows * width, 4 * query.size),
        name="pack_query",
    )(plan, query)


def pack_rows_kernel(dp, plan_ref, hidden_ref, cos_ref, sin_ref, proj_ref, kv_ref, hid_ref, sorted_ref):
    step = pl.program_id(0)
    rows, width = hidden_ref.shape
    send = rows // dp
    ctx = KV_HEADS * SIDES
    eighth = width // ctx

    @pl.when(step == 0)
    def _():
        select = sort_matrix(plan_ref, rows)
        for col in range(ctx):
            window = pl.ds(col * eighth, eighth)
            part = jnp.dot(select, hidden_ref[:, window], preferred_element_type=jnp.float32).astype(jnp.bfloat16)
            sorted_ref[:, window] = part
            for a in range(dp):
                hid_ref[a * ctx + col] = part[a * send : (a + 1) * send]

    block = inner_rows(sorted_ref[...], proj_ref[...])
    heads = block.shape[1] // HEAD_DIM
    for which in range(2 * KV_HEADS // heads):

        @pl.when(step == which)
        def _(which=which):
            for t in range(heads):
                head = which * heads + t
                is_value, group = head // KV_HEADS, head % KV_HEADS
                start = is_value * HEAD_DIM
                for a in range(dp):
                    x = block[a * send : (a + 1) * send, t * HEAD_DIM : (t + 1) * HEAD_DIM]
                    if not is_value:
                        x = x * cos_ref[...] + pltpu.roll(x, HEAD_DIM // 2, 1) * sin_ref[...]
                    x = x.astype(jnp.bfloat16)
                    for side in range(SIDES):
                        kv_ref[a * ctx + group * SIDES + side, :, start : start + HEAD_DIM] = x


def pack_rows(dp, plan, hidden, cosine, sine, projection):
    rows, width = hidden.shape
    send = rows // dp
    ctx = KV_HEADS * SIDES
    proj_rows = 2 * HEAD_DIM
    steps = projection.shape[0] // proj_rows
    full = lambda shape: pl.BlockSpec(shape, lambda i: (0,) * len(shape))
    kv_shape = (dp * ctx, send, 2 * HEAD_DIM)
    hid_shape = (dp * ctx, send, width // ctx)
    return pl.pallas_call(
        functools.partial(pack_rows_kernel, dp),
        grid=(steps,),
        in_specs=[
            full(plan.shape),
            full(hidden.shape),
            full(cosine.shape),
            full(sine.shape),
            pl.BlockSpec((proj_rows, width), lambda i: (i, 0)),
        ],
        out_specs=[full(kv_shape), full(hid_shape)],
        out_shape=[struct(kv_shape), struct(hid_shape)],
        scratch_shapes=[VMEM((rows, width), jnp.bfloat16)],
        cost_estimate=cost(2 * rows * width * projection.shape[0], 2 * (projection.size + 3 * hidden.size)),
        name="pack_rows",
    )(plan, hidden, cosine, sine, projection)


def split_kernel(group_ref, in_ref, *out_refs):
    width = out_refs[0].shape[1]
    for e, out_ref in enumerate(out_refs):
        at = jnp.bitwise_xor(group_ref[0], e) * width
        out_ref[...] = in_ref[:, pl.ds(pl.multiple_of(at, width), width)]


def split_columns(group, array):
    rows, width = array.shape
    return pl.pallas_call(
        split_kernel,
        in_specs=[pl.BlockSpec(memory_space=SMEM)] + vmem_specs(1),
        out_specs=vmem_specs(KV_HEADS),
        out_shape=[struct((rows, width // KV_HEADS))] * KV_HEADS,
        cost_estimate=cost(0, 4 * array.size),
        name="split_columns",
    )(group, array)


def join_kernel(group_ref, *refs):
    pieces, outs = refs[:KV_HEADS], refs[KV_HEADS:]
    width = pieces[0].shape[1] // len(outs)
    for e, piece in enumerate(pieces):
        at = pl.multiple_of(jnp.bitwise_xor(group_ref[0], e) * width, width)
        for k, out_ref in enumerate(outs):
            out_ref[:, pl.ds(at, width)] = piece[:, k * width : (k + 1) * width]


def join_columns(group, pieces, outs):
    rows, width = pieces[0].shape
    return pl.pallas_call(
        join_kernel,
        in_specs=[pl.BlockSpec(memory_space=SMEM)] + vmem_specs(KV_HEADS),
        out_specs=vmem_specs(outs),
        out_shape=[struct((rows, KV_HEADS * width // outs))] * outs,
        cost_estimate=cost(0, 4 * KV_HEADS * rows * width),
        name="join_columns",
    )(group, *pieces)


def attend_kernel(dp, index_ref, query_ref, kv_ref, *refs):
    grads = refs[:KV_HEADS]
    row_doc_ref, col_doc_ref = refs[KV_HEADS : KV_HEADS + 2]
    outs = refs[KV_HEADS + 2 : 2 * KV_HEADS + 2]
    keep_ref, send_ref, key_s, value_s, key_t, value_t, query_s, grad_s, dk_s, dv_s, out_s = refs[2 * KV_HEADS + 2 :]
    which, group, side = index_ref[0], index_ref[1], index_ref[2]
    send = query_ref.shape[1]
    rows = dp * send
    width = query_ref.shape[2]
    heads = width // HEAD_DIM
    ctx = KV_HEADS * SIDES
    score_scale = HEAD_DIM ** (-0.5)
    power = score_scale * math.log2(math.e)
    for c in range(ctx):
        for s in range(dp):
            at = c * rows + s * send
            key_s[at : at + send, :] = kv_ref[s * ctx + c, :, 0:HEAD_DIM]
            value_s[at : at + send, :] = kv_ref[s * ctx + c, :, HEAD_DIM : 2 * HEAD_DIM]
    for e in range(KV_HEADS):
        zone = jnp.bitwise_xor(group, e)
        for head in range(heads):
            grad_s[zone, head * rows : (head + 1) * rows, :] = grads[e][:, head * HEAD_DIM : (head + 1) * HEAD_DIM]
            for s in range(dp):
                query_s[e, head * rows + s * send : head * rows + (s + 1) * send, :] = query_ref[
                    s * KV_HEADS + e, :, head * HEAD_DIM : (head + 1) * HEAD_DIM
                ]
    for c in range(ctx):
        part = slice(c * rows, (c + 1) * rows)
        key_t[:, part] = key_s[part, :].astype(jnp.float32).T.astype(jnp.bfloat16)
        value_t[:, part] = value_s[part, :].astype(jnp.float32).T.astype(jnp.bfloat16)
    for zone in reversed(range(KV_HEADS)):
        hi = (zone + 1) * SIDES * rows
        start = pl.multiple_of((zone * SIDES + side) * rows, rows)
        keys = key_s[0:hi, :]
        values = value_s[0:hi, :]
        key_index = lax.broadcasted_iota(jnp.int32, (hi, rows), 0)
        query_index = lax.broadcasted_iota(jnp.int32, (hi, rows), 1) + start
        allowed = (key_index <= query_index) & (col_doc_ref[0:hi, :] == row_doc_ref[zone * SIDES + side])
        bias = jnp.where(allowed, 0.0, MASK_VALUE)
        query = query_s[zone]
        grad = grad_s[zone]
        scores = inner_rows(keys, query) + jnp.concatenate([bias] * heads, axis=1)
        row_max = jnp.max(scores, axis=0, keepdims=True)
        exponent = jnp.exp2((scores - row_max) * power)
        inverse = 1.0 / jnp.sum(exponent, axis=0, keepdims=True)
        probability = exponent * inverse
        rounded = probability.astype(jnp.bfloat16)
        attended = jnp.dot(value_t[:, 0:hi], rounded, preferred_element_type=jnp.float32)
        weighted = inner_rows(values, grad) * probability
        delta = jnp.sum(weighted, axis=0, keepdims=True)
        grad_score = (weighted - probability * delta).astype(jnp.bfloat16)
        query_grad = jnp.dot(key_t[:, 0:hi], grad_score, preferred_element_type=jnp.float32) * score_scale
        dk_part = jnp.dot(grad_score, query, preferred_element_type=jnp.float32)
        dv_part = jnp.dot(rounded, grad, preferred_element_type=jnp.float32)
        if zone == KV_HEADS - 1:
            dk_s[0:hi, :] = dk_part
            dv_s[0:hi, :] = dv_part
        else:
            dk_s[0:hi, :] += dk_part
            dv_s[0:hi, :] += dv_part
        for head in range(heads):
            part = slice(head * rows, (head + 1) * rows)
            out_s[zone, :, head * HEAD_DIM : (head + 1) * HEAD_DIM] = attended[:, part].T.astype(jnp.bfloat16)
            out_s[zone, :, width + head * HEAD_DIM : width + (head + 1) * HEAD_DIM] = (
                query_grad[:, part].T.astype(jnp.bfloat16)
            )
    for e in range(KV_HEADS):
        outs[e][...] = out_s[jnp.bitwise_xor(group, e)]

    @pl.when(which == 0)
    def _():
        keep_ref[...] = dk_s[...] * score_scale
        send_ref[...] = dv_s[...].astype(send_ref.dtype)

    @pl.when(which != 0)
    def _():
        keep_ref[...] = dv_s[...]
        send_ref[...] = (dk_s[...] * score_scale).astype(send_ref.dtype)


def attend(dp, index, query, kv, grads, documents, document_column):
    rows, width = grads[0].shape
    heads = width // HEAD_DIM
    length = KV_HEADS * SIDES * rows
    pairs = heads * length * length // 4
    return pl.pallas_call(
        functools.partial(attend_kernel, dp),
        in_specs=[pl.BlockSpec(memory_space=SMEM)] + vmem_specs(KV_HEADS + 4),
        out_specs=vmem_specs(KV_HEADS + 2),
        out_shape=[struct((rows, 2 * width))] * KV_HEADS
        + [struct((length, HEAD_DIM), jnp.float32), struct((length, HEAD_DIM))],
        scratch_shapes=[
            VMEM((length, HEAD_DIM), jnp.bfloat16),
            VMEM((length, HEAD_DIM), jnp.bfloat16),
            VMEM((HEAD_DIM, length), jnp.bfloat16),
            VMEM((HEAD_DIM, length), jnp.bfloat16),
            VMEM((KV_HEADS, heads * rows, HEAD_DIM), jnp.bfloat16),
            VMEM((KV_HEADS, heads * rows, HEAD_DIM), jnp.bfloat16),
            VMEM((length, HEAD_DIM), jnp.float32),
            VMEM((length, HEAD_DIM), jnp.float32),
            VMEM((KV_HEADS, rows, 2 * width), jnp.bfloat16),
        ],
        cost_estimate=cost(10 * pairs * HEAD_DIM, 2 * (2 * kv.size + 4 * query.size), pairs),
        name="attend",
    )(index, query, kv, *grads, documents.reshape(KV_HEADS * SIDES, 1, rows), document_column)


def combine_kernel(dp, keep_ref, recv_ref, cos_ref, sin_ref, out_ref):
    length = keep_ref.shape[0]
    ctx = KV_HEADS * SIDES
    send = length // (dp * ctx)
    total = (keep_ref[...] + recv_ref[...].astype(jnp.float32)).astype(jnp.bfloat16).astype(jnp.float32)
    back = total * cos_ref[...] + pltpu.roll(total, HEAD_DIM // 2, 1) * sin_ref[...]
    back = back.astype(jnp.bfloat16)
    for c in range(ctx):
        for s in range(dp):
            at = (c * dp + s) * send
            to = (s * ctx + c) * send
            out_ref[to : to + send, :] = back[at : at + send]


def combine(dp, keep, recv, cosine, sine):
    return pl.pallas_call(
        functools.partial(combine_kernel, dp),
        in_specs=vmem_specs(4),
        out_specs=pl.BlockSpec(memory_space=VMEM),
        out_shape=struct(keep.shape),
        cost_estimate=cost(4 * keep.size, 16 * keep.size),
        name="combine",
    )(keep, recv, cosine, sine)


def product_kernel(dp, index_ref, *refs):
    group, block_id, high = index_ref[1], index_ref[3], index_ref[4]
    grads = refs[:KV_HEADS]
    hid_refs = refs[KV_HEADS : KV_HEADS + SIDES]
    out_refs = refs[KV_HEADS + SIDES : KV_HEADS + SIDES + dp]
    own_ref, other_ref, heads_s = refs[KV_HEADS + SIDES + dp :]
    ctx = KV_HEADS * SIDES
    length = grads[0].shape[0]
    send = length // (dp * ctx)
    for e in range(KV_HEADS):
        heads_s[jnp.bitwise_xor(group, e)] = grads[e][...]
    for s in range(dp):
        own = pl.ds(pl.multiple_of(s * ctx * send + block_id * send, send), send)
        other = pl.ds(pl.multiple_of(s * ctx * send + jnp.bitwise_xor(block_id, 1) * send, send), send)
        for head in range(KV_HEADS):
            cols = slice(head * HEAD_DIM, (head + 1) * HEAD_DIM)
            own_ref[s * send : (s + 1) * send, cols] = heads_s[head, own, :]
            other_ref[s * send : (s + 1) * send, cols] = heads_s[head, other, :]
    halves = dp // SIDES
    per = KV_HEADS // halves
    for ek in range(halves):
        first = jnp.bitwise_xor(high, ek) * per
        for t in range(per):
            left = heads_s[first + t]
            for ey in range(SIDES):
                part = outer_rows(left, hid_refs[ey][...])
                out_refs[ek * SIDES + ey][t * HEAD_DIM : (t + 1) * HEAD_DIM, :] = part.astype(jnp.bfloat16)


def product(dp, index, grads, hid_own, hid_other):
    length = grads[0].shape[0]
    columns = hid_own.shape[1]
    rows = length // (KV_HEADS * SIDES)
    block = (2 * KV_HEADS * HEAD_DIM // dp, columns)
    return pl.pallas_call(
        functools.partial(product_kernel, dp),
        in_specs=[pl.BlockSpec(memory_space=SMEM)] + vmem_specs(KV_HEADS + SIDES),
        out_specs=vmem_specs(dp + 2),
        out_shape=[struct(block)] * dp + [struct((rows, KV_HEADS * HEAD_DIM))] * 2,
        scratch_shapes=[VMEM((KV_HEADS, length, HEAD_DIM), jnp.bfloat16)],
        cost_estimate=cost(
            4 * length * KV_HEADS * HEAD_DIM * columns,
            2 * (2 * length * columns + length * KV_HEADS * HEAD_DIM + 4 * columns * HEAD_DIM * KV_HEADS),
        ),
        name="weight_product",
    )(index, *grads, hid_own, hid_other)


AXES = ("dp", "group", "side")


def paired_body(hidden_rows, query_rows, out_grad, projection, packing_plan, document_ids):
    rows, width = hidden_rows.shape
    dp = lax.axis_size("dp")
    ctx = KV_HEADS * SIDES
    a, group, side = (lax.axis_index(name) for name in AXES)
    block_id = group * SIDES + side
    send = rows // dp
    length = rows * ctx
    which = jnp.bitwise_xor(side, a % SIDES)
    index = jnp.stack([which, group, side, block_id, a // SIDES]).astype(jnp.int32)
    group_index = group.reshape(1)

    def move(value, target):
        flat = lambda i, g, p: (i * KV_HEADS + g) * SIDES + p
        moves = [
            (flat(i, g, p), flat(*target(i, g, p)))
            for i in range(dp)
            for g in range(KV_HEADS)
            for p in range(SIDES)
        ]
        return lax.ppermute(value, AXES, moves)

    def spread(pieces):
        return [pieces[0]] + [move(pieces[e], lambda i, g, p, e=e: (i, g ^ e, p)) for e in range(1, KV_HEADS)]

    other_side = lambda i, g, p: (i, g, 1 - p)
    scatter = lambda value, axes: lax.all_to_all(value, axes, split_axis=0, concat_axis=0, tiled=True)

    document_column = document_ids.reshape(length, 1)
    packing_plan, index, document_column = lax.optimization_barrier((packing_plan, index, document_column))
    query_pieces = pack_query(dp, packing_plan, query_rows)
    query = scatter(query_pieces, AXES[:2])

    slot = block_id * rows + a * send + jnp.arange(send, dtype=jnp.int32)
    cosine, sine = rotary_tables(slot, HEAD_DIM)
    kv_pieces, hid_pieces = pack_rows(
        dp, packing_plan, hidden_rows,
        jnp.concatenate([cosine, cosine], axis=1), jnp.concatenate([-sine, sine], axis=1), projection,
    )
    out_grad, kv_pieces = lax.optimization_barrier((out_grad, kv_pieces))
    grads_in = spread(split_columns(group_index, out_grad))
    query, kv_pieces = lax.optimization_barrier((query, kv_pieces))
    kv = scatter(kv_pieces, AXES)
    kv, hid_pieces = lax.optimization_barrier((kv, hid_pieces))
    hid = scatter(hid_pieces, AXES)

    *outputs, keep, give = attend(dp, index, query, kv, grads_in, document_ids, document_column)
    recv = move(give, other_side)
    cosine, sine = rotary_tables(jnp.arange(length, dtype=jnp.int32), HEAD_DIM)
    cosine = jnp.where(which == 0, jnp.concatenate([cosine, cosine], axis=1), 1.0)
    sine = jnp.where(which == 0, jnp.concatenate([sine, -sine], axis=1), 0.0)
    piece = combine(dp, keep, recv, cosine, sine)
    piece, hid = lax.optimization_barrier((piece, hid))
    hid_own = hid.reshape(length, width // ctx)
    hid_other = move(hid_own, other_side)
    shift = lambda value, e: move(value, lambda i, g, p: (i, g ^ e, p))
    grads = [piece, shift(piece, 1), shift(piece, 2)]
    grads.append(shift(grads[2], 1))

    outputs, *early = lax.optimization_barrier((outputs, *grads[:3]))
    grads = [*early, grads[3]]
    back = spread(outputs)
    products = product(dp, index, grads, hid_own, hid_other)
    half = dp // SIDES
    blocks = [
        move(
            products[ek * SIDES + ey],
            lambda i, g, p, ek=ek, ey=ey: ((p ^ (i % SIDES)) * half + ((i // SIDES) ^ ek), g, p ^ ey),
        )
        for ek in range(half)
        for ey in range(SIDES)
    ]

    own_rows, other_rows = products[dp], products[dp + 1]
    other_half = move(other_rows, other_side)
    first = jnp.where(which == 0, own_rows, other_half)
    second = jnp.where(which == 0, other_half, own_rows)
    projected_grad = jnp.concatenate([first, second], axis=1)
    hidden_grad = jnp.dot(projected_grad, projection, preferred_element_type=jnp.float32).astype(jnp.bfloat16)
    weight_grad = functools.reduce(jnp.add, [b.astype(jnp.float32) for b in blocks]) / dp

    back, hidden_grad = lax.optimization_barrier((back, hidden_grad))
    attended, query_grad = join_columns(group_index, back, 2)
    return (attended, query_grad, hidden_grad, weight_grad)


def paired(mesh):
    dp, ctx = mesh.shape["dp"], mesh.shape["ctx"]
    return ctx == KV_HEADS * SIDES and dp in (2, 4, 8)


def solution(mesh):
    if paired(mesh):
        body = paired_body
        inner = Mesh(mesh.devices.reshape(mesh.shape["dp"], KV_HEADS, SIDES), AXES)
        ctx = AXES[1:]
    else:
        body = general_body
        inner = mesh
        ctx = ("ctx",)
    rows = P(("dp", *ctx), None)
    step = jax.shard_map(
        body,
        mesh=inner,
        in_specs=(rows, rows, rows, P(), rows, P("dp", None)),
        out_specs=(rows, rows, rows, P("dp", ctx)),
        check_vma=False,
    )
    if body is general_body:
        return step

    return step
```

```python
import functools
import math

import jax
import jax.numpy as jnp
from jax import lax
from jax.experimental import pallas as pl
from jax.experimental.pallas import tpu as pltpu
from jax.sharding import Mesh, PartitionSpec as P

KV_HEADS = 4
HEAD_DIM = 128


ROPE_BASE = 500000.0
MASK_VALUE = -1e30


def rotary_tables(positions, head_width):
    half_width = head_width // 2
    exponent = jnp.arange(half_width, dtype=jnp.float32) * (-2.0 * math.log(ROPE_BASE) / head_width)
    angles = positions.astype(jnp.float32)[:, None] * jnp.exp(exponent)[None, :]
    return (jnp.cos(angles), jnp.sin(angles))


def rotate_forward(head_rows, cosine_table, sine_table):
    half_width = head_rows.shape[-1] // 2
    first_half = head_rows[..., :half_width]
    second_half = head_rows[..., half_width:]
    cosine_part = cosine_table[:, None, :]
    sine_part = sine_table[:, None, :]
    return jnp.concatenate(
        [
            first_half * cosine_part - second_half * sine_part,
            second_half * cosine_part + first_half * sine_part,
        ],
        axis=-1,
    )


def rotate_adjoint(head_grads, cosine_table, sine_table):
    half_width = head_grads.shape[-1] // 2
    first_half = head_grads[..., :half_width]
    second_half = head_grads[..., half_width:]
    cosine_part = cosine_table[:, None, :]
    sine_part = sine_table[:, None, :]
    return jnp.concatenate(
        [
            first_half * cosine_part + second_half * sine_part,
            second_half * cosine_part - first_half * sine_part,
        ],
        axis=-1,
    )


def inner_rows(left_side, right_side):
    return lax.dot_general(
        left_side, right_side, (((1,), (1,)), ((), ())), preferred_element_type=jnp.float32
    )


def outer_rows(left_side, right_side):
    return lax.dot_general(
        left_side, right_side, (((0,), (0,)), ((), ())), preferred_element_type=jnp.float32
    )


def block_terms(
    query_block, grad_block, key_rows, value_rows, query_index, query_document, key_document
):
    score_scale = key_rows.shape[1] ** (-0.5)
    scores = inner_rows(query_block, key_rows) * score_scale
    key_index = jnp.arange(key_rows.shape[0], dtype=jnp.int32)
    allowed = (key_index[None, :] <= query_index[:, None]) & (
        key_document[None, :] == query_document[:, None]
    )
    scores = jnp.where(allowed, scores, MASK_VALUE)
    row_max = jnp.max(scores, axis=1, keepdims=True)
    exponent = jnp.exp(scores - row_max)
    probability = exponent / jnp.sum(exponent, axis=1, keepdims=True)
    rounded = probability.astype(jnp.bfloat16)
    attended = jnp.dot(rounded, value_rows, preferred_element_type=jnp.float32).astype(jnp.bfloat16)
    grad_prob = inner_rows(grad_block, value_rows)
    delta_sum = jnp.sum(probability * grad_prob, axis=1, keepdims=True)
    grad_score = (probability * (grad_prob - delta_sum)).astype(jnp.bfloat16)
    query_grad = (
        jnp.dot(grad_score, key_rows, preferred_element_type=jnp.float32) * score_scale
    ).astype(jnp.bfloat16)
    key_part = outer_rows(grad_score, query_block) * score_scale
    value_part = outer_rows(rounded, grad_block)
    return (attended, query_grad, key_part, value_part)


def general_body(hidden_rows, query_rows, out_grad, projection, packing_plan, document_ids):
    row_count = hidden_rows.shape[0]
    split_size = lax.axis_size("ctx")
    part_index = lax.axis_index("ctx")
    sequences = lax.axis_size("dp")
    order_rows = jnp.argsort(packing_plan[0])
    send_hidden = jnp.take(hidden_rows, order_rows, axis=0)
    send_query = jnp.take(query_rows, order_rows, axis=0)
    packed_hidden, packed_query = (
        lax.all_to_all(send_hidden, "dp", split_axis=0, concat_axis=0, tiled=True),
        lax.all_to_all(send_query, "dp", split_axis=0, concat_axis=0, tiled=True),
    )
    projected = inner_rows(packed_hidden, projection)
    positions = part_index * row_count + jnp.arange(row_count, dtype=jnp.int32)
    cosine_table, sine_table = rotary_tables(positions, HEAD_DIM)
    key_width = KV_HEADS * HEAD_DIM
    key_heads = rotate_forward(
        projected[:, :key_width].reshape(row_count, KV_HEADS, HEAD_DIM), cosine_table, sine_table
    ).astype(jnp.bfloat16)
    values = projected[:, key_width:].reshape(row_count, KV_HEADS, HEAD_DIM).astype(jnp.bfloat16)
    repeats = split_size // KV_HEADS
    key_slots = jnp.repeat(key_heads, repeats, axis=1).reshape(row_count, split_size * HEAD_DIM)
    value_slots = jnp.repeat(values, repeats, axis=1).reshape(row_count, split_size * HEAD_DIM)
    local_query, local_keys, local_values = (
        lax.all_to_all(packed_query, "ctx", split_axis=1, concat_axis=0, tiled=True),
        lax.all_to_all(key_slots, "ctx", split_axis=1, concat_axis=0, tiled=True),
        lax.all_to_all(value_slots, "ctx", split_axis=1, concat_axis=0, tiled=True),
    )
    local_grad = lax.all_to_all(out_grad, "ctx", split_axis=1, concat_axis=0, tiled=True)
    length = local_query.shape[0]
    block_rows = math.gcd(length, 512)
    block_count = length // block_rows
    documents = document_ids[0]
    head_count = local_query.shape[1] // HEAD_DIM
    starts = jnp.arange(block_count, dtype=jnp.int32) * block_rows
    key_total = jnp.zeros((length, HEAD_DIM), jnp.float32)
    value_total = jnp.zeros((length, HEAD_DIM), jnp.float32)
    attended_parts = []
    query_parts = []
    for head_index in range(head_count):
        query_blocks = local_query[:, head_index * HEAD_DIM : (head_index + 1) * HEAD_DIM].reshape(
            block_count, block_rows, HEAD_DIM
        )
        grad_blocks = local_grad[:, head_index * HEAD_DIM : (head_index + 1) * HEAD_DIM].reshape(
            block_count, block_rows, HEAD_DIM
        )

        def block_step(carry_pair, inputs):
            query_block, grad_block, block_start = inputs
            query_index = block_start + jnp.arange(block_rows, dtype=jnp.int32)
            query_document = lax.dynamic_slice_in_dim(documents, block_start, block_rows)
            attended_block, query_block_grad, key_part, value_part = block_terms(
                query_block,
                grad_block,
                local_keys,
                local_values,
                query_index,
                query_document,
                documents,
            )
            return (
                (carry_pair[0] + key_part, carry_pair[1] + value_part),
                (attended_block, query_block_grad),
            )

        (key_total, value_total), (attended_blocks, query_grad_blocks) = lax.scan(
            block_step, (key_total, value_total), (query_blocks, grad_blocks, starts)
        )
        attended_parts.append(attended_blocks.reshape(length, HEAD_DIM))
        query_parts.append(query_grad_blocks.reshape(length, HEAD_DIM))
    local_attended = jnp.concatenate(attended_parts, axis=1)
    local_query_grad = jnp.concatenate(query_parts, axis=1)
    attended = lax.all_to_all(local_attended, "ctx", split_axis=0, concat_axis=1, tiled=True)
    query_grad = lax.all_to_all(local_query_grad, "ctx", split_axis=0, concat_axis=1, tiled=True)
    key_slots_grad, value_slots_grad = (
        lax.all_to_all(key_total, "ctx", split_axis=0, concat_axis=1, tiled=True),
        lax.all_to_all(value_total, "ctx", split_axis=0, concat_axis=1, tiled=True),
    )
    key_grad = (
        key_slots_grad.reshape(row_count, KV_HEADS, repeats, HEAD_DIM)
        .sum(axis=2)
        .astype(jnp.bfloat16)
    )
    value_grad = (
        value_slots_grad.reshape(row_count, KV_HEADS, repeats, HEAD_DIM)
        .sum(axis=2)
        .astype(jnp.bfloat16)
    )
    key_back = rotate_adjoint(key_grad.astype(jnp.float32), cosine_table, sine_table).reshape(
        row_count, key_width
    )
    projected_grad = jnp.concatenate(
        [key_back, value_grad.reshape(row_count, key_width).astype(jnp.float32)], axis=1
    ).astype(jnp.bfloat16)
    hidden_grad = jnp.dot(projected_grad, projection, preferred_element_type=jnp.float32).astype(
        jnp.bfloat16
    )
    block_term = outer_rows(projected_grad, packed_hidden)
    partial_sum = lax.psum_scatter(
        block_term.astype(jnp.bfloat16), "ctx", scatter_dimension=1, tiled=True
    ).astype(jnp.float32)
    weight_grad = lax.psum_scatter(partial_sum, "dp", scatter_dimension=0, tiled=True)
    weight_grad = weight_grad / sequences
    return (attended, query_grad, hidden_grad, weight_grad)


VMEM = pltpu.VMEM
SMEM = pltpu.SMEM
SIDES = 2


def vmem_specs(count):
    return [pl.BlockSpec(memory_space=VMEM)] * count


def struct(shape, dtype=jnp.bfloat16):
    return jax.ShapeDtypeStruct(shape, dtype)


def cost(flops, count, transcendentals=0):
    return pl.CostEstimate(flops=flops, bytes_accessed=count, transcendentals=transcendentals)


def pack_kernel(dp, plan_ref, query_ref, hidden_ref, cos_ref, sin_ref, proj_ref, qkv_ref, hid_ref, sorted_ref):
    step = pl.program_id(0)
    rows, width = hidden_ref.shape
    send = rows // dp
    query_width = query_ref.shape[1] // KV_HEADS
    quarter = width // KV_HEADS

    @pl.when(step == 0)
    def _():
        slot = lax.broadcasted_iota(jnp.int32, (rows, rows), 0)
        select = (plan_ref[...] == slot).astype(jnp.bfloat16)
        for group in range(KV_HEADS):
            window = slice(group * quarter, (group + 1) * quarter)
            part = jnp.dot(select, hidden_ref[:, window], preferred_element_type=jnp.float32).astype(jnp.bfloat16)
            sorted_ref[:, window] = part
            query = jnp.dot(
                select,
                query_ref[:, group * query_width : (group + 1) * query_width],
                preferred_element_type=jnp.float32,
            ).astype(jnp.bfloat16)
            for a in range(dp):
                hid_ref[a * KV_HEADS + group] = part[a * send : (a + 1) * send]
                qkv_ref[a * KV_HEADS + group, :, 0:query_width] = query[a * send : (a + 1) * send]

    block = inner_rows(sorted_ref[...], proj_ref[...])
    heads = block.shape[1] // HEAD_DIM
    for which in range(2 * KV_HEADS // heads):

        @pl.when(step == which)
        def _(which=which):
            for t in range(heads):
                head = which * heads + t
                is_value, group = head // KV_HEADS, head % KV_HEADS
                start = query_width + is_value * HEAD_DIM
                for a in range(dp):
                    x = block[a * send : (a + 1) * send, t * HEAD_DIM : (t + 1) * HEAD_DIM]
                    if not is_value:
                        x = x * cos_ref[...] + pltpu.roll(x, HEAD_DIM // 2, 1) * sin_ref[...]
                    qkv_ref[a * KV_HEADS + group, :, start : start + HEAD_DIM] = x.astype(jnp.bfloat16)


def pack_rows(dp, plan, query, hidden, cosine, sine, projection):
    rows, width = hidden.shape
    send = rows // dp
    proj_rows = 2 * HEAD_DIM
    steps = projection.shape[0] // proj_rows
    full = lambda shape: pl.BlockSpec(shape, lambda i: (0,) * len(shape))
    qkv_shape = (dp * KV_HEADS, send, query.shape[1] // KV_HEADS + 2 * HEAD_DIM)
    hid_shape = (dp * KV_HEADS, send, width // KV_HEADS)
    return pl.pallas_call(
        functools.partial(pack_kernel, dp),
        grid=(steps,),
        in_specs=[
            full(plan.shape),
            full(query.shape),
            full(hidden.shape),
            full(cosine.shape),
            full(sine.shape),
            pl.BlockSpec((proj_rows, width), lambda i: (i, 0)),
        ],
        out_specs=[full(qkv_shape), full(hid_shape)],
        out_shape=[struct(qkv_shape), struct(hid_shape)],
        scratch_shapes=[VMEM((rows, width), jnp.bfloat16)],
        cost_estimate=cost(2 * rows * width * projection.shape[0], 2 * (projection.size + 3 * hidden.size)),
        name="pack_rows",
    )(plan, query, hidden, cosine, sine, projection)


def split_kernel(group_ref, in_ref, *out_refs):
    width = out_refs[0].shape[1]
    for e, out_ref in enumerate(out_refs):
        at = jnp.bitwise_xor(group_ref[0], e) * width
        out_ref[...] = in_ref[:, pl.ds(pl.multiple_of(at, width), width)]


def split_columns(group, array):
    rows, width = array.shape
    return pl.pallas_call(
        split_kernel,
        in_specs=[pl.BlockSpec(memory_space=SMEM)] + vmem_specs(1),
        out_specs=vmem_specs(KV_HEADS),
        out_shape=[struct((rows, width // KV_HEADS))] * KV_HEADS,
        cost_estimate=cost(0, 4 * array.size),
        name="split_columns",
    )(group, array)


def join_kernel(group_ref, *refs):
    pieces, outs = refs[:KV_HEADS], refs[KV_HEADS:]
    width = pieces[0].shape[1] // len(outs)
    for e, piece in enumerate(pieces):
        at = pl.multiple_of(jnp.bitwise_xor(group_ref[0], e) * width, width)
        for k, out_ref in enumerate(outs):
            out_ref[:, pl.ds(at, width)] = piece[:, k * width : (k + 1) * width]


def join_columns(group, pieces, outs):
    rows, width = pieces[0].shape
    return pl.pallas_call(
        join_kernel,
        in_specs=[pl.BlockSpec(memory_space=SMEM)] + vmem_specs(KV_HEADS),
        out_specs=vmem_specs(outs),
        out_shape=[struct((rows, KV_HEADS * width // outs))] * outs,
        cost_estimate=cost(0, 4 * KV_HEADS * rows * width),
        name="join_columns",
    )(group, *pieces)


def attend_kernel(dp, index_ref, qkv_ref, kv_ref, *refs):
    grads = refs[:KV_HEADS]
    doc_ref = refs[KV_HEADS]
    outs = refs[KV_HEADS + 1 : 2 * KV_HEADS + 1]
    keep_ref, send_ref, key_s, value_s, key_t, value_t, query_s, grad_s, dk_s, dv_s, out_s, doc_s = refs[2 * KV_HEADS + 1 :]
    which, group, side = index_ref[0], index_ref[1], index_ref[2]
    send = qkv_ref.shape[1]
    rows = dp * send
    width = qkv_ref.shape[2] - 2 * HEAD_DIM
    heads = width // HEAD_DIM
    ctx = KV_HEADS * SIDES
    score_scale = HEAD_DIM ** (-0.5)
    power = score_scale * math.log2(math.e)
    for s in range(dp):
        for zone in range(KV_HEADS):
            piece = s * KV_HEADS + zone
            own = pl.ds(pl.multiple_of((zone * SIDES + side) * rows + s * send, send), send)
            other = pl.ds(pl.multiple_of((zone * SIDES + 1 - side) * rows + s * send, send), send)
            key_s[own, :] = qkv_ref[piece, :, width : width + HEAD_DIM]
            value_s[own, :] = qkv_ref[piece, :, width + HEAD_DIM :]
            key_s[other, :] = kv_ref[piece, :, 0:HEAD_DIM]
            value_s[other, :] = kv_ref[piece, :, HEAD_DIM:]
    for e in range(KV_HEADS):
        zone = jnp.bitwise_xor(group, e)
        for head in range(heads):
            grad_s[zone, head * rows : (head + 1) * rows, :] = grads[e][:, head * HEAD_DIM : (head + 1) * HEAD_DIM]
            for s in range(dp):
                query_s[e, head * rows + s * send : head * rows + (s + 1) * send, :] = qkv_ref[
                    s * KV_HEADS + e, :, head * HEAD_DIM : (head + 1) * HEAD_DIM
                ]
    for c in range(ctx):
        part = slice(c * rows, (c + 1) * rows)
        key_t[:, part] = key_s[part, :].astype(jnp.float32).T.astype(jnp.bfloat16)
        value_t[:, part] = value_s[part, :].astype(jnp.float32).T.astype(jnp.bfloat16)
        doc_s[part, :] = jnp.broadcast_to(doc_ref[c].astype(jnp.float32), (rows, rows)).T
    for zone in reversed(range(KV_HEADS)):
        hi = (zone + 1) * SIDES * rows
        start = pl.multiple_of((zone * SIDES + side) * rows, rows)
        keys = key_s[0:hi, :]
        values = value_s[0:hi, :]
        key_index = lax.broadcasted_iota(jnp.int32, (hi, rows), 0)
        query_index = lax.broadcasted_iota(jnp.int32, (hi, rows), 1) + start
        allowed = (key_index <= query_index) & (doc_s[0:hi, :] == doc_ref[zone * SIDES + side].astype(jnp.float32))
        bias = jnp.where(allowed, 0.0, MASK_VALUE)
        query = query_s[zone]
        grad = grad_s[zone]
        scores = inner_rows(keys, query) + jnp.concatenate([bias] * heads, axis=1)
        row_max = jnp.max(scores, axis=0, keepdims=True)
        exponent = jnp.exp2((scores - row_max) * power)
        inverse = 1.0 / jnp.sum(exponent, axis=0, keepdims=True)
        probability = exponent * inverse
        rounded = probability.astype(jnp.bfloat16)
        attended = jnp.dot(value_t[:, 0:hi], rounded, preferred_element_type=jnp.float32)
        weighted = inner_rows(values, grad) * probability
        delta = jnp.sum(weighted, axis=0, keepdims=True)
        grad_score = (weighted - probability * delta).astype(jnp.bfloat16)
        query_grad = jnp.dot(key_t[:, 0:hi], grad_score, preferred_element_type=jnp.float32) * score_scale
        dk_part = jnp.dot(grad_score, query, preferred_element_type=jnp.float32)
        dv_part = jnp.dot(rounded, grad, preferred_element_type=jnp.float32)
        if zone == KV_HEADS - 1:
            dk_s[0:hi, :] = dk_part
            dv_s[0:hi, :] = dv_part
        else:
            dk_s[0:hi, :] += dk_part
            dv_s[0:hi, :] += dv_part
        for head in range(heads):
            part = slice(head * rows, (head + 1) * rows)
            out_s[zone, :, head * HEAD_DIM : (head + 1) * HEAD_DIM] = attended[:, part].T.astype(jnp.bfloat16)
            out_s[zone, :, width + head * HEAD_DIM : width + (head + 1) * HEAD_DIM] = (
                query_grad[:, part].T.astype(jnp.bfloat16)
            )
    for e in range(KV_HEADS):
        outs[e][...] = out_s[jnp.bitwise_xor(group, e)]

    @pl.when(which == 0)
    def _():
        keep_ref[...] = dk_s[...] * score_scale
        send_ref[...] = dv_s[...].astype(send_ref.dtype)

    @pl.when(which != 0)
    def _():
        keep_ref[...] = dv_s[...]
        send_ref[...] = (dk_s[...] * score_scale).astype(send_ref.dtype)


def attend(dp, index, qkv, kv, grads, documents):
    rows, width = grads[0].shape
    heads = width // HEAD_DIM
    length = KV_HEADS * SIDES * rows
    pairs = heads * length * length // 4
    return pl.pallas_call(
        functools.partial(attend_kernel, dp),
        in_specs=[pl.BlockSpec(memory_space=SMEM)] + vmem_specs(KV_HEADS + 3),
        out_specs=vmem_specs(KV_HEADS + 2),
        out_shape=[struct((rows, 2 * width))] * KV_HEADS
        + [struct((length, HEAD_DIM), jnp.float32), struct((length, HEAD_DIM))],
        scratch_shapes=[
            VMEM((length, HEAD_DIM), jnp.bfloat16),
            VMEM((length, HEAD_DIM), jnp.bfloat16),
            VMEM((HEAD_DIM, length), jnp.bfloat16),
            VMEM((HEAD_DIM, length), jnp.bfloat16),
            VMEM((KV_HEADS, heads * rows, HEAD_DIM), jnp.bfloat16),
            VMEM((KV_HEADS, heads * rows, HEAD_DIM), jnp.bfloat16),
            VMEM((length, HEAD_DIM), jnp.float32),
            VMEM((length, HEAD_DIM), jnp.float32),
            VMEM((KV_HEADS, rows, 2 * width), jnp.bfloat16),
            VMEM((length, rows), jnp.float32),
        ],
        cost_estimate=cost(10 * pairs * HEAD_DIM, 2 * (kv.size + 4 * qkv.size), pairs),
        name="attend",
    )(index, qkv, kv, *grads, documents.reshape(KV_HEADS * SIDES, 1, rows))


def combine_kernel(dp, index_ref, keep_ref, recv_ref, cos_ref, sin_ref, out_ref):
    side = index_ref[2]
    length = keep_ref.shape[0]
    ctx = KV_HEADS * SIDES
    send = length // (dp * ctx)
    total = (keep_ref[...] + recv_ref[...].astype(jnp.float32)).astype(jnp.bfloat16).astype(jnp.float32)
    back = total * cos_ref[...] + pltpu.roll(total, HEAD_DIM // 2, 1) * sin_ref[...]
    back = back.astype(jnp.bfloat16)
    for c in range(ctx):
        for s in range(dp):
            at = (c * dp + s) * send
            half = jnp.bitwise_xor(side, c % SIDES) * (length // SIDES)
            to = pl.multiple_of(half + (s * KV_HEADS + c // SIDES) * send, send)
            out_ref[pl.ds(to, send), :] = back[at : at + send]


def combine(dp, index, keep, recv, cosine, sine):
    return pl.pallas_call(
        functools.partial(combine_kernel, dp),
        in_specs=[pl.BlockSpec(memory_space=SMEM)] + vmem_specs(4),
        out_specs=pl.BlockSpec(memory_space=VMEM),
        out_shape=struct(keep.shape),
        cost_estimate=cost(4 * keep.size, 16 * keep.size),
        name="combine",
    )(index, keep, recv, cosine, sine)


def product_kernel(dp, index_ref, *refs):
    group, side, high = index_ref[1], index_ref[2], index_ref[3]
    grads = refs[:KV_HEADS]
    hid_refs = refs[KV_HEADS : KV_HEADS + SIDES]
    out_refs = refs[KV_HEADS + SIDES : KV_HEADS + SIDES + dp]
    own_ref, other_ref, heads_s = refs[KV_HEADS + SIDES + dp :]
    ctx = KV_HEADS * SIDES
    length = grads[0].shape[0]
    send = length // (dp * ctx)
    for e in range(KV_HEADS):
        heads_s[jnp.bitwise_xor(group, e)] = grads[e][...]
    part = length // SIDES
    columns = hid_refs[0].shape[1] // SIDES
    for s in range(dp):
        at = pl.multiple_of((s * KV_HEADS + group) * send, send)
        own, other = pl.ds(at, send), pl.ds(part + at, send)
        for head in range(KV_HEADS):
            cols = slice(head * HEAD_DIM, (head + 1) * HEAD_DIM)
            own_ref[s * send : (s + 1) * send, cols] = heads_s[head, own, :]
            other_ref[s * send : (s + 1) * send, cols] = heads_s[head, other, :]
    halves = dp // SIDES
    per = KV_HEADS // halves
    for ek in range(halves):
        first = jnp.bitwise_xor(high, ek) * per
        for t in range(per):
            left = heads_s[first + t]
            for ey in range(SIDES):
                window = pl.ds(pl.multiple_of(jnp.bitwise_xor(side, ey) * columns, columns), columns)
                total = outer_rows(left[:part], hid_refs[0][:, window]) + outer_rows(left[part:], hid_refs[1][:, window])
                out_refs[ek * SIDES + ey][t * HEAD_DIM : (t + 1) * HEAD_DIM, :] = total.astype(jnp.bfloat16)


def product(dp, index, grads, hid_own, hid_other):
    length = grads[0].shape[0]
    columns = hid_own.shape[1] // SIDES
    rows = length // (KV_HEADS * SIDES)
    block = (2 * KV_HEADS * HEAD_DIM // dp, columns)
    return pl.pallas_call(
        functools.partial(product_kernel, dp),
        in_specs=[pl.BlockSpec(memory_space=SMEM)] + vmem_specs(KV_HEADS + SIDES),
        out_specs=vmem_specs(dp + 2),
        out_shape=[struct(block)] * dp + [struct((rows, KV_HEADS * HEAD_DIM))] * 2,
        scratch_shapes=[VMEM((KV_HEADS, length, HEAD_DIM), jnp.bfloat16)],
        cost_estimate=cost(
            4 * length * KV_HEADS * HEAD_DIM * columns,
            2 * (2 * length * columns + length * KV_HEADS * HEAD_DIM + 4 * columns * HEAD_DIM * KV_HEADS),
        ),
        name="weight_product",
    )(index, *grads, hid_own, hid_other)


AXES = ("dp", "group", "side")


def paired_body(hidden_rows, query_rows, out_grad, projection, packing_plan, document_ids):
    rows, width = hidden_rows.shape
    dp = lax.axis_size("dp")
    ctx = KV_HEADS * SIDES
    a, group, side = (lax.axis_index(name) for name in AXES)
    block_id = group * SIDES + side
    send = rows // dp
    length = rows * ctx
    which = jnp.bitwise_xor(side, a % SIDES)
    index = jnp.stack([which, group, side, a // SIDES]).astype(jnp.int32)
    group_index = group.reshape(1)

    def move(value, target):
        flat = lambda i, g, p: (i * KV_HEADS + g) * SIDES + p
        moves = [
            (flat(i, g, p), flat(*target(i, g, p)))
            for i in range(dp)
            for g in range(KV_HEADS)
            for p in range(SIDES)
        ]
        return lax.ppermute(value, AXES, moves)

    def spread(pieces):
        return [pieces[0]] + [move(pieces[e], lambda i, g, p, e=e: (i, g ^ e, p)) for e in range(1, KV_HEADS)]

    other_side = lambda i, g, p: (i, g, 1 - p)
    scatter = lambda value, axes: lax.all_to_all(value, axes, split_axis=0, concat_axis=0, tiled=True)

    packing_plan, index = lax.optimization_barrier((packing_plan, index))
    slot = block_id * rows + a * send + jnp.arange(send, dtype=jnp.int32)
    cosine, sine = rotary_tables(slot, HEAD_DIM)
    qkv_pieces, hid_pieces = pack_rows(
        dp, packing_plan, query_rows, hidden_rows,
        jnp.concatenate([cosine, cosine], axis=1), jnp.concatenate([-sine, sine], axis=1), projection,
    )
    qkv = scatter(qkv_pieces, AXES[:2])
    out_grad, qkv_pieces = lax.optimization_barrier((out_grad, qkv_pieces))
    grads_in = spread(split_columns(group_index, out_grad))
    qkv, grads_in = lax.optimization_barrier((qkv, grads_in))
    kv_other = move(qkv[:, :, query_rows.shape[1] // KV_HEADS :], other_side)
    qkv, hid_pieces = lax.optimization_barrier((qkv, hid_pieces))
    hid = scatter(hid_pieces, AXES[:2])

    *outputs, keep, give = attend(dp, index, qkv, kv_other, grads_in, document_ids)
    recv = move(give, other_side)
    cosine, sine = rotary_tables(jnp.arange(length, dtype=jnp.int32), HEAD_DIM)
    cosine = jnp.where(which == 0, jnp.concatenate([cosine, cosine], axis=1), 1.0)
    sine = jnp.where(which == 0, jnp.concatenate([sine, -sine], axis=1), 0.0)
    piece = combine(dp, index, keep, recv, cosine, sine)
    piece, hid = lax.optimization_barrier((piece, hid))
    hid_own = hid.reshape(length // SIDES, width // KV_HEADS)
    hid_other = move(hid_own, other_side)
    shift = lambda value, e: move(value, lambda i, g, p: (i, g ^ e, p))
    grads = [piece, shift(piece, 1), shift(piece, 2)]
    grads.append(shift(grads[2], 1))

    outputs, *early = lax.optimization_barrier((outputs, *grads[:3]))
    grads = [*early, grads[3]]
    back = spread(outputs)
    products = product(dp, index, grads, hid_own, hid_other)
    half = dp // SIDES
    blocks = [
        move(
            products[ek * SIDES + ey],
            lambda i, g, p, ek=ek, ey=ey: ((p ^ (i % SIDES)) * half + ((i // SIDES) ^ ek), g, p ^ ey),
        )
        for ek in range(half)
        for ey in range(SIDES)
    ]

    own_rows, other_rows = products[dp], products[dp + 1]
    other_half = move(other_rows, other_side)
    first = jnp.where(which == 0, own_rows, other_half)
    second = jnp.where(which == 0, other_half, own_rows)
    projected_grad = jnp.concatenate([first, second], axis=1)
    hidden_grad = jnp.dot(projected_grad, projection, preferred_element_type=jnp.float32).astype(jnp.bfloat16)
    weight_grad = functools.reduce(jnp.add, [b.astype(jnp.float32) for b in blocks]) / dp

    back, hidden_grad = lax.optimization_barrier((back, hidden_grad))
    attended, query_grad = join_columns(group_index, back, 2)
    return (attended, query_grad, hidden_grad, weight_grad)


def paired(mesh):
    dp, ctx = mesh.shape["dp"], mesh.shape["ctx"]
    return ctx == KV_HEADS * SIDES and dp in (2, 4, 8)


def solution(mesh):
    if paired(mesh):
        body = paired_body
        inner = Mesh(mesh.devices.reshape(mesh.shape["dp"], KV_HEADS, SIDES), AXES)
        ctx = AXES[1:]
    else:
        body = general_body
        inner = mesh
        ctx = ("ctx",)
    rows = P(("dp", *ctx), None)
    step = jax.shard_map(
        body,
        mesh=inner,
        in_specs=(rows, rows, rows, P(), rows, P("dp", None)),
        out_specs=(rows, rows, rows, P("dp", ctx)),
        check_vma=False,
    )
    if body is general_body:
        return step

    return step
```

```python
import functools
import math

import jax
import jax.numpy as jnp
from jax import lax
from jax.experimental import pallas as pl
from jax.experimental.pallas import tpu as pltpu
from jax.sharding import Mesh, PartitionSpec as P

KV_HEADS = 4
HEAD_DIM = 128


ROPE_BASE = 500000.0
MASK_VALUE = -1e30


def rotary_tables(positions, head_width):
    half_width = head_width // 2
    exponent = jnp.arange(half_width, dtype=jnp.float32) * (-2.0 * math.log(ROPE_BASE) / head_width)
    angles = positions.astype(jnp.float32)[:, None] * jnp.exp(exponent)[None, :]
    return (jnp.cos(angles), jnp.sin(angles))


def rotate_forward(head_rows, cosine_table, sine_table):
    half_width = head_rows.shape[-1] // 2
    first_half = head_rows[..., :half_width]
    second_half = head_rows[..., half_width:]
    cosine_part = cosine_table[:, None, :]
    sine_part = sine_table[:, None, :]
    return jnp.concatenate(
        [
            first_half * cosine_part - second_half * sine_part,
            second_half * cosine_part + first_half * sine_part,
        ],
        axis=-1,
    )


def rotate_adjoint(head_grads, cosine_table, sine_table):
    half_width = head_grads.shape[-1] // 2
    first_half = head_grads[..., :half_width]
    second_half = head_grads[..., half_width:]
    cosine_part = cosine_table[:, None, :]
    sine_part = sine_table[:, None, :]
    return jnp.concatenate(
        [
            first_half * cosine_part + second_half * sine_part,
            second_half * cosine_part - first_half * sine_part,
        ],
        axis=-1,
    )


def inner_rows(left_side, right_side):
    return lax.dot_general(
        left_side, right_side, (((1,), (1,)), ((), ())), preferred_element_type=jnp.float32
    )


def outer_rows(left_side, right_side):
    return lax.dot_general(
        left_side, right_side, (((0,), (0,)), ((), ())), preferred_element_type=jnp.float32
    )


def block_terms(
    query_block, grad_block, key_rows, value_rows, query_index, query_document, key_document
):
    score_scale = key_rows.shape[1] ** (-0.5)
    scores = inner_rows(query_block, key_rows) * score_scale
    key_index = jnp.arange(key_rows.shape[0], dtype=jnp.int32)
    allowed = (key_index[None, :] <= query_index[:, None]) & (
        key_document[None, :] == query_document[:, None]
    )
    scores = jnp.where(allowed, scores, MASK_VALUE)
    row_max = jnp.max(scores, axis=1, keepdims=True)
    exponent = jnp.exp(scores - row_max)
    probability = exponent / jnp.sum(exponent, axis=1, keepdims=True)
    rounded = probability.astype(jnp.bfloat16)
    attended = jnp.dot(rounded, value_rows, preferred_element_type=jnp.float32).astype(jnp.bfloat16)
    grad_prob = inner_rows(grad_block, value_rows)
    delta_sum = jnp.sum(probability * grad_prob, axis=1, keepdims=True)
    grad_score = (probability * (grad_prob - delta_sum)).astype(jnp.bfloat16)
    query_grad = (
        jnp.dot(grad_score, key_rows, preferred_element_type=jnp.float32) * score_scale
    ).astype(jnp.bfloat16)
    key_part = outer_rows(grad_score, query_block) * score_scale
    value_part = outer_rows(rounded, grad_block)
    return (attended, query_grad, key_part, value_part)


def general_body(hidden_rows, query_rows, out_grad, projection, packing_plan, document_ids):
    row_count = hidden_rows.shape[0]
    split_size = lax.axis_size("ctx")
    part_index = lax.axis_index("ctx")
    sequences = lax.axis_size("dp")
    order_rows = jnp.argsort(packing_plan[0])
    send_hidden = jnp.take(hidden_rows, order_rows, axis=0)
    send_query = jnp.take(query_rows, order_rows, axis=0)
    packed_hidden, packed_query = (
        lax.all_to_all(send_hidden, "dp", split_axis=0, concat_axis=0, tiled=True),
        lax.all_to_all(send_query, "dp", split_axis=0, concat_axis=0, tiled=True),
    )
    projected = inner_rows(packed_hidden, projection)
    positions = part_index * row_count + jnp.arange(row_count, dtype=jnp.int32)
    cosine_table, sine_table = rotary_tables(positions, HEAD_DIM)
    key_width = KV_HEADS * HEAD_DIM
    key_heads = rotate_forward(
        projected[:, :key_width].reshape(row_count, KV_HEADS, HEAD_DIM), cosine_table, sine_table
    ).astype(jnp.bfloat16)
    values = projected[:, key_width:].reshape(row_count, KV_HEADS, HEAD_DIM).astype(jnp.bfloat16)
    repeats = split_size // KV_HEADS
    key_slots = jnp.repeat(key_heads, repeats, axis=1).reshape(row_count, split_size * HEAD_DIM)
    value_slots = jnp.repeat(values, repeats, axis=1).reshape(row_count, split_size * HEAD_DIM)
    local_query, local_keys, local_values = (
        lax.all_to_all(packed_query, "ctx", split_axis=1, concat_axis=0, tiled=True),
        lax.all_to_all(key_slots, "ctx", split_axis=1, concat_axis=0, tiled=True),
        lax.all_to_all(value_slots, "ctx", split_axis=1, concat_axis=0, tiled=True),
    )
    local_grad = lax.all_to_all(out_grad, "ctx", split_axis=1, concat_axis=0, tiled=True)
    length = local_query.shape[0]
    block_rows = math.gcd(length, 512)
    block_count = length // block_rows
    documents = document_ids[0]
    head_count = local_query.shape[1] // HEAD_DIM
    starts = jnp.arange(block_count, dtype=jnp.int32) * block_rows
    key_total = jnp.zeros((length, HEAD_DIM), jnp.float32)
    value_total = jnp.zeros((length, HEAD_DIM), jnp.float32)
    attended_parts = []
    query_parts = []
    for head_index in range(head_count):
        query_blocks = local_query[:, head_index * HEAD_DIM : (head_index + 1) * HEAD_DIM].reshape(
            block_count, block_rows, HEAD_DIM
        )
        grad_blocks = local_grad[:, head_index * HEAD_DIM : (head_index + 1) * HEAD_DIM].reshape(
            block_count, block_rows, HEAD_DIM
        )

        def block_step(carry_pair, inputs):
            query_block, grad_block, block_start = inputs
            query_index = block_start + jnp.arange(block_rows, dtype=jnp.int32)
            query_document = lax.dynamic_slice_in_dim(documents, block_start, block_rows)
            attended_block, query_block_grad, key_part, value_part = block_terms(
                query_block,
                grad_block,
                local_keys,
                local_values,
                query_index,
                query_document,
                documents,
            )
            return (
                (carry_pair[0] + key_part, carry_pair[1] + value_part),
                (attended_block, query_block_grad),
            )

        (key_total, value_total), (attended_blocks, query_grad_blocks) = lax.scan(
            block_step, (key_total, value_total), (query_blocks, grad_blocks, starts)
        )
        attended_parts.append(attended_blocks.reshape(length, HEAD_DIM))
        query_parts.append(query_grad_blocks.reshape(length, HEAD_DIM))
    local_attended = jnp.concatenate(attended_parts, axis=1)
    local_query_grad = jnp.concatenate(query_parts, axis=1)
    attended = lax.all_to_all(local_attended, "ctx", split_axis=0, concat_axis=1, tiled=True)
    query_grad = lax.all_to_all(local_query_grad, "ctx", split_axis=0, concat_axis=1, tiled=True)
    key_slots_grad, value_slots_grad = (
        lax.all_to_all(key_total, "ctx", split_axis=0, concat_axis=1, tiled=True),
        lax.all_to_all(value_total, "ctx", split_axis=0, concat_axis=1, tiled=True),
    )
    key_grad = (
        key_slots_grad.reshape(row_count, KV_HEADS, repeats, HEAD_DIM)
        .sum(axis=2)
        .astype(jnp.bfloat16)
    )
    value_grad = (
        value_slots_grad.reshape(row_count, KV_HEADS, repeats, HEAD_DIM)
        .sum(axis=2)
        .astype(jnp.bfloat16)
    )
    key_back = rotate_adjoint(key_grad.astype(jnp.float32), cosine_table, sine_table).reshape(
        row_count, key_width
    )
    projected_grad = jnp.concatenate(
        [key_back, value_grad.reshape(row_count, key_width).astype(jnp.float32)], axis=1
    ).astype(jnp.bfloat16)
    hidden_grad = jnp.dot(projected_grad, projection, preferred_element_type=jnp.float32).astype(
        jnp.bfloat16
    )
    block_term = outer_rows(projected_grad, packed_hidden)
    partial_sum = lax.psum_scatter(
        block_term.astype(jnp.bfloat16), "ctx", scatter_dimension=1, tiled=True
    ).astype(jnp.float32)
    weight_grad = lax.psum_scatter(partial_sum, "dp", scatter_dimension=0, tiled=True)
    weight_grad = weight_grad / sequences
    return (attended, query_grad, hidden_grad, weight_grad)


VMEM = pltpu.VMEM
SMEM = pltpu.SMEM
SIDES = 2


def vmem_specs(count):
    return [pl.BlockSpec(memory_space=VMEM)] * count


def any_specs(count):
    return [pl.BlockSpec(memory_space=pl.ANY)] * count


def begin(pairs, semaphores):
    copies = [pltpu.make_async_copy(source, target, semaphores.at[i]) for i, (source, target) in enumerate(pairs)]
    for copy in copies:
        copy.start()
    return copies


def finish(copies):
    for copy in copies:
        copy.wait()


def kernel_params(mebibytes):
    return pltpu.CompilerParams(vmem_limit_bytes=mebibytes * 2**20)


def struct(shape, dtype=jnp.bfloat16):
    return jax.ShapeDtypeStruct(shape, dtype)


def cost(flops, count, transcendentals=0):
    return pl.CostEstimate(flops=flops, bytes_accessed=count, transcendentals=transcendentals)


def pack_kernel(dp, plan_ref, query_ref, hidden_ref, cos_ref, sin_ref, proj_ref, qkv_ref, hid_ref, proj_s, sorted_s, sems):
    steps = proj_s.shape[0]
    copies = begin([(proj_ref.at[i], proj_s.at[i]) for i in range(steps)], sems)
    rows, width = hidden_ref.shape
    send = rows // dp
    query_width = query_ref.shape[1] // KV_HEADS
    quarter = width // KV_HEADS
    slot = lax.broadcasted_iota(jnp.int32, (rows, rows), 0)
    select = (plan_ref[...] == slot).astype(jnp.bfloat16)
    for group in range(KV_HEADS):
        hidden = hidden_ref[:, group * quarter : (group + 1) * quarter]
        part = jnp.dot(select, hidden, preferred_element_type=jnp.float32)
        sorted_s[group * quarter : (group + 1) * quarter, :] = part.T.astype(jnp.bfloat16)
        part = part.astype(jnp.bfloat16)
        query = query_ref[:, group * query_width : (group + 1) * query_width]
        query = jnp.dot(select, query, preferred_element_type=jnp.float32).astype(jnp.bfloat16)
        for a in range(dp):
            hid_ref[a * KV_HEADS + group] = part[a * send : (a + 1) * send]
            qkv_ref[a * KV_HEADS + group, :, 0:query_width] = query[a * send : (a + 1) * send]
    heads = proj_s.shape[1] // HEAD_DIM
    for step in range(steps):
        copies[step].wait()
        block = jnp.dot(proj_s[step], sorted_s[...], preferred_element_type=jnp.float32)
        for t in range(heads):
            head = step * heads + t
            is_value, group = head // KV_HEADS, head % KV_HEADS
            start = query_width + is_value * HEAD_DIM
            head_rows = block[t * HEAD_DIM : (t + 1) * HEAD_DIM, :].T
            for a in range(dp):
                x = head_rows[a * send : (a + 1) * send]
                if not is_value:
                    x = x * cos_ref[...] + pltpu.roll(x, HEAD_DIM // 2, 1) * sin_ref[...]
                qkv_ref[a * KV_HEADS + group, :, start : start + HEAD_DIM] = x.astype(jnp.bfloat16)


def pack_rows(dp, plan, query, hidden, cosine, sine, projection):
    rows, width = hidden.shape
    send = rows // dp
    proj_rows = 2 * HEAD_DIM
    steps = projection.shape[0] // proj_rows
    qkv_shape = (dp * KV_HEADS, send, query.shape[1] // KV_HEADS + 2 * HEAD_DIM)
    hid_shape = (dp * KV_HEADS, send, width // KV_HEADS)
    return pl.pallas_call(
        functools.partial(pack_kernel, dp),
        in_specs=vmem_specs(5) + any_specs(1),
        out_specs=vmem_specs(2),
        out_shape=[struct(qkv_shape), struct(hid_shape)],
        scratch_shapes=[
            VMEM((steps, proj_rows, width), jnp.bfloat16),
            VMEM((width, rows), jnp.bfloat16),
            pltpu.SemaphoreType.DMA((steps,)),
        ],
        cost_estimate=cost(2 * rows * width * projection.shape[0], 2 * (projection.size + 3 * hidden.size)),
        name="pack_rows",
    )(plan, query, hidden, cosine, sine, projection.reshape(steps, proj_rows, width))


def split_kernel(group_ref, in_ref, *out_refs):
    width = out_refs[0].shape[1]
    for e, out_ref in enumerate(out_refs):
        at = jnp.bitwise_xor(group_ref[0], e) * width
        out_ref[...] = in_ref[:, pl.ds(pl.multiple_of(at, width), width)]


def split_columns(group, array):
    rows, width = array.shape
    return pl.pallas_call(
        split_kernel,
        in_specs=[pl.BlockSpec(memory_space=SMEM)] + vmem_specs(1),
        out_specs=vmem_specs(KV_HEADS),
        out_shape=[struct((rows, width // KV_HEADS))] * KV_HEADS,
        cost_estimate=cost(0, 4 * array.size),
        name="split_columns",
    )(group, array)


def join_kernel(group_ref, *refs):
    pieces, outs, sems = refs[:KV_HEADS], refs[KV_HEADS:-1], refs[-1]
    width = pieces[0].shape[1] // len(outs)
    pairs = []
    for e, piece in enumerate(pieces):
        at = pl.multiple_of(jnp.bitwise_xor(group_ref[0], e) * width, width)
        for k, out_ref in enumerate(outs):
            pairs.append((piece.at[:, pl.ds(k * width, width)], out_ref.at[:, pl.ds(at, width)]))
    finish(begin(pairs, sems))


def join_columns(group, pieces, outs):
    rows, width = pieces[0].shape
    return pl.pallas_call(
        join_kernel,
        in_specs=[pl.BlockSpec(memory_space=SMEM)] + any_specs(KV_HEADS),
        out_specs=vmem_specs(outs),
        out_shape=[struct((rows, KV_HEADS * width // outs))] * outs,
        scratch_shapes=[pltpu.SemaphoreType.DMA((KV_HEADS * outs,))],
        compiler_params=kernel_params(8),
        cost_estimate=cost(0, 4 * KV_HEADS * rows * width),
        name="join_columns",
    )(group, *pieces)


def attend_kernel(dp, index_ref, qkv_ref, kv_ref, *refs):
    grads = refs[:KV_HEADS]
    doc_ref = refs[KV_HEADS]
    outs = refs[KV_HEADS + 1 : 2 * KV_HEADS + 1]
    keep_ref, send_ref, key_s, value_s, key_t, value_t, query_s, grad_s, dk_s, dv_s, out_s, doc_s = refs[2 * KV_HEADS + 1 :]
    which, group, side = index_ref[0], index_ref[1], index_ref[2]
    send = qkv_ref.shape[1]
    rows = dp * send
    width = qkv_ref.shape[2] - 2 * HEAD_DIM
    heads = width // HEAD_DIM
    ctx = KV_HEADS * SIDES
    score_scale = HEAD_DIM ** (-0.5)
    power = score_scale * math.log2(math.e)
    for e in range(KV_HEADS):
        zone = jnp.bitwise_xor(group, e)
        for head in range(heads):
            grad_s[zone, head * rows : (head + 1) * rows, :] = grads[e][:, head * HEAD_DIM : (head + 1) * HEAD_DIM]
            for s in range(dp):
                query_s[e, head * rows + s * send : head * rows + (s + 1) * send, :] = qkv_ref[
                    s * KV_HEADS + e, :, head * HEAD_DIM : (head + 1) * HEAD_DIM
                ]
    for s in range(dp):
        for zone in range(KV_HEADS):
            piece = s * KV_HEADS + zone
            own = pl.ds(pl.multiple_of((zone * SIDES + side) * rows + s * send, send), send)
            other = pl.ds(pl.multiple_of((zone * SIDES + 1 - side) * rows + s * send, send), send)
            key_s[own, :] = qkv_ref[piece, :, width : width + HEAD_DIM]
            value_s[own, :] = qkv_ref[piece, :, width + HEAD_DIM :]
            key_s[other, :] = kv_ref[piece, :, 0:HEAD_DIM]
            value_s[other, :] = kv_ref[piece, :, HEAD_DIM:]
    for c in range(ctx):
        part = slice(c * rows, (c + 1) * rows)
        key_t[:, part] = key_s[part, :].astype(jnp.float32).T.astype(jnp.bfloat16)
        value_t[:, part] = value_s[part, :].astype(jnp.float32).T.astype(jnp.bfloat16)
        doc_s[part, :] = jnp.broadcast_to(doc_ref[c].astype(jnp.float32), (rows, rows)).T
    for zone in reversed(range(KV_HEADS)):
        hi = (zone + 1) * SIDES * rows
        start = pl.multiple_of((zone * SIDES + side) * rows, rows)
        keys = key_s[0:hi, :]
        values = value_s[0:hi, :]
        key_index = lax.broadcasted_iota(jnp.int32, (hi, rows), 0)
        query_index = lax.broadcasted_iota(jnp.int32, (hi, rows), 1) + start
        allowed = (key_index <= query_index) & (doc_s[0:hi, :] == doc_ref[zone * SIDES + side].astype(jnp.float32))
        bias = jnp.where(allowed, 0.0, MASK_VALUE)
        query = query_s[zone]
        grad = grad_s[zone]
        scores = inner_rows(keys, query) + jnp.concatenate([bias] * heads, axis=1)
        row_max = jnp.max(scores, axis=0, keepdims=True)
        exponent = jnp.exp2((scores - row_max) * power)
        inverse = 1.0 / jnp.sum(exponent, axis=0, keepdims=True)
        probability = exponent * inverse
        rounded = probability.astype(jnp.bfloat16)
        attended = jnp.dot(value_t[:, 0:hi], rounded, preferred_element_type=jnp.float32)
        weighted = inner_rows(values, grad) * probability
        delta = jnp.sum(weighted, axis=0, keepdims=True)
        grad_score = (weighted - probability * delta).astype(jnp.bfloat16)
        query_grad = jnp.dot(key_t[:, 0:hi], grad_score, preferred_element_type=jnp.float32) * score_scale
        dk_part = jnp.dot(grad_score, query, preferred_element_type=jnp.float32)
        dv_part = jnp.dot(rounded, grad, preferred_element_type=jnp.float32)
        if zone == KV_HEADS - 1:
            dk_s[0:hi, :] = dk_part
            dv_s[0:hi, :] = dv_part
        else:
            dk_s[0:hi, :] += dk_part
            dv_s[0:hi, :] += dv_part
        for head in range(heads):
            part = slice(head * rows, (head + 1) * rows)
            out_s[zone, :, head * HEAD_DIM : (head + 1) * HEAD_DIM] = attended[:, part].T.astype(jnp.bfloat16)
            out_s[zone, :, width + head * HEAD_DIM : width + (head + 1) * HEAD_DIM] = (
                query_grad[:, part].T.astype(jnp.bfloat16)
            )
    for e in range(KV_HEADS):
        outs[e][...] = out_s[jnp.bitwise_xor(group, e)]

    @pl.when(which == 0)
    def _():
        keep_ref[...] = dk_s[...] * score_scale
        send_ref[...] = dv_s[...].astype(send_ref.dtype)

    @pl.when(which != 0)
    def _():
        keep_ref[...] = dv_s[...]
        send_ref[...] = (dk_s[...] * score_scale).astype(send_ref.dtype)


def attend(dp, index, qkv, kv, grads, documents):
    rows, width = grads[0].shape
    heads = width // HEAD_DIM
    length = KV_HEADS * SIDES * rows
    pairs = heads * length * length // 4
    return pl.pallas_call(
        functools.partial(attend_kernel, dp),
        in_specs=[pl.BlockSpec(memory_space=SMEM)] + vmem_specs(KV_HEADS + 3),
        out_specs=vmem_specs(KV_HEADS + 2),
        out_shape=[struct((rows, 2 * width))] * KV_HEADS
        + [struct((length, HEAD_DIM), jnp.float32), struct((length, HEAD_DIM))],
        scratch_shapes=[
            VMEM((length, HEAD_DIM), jnp.bfloat16),
            VMEM((length, HEAD_DIM), jnp.bfloat16),
            VMEM((HEAD_DIM, length), jnp.bfloat16),
            VMEM((HEAD_DIM, length), jnp.bfloat16),
            VMEM((KV_HEADS, heads * rows, HEAD_DIM), jnp.bfloat16),
            VMEM((KV_HEADS, heads * rows, HEAD_DIM), jnp.bfloat16),
            VMEM((length, HEAD_DIM), jnp.float32),
            VMEM((length, HEAD_DIM), jnp.float32),
            VMEM((KV_HEADS, rows, 2 * width), jnp.bfloat16),
            VMEM((length, rows), jnp.float32),
        ],
        cost_estimate=cost(10 * pairs * HEAD_DIM, 2 * (kv.size + 4 * qkv.size), pairs),
        name="attend",
    )(index, qkv, kv, *grads, documents.reshape(KV_HEADS * SIDES, 1, rows))


def combine_kernel(dp, index_ref, keep_ref, recv_any, cos_ref, sin_ref, out_ref, recv_ref, sems):
    side = index_ref[2]
    finish(begin([(recv_any, recv_ref)], sems))
    length = keep_ref.shape[0]
    ctx = KV_HEADS * SIDES
    send = length // (dp * ctx)
    total = (keep_ref[...] + recv_ref[...].astype(jnp.float32)).astype(jnp.bfloat16).astype(jnp.float32)
    back = total * cos_ref[...] + pltpu.roll(total, HEAD_DIM // 2, 1) * sin_ref[...]
    back = back.astype(jnp.bfloat16)
    for c in range(ctx):
        for s in range(dp):
            at = (c * dp + s) * send
            half = jnp.bitwise_xor(side, c % SIDES) * (length // SIDES)
            to = pl.multiple_of(half + (s * KV_HEADS + c // SIDES) * send, send)
            out_ref[pl.ds(to, send), :] = back[at : at + send]


def combine(dp, index, keep, recv, cosine, sine):
    return pl.pallas_call(
        functools.partial(combine_kernel, dp),
        in_specs=[pl.BlockSpec(memory_space=SMEM)] + vmem_specs(1) + any_specs(1) + vmem_specs(2),
        out_specs=pl.BlockSpec(memory_space=VMEM),
        out_shape=struct(keep.shape),
        scratch_shapes=[VMEM(recv.shape, recv.dtype), pltpu.SemaphoreType.DMA((1,))],
        compiler_params=kernel_params(12),
        cost_estimate=cost(4 * keep.size, 16 * keep.size),
        name="combine",
    )(index, keep, recv, cosine, sine)


def product_kernel(dp, index_ref, *refs):
    group, side, high = index_ref[1], index_ref[2], index_ref[3]
    grads = refs[:KV_HEADS]
    hid_any = refs[KV_HEADS : KV_HEADS + SIDES]
    out_refs = refs[KV_HEADS + SIDES : KV_HEADS + SIDES + dp]
    own_ref, other_ref, heads_s, own_s, other_s, sems = refs[KV_HEADS + SIDES + dp :]
    hid_refs = (own_s, other_s)
    ctx = KV_HEADS * SIDES
    length = grads[0].shape[0]
    send = length // (dp * ctx)
    pairs = [(grads[e], heads_s.at[jnp.bitwise_xor(group, e)]) for e in range(KV_HEADS)]
    copies = begin(pairs + list(zip(hid_any, hid_refs)), sems)
    finish(copies[:KV_HEADS])
    part = length // SIDES
    columns = hid_refs[0].shape[1] // SIDES
    for s in range(dp):
        at = pl.multiple_of((s * KV_HEADS + group) * send, send)
        own, other = pl.ds(at, send), pl.ds(part + at, send)
        for head in range(KV_HEADS):
            cols = slice(head * HEAD_DIM, (head + 1) * HEAD_DIM)
            own_ref[s * send : (s + 1) * send, cols] = heads_s[head, own, :]
            other_ref[s * send : (s + 1) * send, cols] = heads_s[head, other, :]
    finish(copies[KV_HEADS:])
    halves = dp // SIDES
    per = KV_HEADS // halves
    for ek in range(halves):
        first = jnp.bitwise_xor(high, ek) * per
        for t in range(per):
            left = heads_s[first + t]
            for ey in range(SIDES):
                window = pl.ds(pl.multiple_of(jnp.bitwise_xor(side, ey) * columns, columns), columns)
                total = outer_rows(left[:part], hid_refs[0][:, window]) + outer_rows(left[part:], hid_refs[1][:, window])
                out_refs[ek * SIDES + ey][t * HEAD_DIM : (t + 1) * HEAD_DIM, :] = total.astype(jnp.bfloat16)


def product(dp, index, grads, hid_own, hid_other):
    length = grads[0].shape[0]
    columns = hid_own.shape[1] // SIDES
    rows = length // (KV_HEADS * SIDES)
    block = (2 * KV_HEADS * HEAD_DIM // dp, columns)
    return pl.pallas_call(
        functools.partial(product_kernel, dp),
        in_specs=[pl.BlockSpec(memory_space=SMEM)] + any_specs(KV_HEADS + SIDES),
        out_specs=vmem_specs(dp + 2),
        out_shape=[struct(block)] * dp + [struct((rows, KV_HEADS * HEAD_DIM))] * 2,
        scratch_shapes=[
            VMEM((KV_HEADS, length, HEAD_DIM), jnp.bfloat16),
            VMEM(hid_own.shape, jnp.bfloat16),
            VMEM(hid_other.shape, jnp.bfloat16),
            pltpu.SemaphoreType.DMA((KV_HEADS + SIDES,)),
        ],
        compiler_params=kernel_params(20),
        cost_estimate=cost(
            4 * length * KV_HEADS * HEAD_DIM * columns,
            2 * (2 * length * columns + length * KV_HEADS * HEAD_DIM + 4 * columns * HEAD_DIM * KV_HEADS),
        ),
        name="weight_product",
    )(index, *grads, hid_own, hid_other)


def hidden_kernel(which_ref, own_ref, other_ref, own_proj_ref, other_proj_ref, out_ref):
    total = jnp.dot(own_ref[...], own_proj_ref[0], preferred_element_type=jnp.float32)
    total += jnp.dot(other_ref[...], other_proj_ref[0], preferred_element_type=jnp.float32)
    out_ref[...] = total.astype(out_ref.dtype)


def hidden_product(which, own, other, projection):
    rows, half = own.shape
    width = projection.shape[1]
    columns = math.gcd(width, 1024)
    halves = projection.reshape(2, half, width)
    spec = pltpu.PrefetchScalarGridSpec(
        num_scalar_prefetch=1,
        grid=(width // columns,),
        in_specs=[
            pl.BlockSpec((rows, half), lambda i, w: (0, 0)),
            pl.BlockSpec((rows, half), lambda i, w: (0, 0)),
            pl.BlockSpec((1, half, columns), lambda i, w: (w[0], 0, i)),
            pl.BlockSpec((1, half, columns), lambda i, w: (1 - w[0], 0, i)),
        ],
        out_specs=pl.BlockSpec((rows, columns), lambda i, w: (0, i)),
    )
    return pl.pallas_call(
        hidden_kernel,
        grid_spec=spec,
        out_shape=struct((rows, width)),
        compiler_params=kernel_params(16),
        cost_estimate=cost(4 * rows * half * width, 2 * projection.size + 4 * rows * width),
        name="hidden_product",
    )(which, own, other, halves, halves)


AXES = ("dp", "group", "side")


def paired_body(hidden_rows, query_rows, out_grad, projection, packing_plan, document_ids):
    rows, width = hidden_rows.shape
    dp = lax.axis_size("dp")
    ctx = KV_HEADS * SIDES
    a, group, side = (lax.axis_index(name) for name in AXES)
    block_id = group * SIDES + side
    send = rows // dp
    length = rows * ctx
    which = jnp.bitwise_xor(side, a % SIDES)
    index = jnp.stack([which, group, side, a // SIDES]).astype(jnp.int32)
    group_index = group.reshape(1)

    def move(value, target):
        flat = lambda i, g, p: (i * KV_HEADS + g) * SIDES + p
        moves = [
            (flat(i, g, p), flat(*target(i, g, p)))
            for i in range(dp)
            for g in range(KV_HEADS)
            for p in range(SIDES)
        ]
        return lax.ppermute(value, AXES, moves)

    def spread(pieces):
        return [pieces[0]] + [move(pieces[e], lambda i, g, p, e=e: (i, g ^ e, p)) for e in range(1, KV_HEADS)]

    other_side = lambda i, g, p: (i, g, 1 - p)
    scatter = lambda value, axes: lax.all_to_all(value, axes, split_axis=0, concat_axis=0, tiled=True)

    grads_in = split_columns(group_index, out_grad)
    packing_plan, index, grads_in = lax.optimization_barrier((packing_plan, index, grads_in))
    grads_in = spread(grads_in)
    slot = block_id * rows + a * send + jnp.arange(send, dtype=jnp.int32)
    cosine, sine = rotary_tables(slot, HEAD_DIM)
    cosine, sine = jnp.concatenate([cosine, cosine], axis=1), jnp.concatenate([-sine, sine], axis=1)
    qkv_pieces, hid_pieces = pack_rows(dp, packing_plan, query_rows, hidden_rows, cosine, sine, projection)
    qkv = scatter(qkv_pieces, AXES[:2])
    kv_other = move(qkv[:, :, query_rows.shape[1] // KV_HEADS :], other_side)
    qkv, hid_pieces = lax.optimization_barrier((qkv, hid_pieces))
    hid = scatter(hid_pieces, AXES[:2])

    *outputs, keep, give = attend(dp, index, qkv, kv_other, grads_in, document_ids)
    recv = move(give, other_side)
    cosine, sine = rotary_tables(jnp.arange(length, dtype=jnp.int32), HEAD_DIM)
    cosine = jnp.where(which == 0, jnp.concatenate([cosine, cosine], axis=1), 1.0)
    sine = jnp.where(which == 0, jnp.concatenate([sine, -sine], axis=1), 0.0)
    piece = combine(dp, index, keep, recv, cosine, sine)
    piece, hid = lax.optimization_barrier((piece, hid))
    hid_own = hid.reshape(length // SIDES, width // KV_HEADS)
    hid_other = move(hid_own, other_side)
    shift = lambda value, e: move(value, lambda i, g, p: (i, g ^ e, p))
    grads = [piece, shift(piece, 1), shift(piece, 2)]
    grads.append(shift(grads[2], 1))

    outputs, *early = lax.optimization_barrier((outputs, *grads[:3]))
    grads = [*early, grads[3]]
    back = spread(outputs)
    products = product(dp, index, grads, hid_own, hid_other)
    own_rows, other_rows = products[dp], products[dp + 1]
    other_half = move(other_rows, other_side)
    half = dp // SIDES
    blocks = [
        move(
            products[ek * SIDES + ey],
            lambda i, g, p, ek=ek, ey=ey: ((p ^ (i % SIDES)) * half + ((i // SIDES) ^ ek), g, p ^ ey),
        )
        for ek in range(half)
        for ey in range(SIDES)
    ]

    hidden_grad = hidden_product(which.reshape(1), own_rows, other_half, projection)
    weight_grad = functools.reduce(jnp.add, [b.astype(jnp.float32) for b in blocks]) / dp

    back, hidden_grad = lax.optimization_barrier((back, hidden_grad))
    attended, query_grad = join_columns(group_index, back, 2)
    return (attended, query_grad, hidden_grad, weight_grad)


def paired(mesh):
    dp, ctx = mesh.shape["dp"], mesh.shape["ctx"]
    return ctx == KV_HEADS * SIDES and dp in (2, 4, 8)


def solution(mesh):
    if paired(mesh):
        body = paired_body
        inner = Mesh(mesh.devices.reshape(mesh.shape["dp"], KV_HEADS, SIDES), AXES)
        ctx = AXES[1:]
    else:
        body = general_body
        inner = mesh
        ctx = ("ctx",)
    rows = P(("dp", *ctx), None)
    step = jax.shard_map(
        body,
        mesh=inner,
        in_specs=(rows, rows, rows, P(), rows, P("dp", None)),
        out_specs=(rows, rows, rows, P("dp", ctx)),
        check_vma=False,
    )
    if body is general_body:
        return step

    return step
```

```python
import functools
import math

import jax
import jax.numpy as jnp
from jax import lax
from jax.experimental import pallas as pl
from jax.experimental.pallas import tpu as pltpu
from jax.sharding import Mesh, PartitionSpec as P

KV_HEADS = 4
HEAD_DIM = 128


ROPE_BASE = 500000.0
MASK_VALUE = -1e30


def rotary_tables(positions, head_width):
    half_width = head_width // 2
    exponent = jnp.arange(half_width, dtype=jnp.float32) * (-2.0 * math.log(ROPE_BASE) / head_width)
    angles = positions.astype(jnp.float32)[:, None] * jnp.exp(exponent)[None, :]
    return (jnp.cos(angles), jnp.sin(angles))


def rotate_forward(head_rows, cosine_table, sine_table):
    half_width = head_rows.shape[-1] // 2
    first_half = head_rows[..., :half_width]
    second_half = head_rows[..., half_width:]
    cosine_part = cosine_table[:, None, :]
    sine_part = sine_table[:, None, :]
    return jnp.concatenate(
        [
            first_half * cosine_part - second_half * sine_part,
            second_half * cosine_part + first_half * sine_part,
        ],
        axis=-1,
    )


def rotate_adjoint(head_grads, cosine_table, sine_table):
    half_width = head_grads.shape[-1] // 2
    first_half = head_grads[..., :half_width]
    second_half = head_grads[..., half_width:]
    cosine_part = cosine_table[:, None, :]
    sine_part = sine_table[:, None, :]
    return jnp.concatenate(
        [
            first_half * cosine_part + second_half * sine_part,
            second_half * cosine_part - first_half * sine_part,
        ],
        axis=-1,
    )


def inner_rows(left_side, right_side):
    return lax.dot_general(
        left_side, right_side, (((1,), (1,)), ((), ())), preferred_element_type=jnp.float32
    )


def outer_rows(left_side, right_side):
    return lax.dot_general(
        left_side, right_side, (((0,), (0,)), ((), ())), preferred_element_type=jnp.float32
    )


def block_terms(
    query_block, grad_block, key_rows, value_rows, query_index, query_document, key_document
):
    score_scale = key_rows.shape[1] ** (-0.5)
    scores = inner_rows(query_block, key_rows) * score_scale
    key_index = jnp.arange(key_rows.shape[0], dtype=jnp.int32)
    allowed = (key_index[None, :] <= query_index[:, None]) & (
        key_document[None, :] == query_document[:, None]
    )
    scores = jnp.where(allowed, scores, MASK_VALUE)
    row_max = jnp.max(scores, axis=1, keepdims=True)
    exponent = jnp.exp(scores - row_max)
    probability = exponent / jnp.sum(exponent, axis=1, keepdims=True)
    rounded = probability.astype(jnp.bfloat16)
    attended = jnp.dot(rounded, value_rows, preferred_element_type=jnp.float32).astype(jnp.bfloat16)
    grad_prob = inner_rows(grad_block, value_rows)
    delta_sum = jnp.sum(probability * grad_prob, axis=1, keepdims=True)
    grad_score = (probability * (grad_prob - delta_sum)).astype(jnp.bfloat16)
    query_grad = (
        jnp.dot(grad_score, key_rows, preferred_element_type=jnp.float32) * score_scale
    ).astype(jnp.bfloat16)
    key_part = outer_rows(grad_score, query_block) * score_scale
    value_part = outer_rows(rounded, grad_block)
    return (attended, query_grad, key_part, value_part)


def general_body(hidden_rows, query_rows, out_grad, projection, packing_plan, document_ids):
    row_count = hidden_rows.shape[0]
    split_size = lax.axis_size("ctx")
    part_index = lax.axis_index("ctx")
    sequences = lax.axis_size("dp")
    order_rows = jnp.argsort(packing_plan[0])
    send_hidden = jnp.take(hidden_rows, order_rows, axis=0)
    send_query = jnp.take(query_rows, order_rows, axis=0)
    packed_hidden, packed_query = (
        lax.all_to_all(send_hidden, "dp", split_axis=0, concat_axis=0, tiled=True),
        lax.all_to_all(send_query, "dp", split_axis=0, concat_axis=0, tiled=True),
    )
    projected = inner_rows(packed_hidden, projection)
    positions = part_index * row_count + jnp.arange(row_count, dtype=jnp.int32)
    cosine_table, sine_table = rotary_tables(positions, HEAD_DIM)
    key_width = KV_HEADS * HEAD_DIM
    key_heads = rotate_forward(
        projected[:, :key_width].reshape(row_count, KV_HEADS, HEAD_DIM), cosine_table, sine_table
    ).astype(jnp.bfloat16)
    values = projected[:, key_width:].reshape(row_count, KV_HEADS, HEAD_DIM).astype(jnp.bfloat16)
    repeats = split_size // KV_HEADS
    key_slots = jnp.repeat(key_heads, repeats, axis=1).reshape(row_count, split_size * HEAD_DIM)
    value_slots = jnp.repeat(values, repeats, axis=1).reshape(row_count, split_size * HEAD_DIM)
    local_query, local_keys, local_values = (
        lax.all_to_all(packed_query, "ctx", split_axis=1, concat_axis=0, tiled=True),
        lax.all_to_all(key_slots, "ctx", split_axis=1, concat_axis=0, tiled=True),
        lax.all_to_all(value_slots, "ctx", split_axis=1, concat_axis=0, tiled=True),
    )
    local_grad = lax.all_to_all(out_grad, "ctx", split_axis=1, concat_axis=0, tiled=True)
    length = local_query.shape[0]
    block_rows = math.gcd(length, 512)
    block_count = length // block_rows
    documents = document_ids[0]
    head_count = local_query.shape[1] // HEAD_DIM
    starts = jnp.arange(block_count, dtype=jnp.int32) * block_rows
    key_total = jnp.zeros((length, HEAD_DIM), jnp.float32)
    value_total = jnp.zeros((length, HEAD_DIM), jnp.float32)
    attended_parts = []
    query_parts = []
    for head_index in range(head_count):
        query_blocks = local_query[:, head_index * HEAD_DIM : (head_index + 1) * HEAD_DIM].reshape(
            block_count, block_rows, HEAD_DIM
        )
        grad_blocks = local_grad[:, head_index * HEAD_DIM : (head_index + 1) * HEAD_DIM].reshape(
            block_count, block_rows, HEAD_DIM
        )

        def block_step(carry_pair, inputs):
            query_block, grad_block, block_start = inputs
            query_index = block_start + jnp.arange(block_rows, dtype=jnp.int32)
            query_document = lax.dynamic_slice_in_dim(documents, block_start, block_rows)
            attended_block, query_block_grad, key_part, value_part = block_terms(
                query_block,
                grad_block,
                local_keys,
                local_values,
                query_index,
                query_document,
                documents,
            )
            return (
                (carry_pair[0] + key_part, carry_pair[1] + value_part),
                (attended_block, query_block_grad),
            )

        (key_total, value_total), (attended_blocks, query_grad_blocks) = lax.scan(
            block_step, (key_total, value_total), (query_blocks, grad_blocks, starts)
        )
        attended_parts.append(attended_blocks.reshape(length, HEAD_DIM))
        query_parts.append(query_grad_blocks.reshape(length, HEAD_DIM))
    local_attended = jnp.concatenate(attended_parts, axis=1)
    local_query_grad = jnp.concatenate(query_parts, axis=1)
    attended = lax.all_to_all(local_attended, "ctx", split_axis=0, concat_axis=1, tiled=True)
    query_grad = lax.all_to_all(local_query_grad, "ctx", split_axis=0, concat_axis=1, tiled=True)
    key_slots_grad, value_slots_grad = (
        lax.all_to_all(key_total, "ctx", split_axis=0, concat_axis=1, tiled=True),
        lax.all_to_all(value_total, "ctx", split_axis=0, concat_axis=1, tiled=True),
    )
    key_grad = (
        key_slots_grad.reshape(row_count, KV_HEADS, repeats, HEAD_DIM)
        .sum(axis=2)
        .astype(jnp.bfloat16)
    )
    value_grad = (
        value_slots_grad.reshape(row_count, KV_HEADS, repeats, HEAD_DIM)
        .sum(axis=2)
        .astype(jnp.bfloat16)
    )
    key_back = rotate_adjoint(key_grad.astype(jnp.float32), cosine_table, sine_table).reshape(
        row_count, key_width
    )
    projected_grad = jnp.concatenate(
        [key_back, value_grad.reshape(row_count, key_width).astype(jnp.float32)], axis=1
    ).astype(jnp.bfloat16)
    hidden_grad = jnp.dot(projected_grad, projection, preferred_element_type=jnp.float32).astype(
        jnp.bfloat16
    )
    block_term = outer_rows(projected_grad, packed_hidden)
    partial_sum = lax.psum_scatter(
        block_term.astype(jnp.bfloat16), "ctx", scatter_dimension=1, tiled=True
    ).astype(jnp.float32)
    weight_grad = lax.psum_scatter(partial_sum, "dp", scatter_dimension=0, tiled=True)
    weight_grad = weight_grad / sequences
    return (attended, query_grad, hidden_grad, weight_grad)


VMEM = pltpu.VMEM
SMEM = pltpu.SMEM
SIDES = 2


def vmem_specs(count):
    return [pl.BlockSpec(memory_space=VMEM)] * count


def any_specs(count):
    return [pl.BlockSpec(memory_space=pl.ANY)] * count


def begin(pairs, semaphores):
    copies = [pltpu.make_async_copy(source, target, semaphores.at[i]) for i, (source, target) in enumerate(pairs)]
    for copy in copies:
        copy.start()
    return copies


def finish(copies):
    for copy in copies:
        copy.wait()


def kernel_params(mebibytes):
    return pltpu.CompilerParams(vmem_limit_bytes=mebibytes * 2**20)


def struct(shape, dtype=jnp.bfloat16):
    return jax.ShapeDtypeStruct(shape, dtype)


def cost(flops, count, transcendentals=0):
    return pl.CostEstimate(flops=flops, bytes_accessed=count, transcendentals=transcendentals)


def pack_kernel(dp, plan_ref, query_ref, hidden_ref, cos_ref, sin_ref, proj_ref, qkv_ref, hid_ref, proj_s, sorted_s, sems):
    steps = proj_s.shape[0]
    copies = begin([(proj_ref.at[i], proj_s.at[i]) for i in range(steps)], sems)
    rows, width = hidden_ref.shape
    send = rows // dp
    query_width = query_ref.shape[1] // KV_HEADS
    quarter = width // KV_HEADS
    slot = lax.broadcasted_iota(jnp.int32, (rows, rows), 0)
    select = (plan_ref[...] == slot).astype(jnp.bfloat16)
    for group in range(KV_HEADS):
        hidden = hidden_ref[:, group * quarter : (group + 1) * quarter]
        part = jnp.dot(select, hidden, preferred_element_type=jnp.float32)
        sorted_s[group * quarter : (group + 1) * quarter, :] = part.T.astype(jnp.bfloat16)
        part = part.astype(jnp.bfloat16)
        query = query_ref[:, group * query_width : (group + 1) * query_width]
        query = jnp.dot(select, query, preferred_element_type=jnp.float32).astype(jnp.bfloat16)
        for a in range(dp):
            hid_ref[a * KV_HEADS + group] = part[a * send : (a + 1) * send]
            qkv_ref[a * KV_HEADS + group, :, 0:query_width] = query[a * send : (a + 1) * send]
    cosine = jnp.concatenate([cos_ref[...]] * 2, axis=1)
    sine = jnp.concatenate([-sin_ref[...], sin_ref[...]], axis=1)
    heads = proj_s.shape[1] // HEAD_DIM
    for step in range(steps):
        copies[step].wait()
        block = jnp.dot(proj_s[step], sorted_s[...], preferred_element_type=jnp.float32)
        for t in range(heads):
            head = step * heads + t
            is_value, group = head // KV_HEADS, head % KV_HEADS
            start = query_width + is_value * HEAD_DIM
            head_rows = block[t * HEAD_DIM : (t + 1) * HEAD_DIM, :].T
            for a in range(dp):
                x = head_rows[a * send : (a + 1) * send]
                if not is_value:
                    x = x * cosine + pltpu.roll(x, HEAD_DIM // 2, 1) * sine
                qkv_ref[a * KV_HEADS + group, :, start : start + HEAD_DIM] = x.astype(jnp.bfloat16)


def pack_rows(dp, plan, query, hidden, cosine, sine, projection):
    rows, width = hidden.shape
    send = rows // dp
    proj_rows = 2 * HEAD_DIM
    steps = projection.shape[0] // proj_rows
    qkv_shape = (dp * KV_HEADS, send, query.shape[1] // KV_HEADS + 2 * HEAD_DIM)
    hid_shape = (dp * KV_HEADS, send, width // KV_HEADS)
    return pl.pallas_call(
        functools.partial(pack_kernel, dp),
        in_specs=vmem_specs(5) + any_specs(1),
        out_specs=vmem_specs(2),
        out_shape=[struct(qkv_shape), struct(hid_shape)],
        scratch_shapes=[
            VMEM((steps, proj_rows, width), jnp.bfloat16),
            VMEM((width, rows), jnp.bfloat16),
            pltpu.SemaphoreType.DMA((steps,)),
        ],
        cost_estimate=cost(2 * rows * width * projection.shape[0], 2 * (projection.size + 3 * hidden.size)),
        name="pack_rows",
    )(plan, query, hidden, cosine, sine, projection.reshape(steps, proj_rows, width))


def split_kernel(group_ref, in_ref, *out_refs):
    width = out_refs[0].shape[1]
    for e, out_ref in enumerate(out_refs):
        at = jnp.bitwise_xor(group_ref[0], e) * width
        out_ref[...] = in_ref[:, pl.ds(pl.multiple_of(at, width), width)]


def split_columns(group, array):
    rows, width = array.shape
    return pl.pallas_call(
        split_kernel,
        in_specs=[pl.BlockSpec(memory_space=SMEM)] + vmem_specs(1),
        out_specs=vmem_specs(KV_HEADS),
        out_shape=[struct((rows, width // KV_HEADS))] * KV_HEADS,
        cost_estimate=cost(0, 4 * array.size),
        name="split_columns",
    )(group, array)


def join_kernel(group_ref, *refs):
    pieces, outs, sems = refs[:KV_HEADS], refs[KV_HEADS:-1], refs[-1]
    width = pieces[0].shape[1] // len(outs)
    pairs = []
    for e, piece in enumerate(pieces):
        at = pl.multiple_of(jnp.bitwise_xor(group_ref[0], e) * width, width)
        for k, out_ref in enumerate(outs):
            pairs.append((piece.at[:, pl.ds(k * width, width)], out_ref.at[:, pl.ds(at, width)]))
    finish(begin(pairs, sems))


def join_columns(group, pieces, outs):
    rows, width = pieces[0].shape
    return pl.pallas_call(
        join_kernel,
        in_specs=[pl.BlockSpec(memory_space=SMEM)] + any_specs(KV_HEADS),
        out_specs=vmem_specs(outs),
        out_shape=[struct((rows, KV_HEADS * width // outs))] * outs,
        scratch_shapes=[pltpu.SemaphoreType.DMA((KV_HEADS * outs,))],
        compiler_params=kernel_params(8),
        cost_estimate=cost(0, 4 * KV_HEADS * rows * width),
        name="join_columns",
    )(group, *pieces)


def attend_kernel(dp, index_ref, qkv_ref, kv_ref, *refs):
    grads = refs[:KV_HEADS]
    doc_ref = refs[KV_HEADS]
    outs = refs[KV_HEADS + 1 : 2 * KV_HEADS + 1]
    keep_ref, send_ref, key_s, value_s, key_t, value_t, query_s, grad_s, dk_s, dv_s, out_s, doc_s = refs[2 * KV_HEADS + 1 :]
    which, group, side = index_ref[0], index_ref[1], index_ref[2]
    send = qkv_ref.shape[1]
    rows = dp * send
    width = qkv_ref.shape[2] - 2 * HEAD_DIM
    heads = width // HEAD_DIM
    ctx = KV_HEADS * SIDES
    score_scale = HEAD_DIM ** (-0.5)
    power = score_scale * math.log2(math.e)
    for e in range(KV_HEADS):
        zone = jnp.bitwise_xor(group, e)
        for head in range(heads):
            grad_s[zone, head * rows : (head + 1) * rows, :] = grads[e][:, head * HEAD_DIM : (head + 1) * HEAD_DIM]
            for s in range(dp):
                query_s[e, head * rows + s * send : head * rows + (s + 1) * send, :] = qkv_ref[
                    s * KV_HEADS + e, :, head * HEAD_DIM : (head + 1) * HEAD_DIM
                ]
    for s in range(dp):
        for zone in range(KV_HEADS):
            piece = s * KV_HEADS + zone
            own = pl.ds(pl.multiple_of((zone * SIDES + side) * rows + s * send, send), send)
            other = pl.ds(pl.multiple_of((zone * SIDES + 1 - side) * rows + s * send, send), send)
            key_s[own, :] = qkv_ref[piece, :, width : width + HEAD_DIM]
            value_s[own, :] = qkv_ref[piece, :, width + HEAD_DIM :]
            key_s[other, :] = kv_ref[piece, :, 0:HEAD_DIM]
            value_s[other, :] = kv_ref[piece, :, HEAD_DIM:]
    for c in range(ctx):
        part = slice(c * rows, (c + 1) * rows)
        key_t[:, part] = key_s[part, :].astype(jnp.float32).T.astype(jnp.bfloat16)
        value_t[:, part] = value_s[part, :].astype(jnp.float32).T.astype(jnp.bfloat16)
        doc_s[part, :] = jnp.broadcast_to(doc_ref[c].astype(jnp.float32), (rows, rows)).T
    for zone in reversed(range(KV_HEADS)):
        hi = (zone + 1) * SIDES * rows
        start = pl.multiple_of((zone * SIDES + side) * rows, rows)
        keys = key_s[0:hi, :]
        values = value_s[0:hi, :]
        key_index = lax.broadcasted_iota(jnp.int32, (hi, rows), 0)
        query_index = lax.broadcasted_iota(jnp.int32, (hi, rows), 1) + start
        allowed = (key_index <= query_index) & (doc_s[0:hi, :] == doc_ref[zone * SIDES + side].astype(jnp.float32))
        bias = jnp.where(allowed, 0.0, MASK_VALUE)
        query = query_s[zone]
        grad = grad_s[zone]
        scores = inner_rows(keys, query) + jnp.concatenate([bias] * heads, axis=1)
        row_max = jnp.max(scores, axis=0, keepdims=True)
        exponent = jnp.exp2((scores - row_max) * power)
        inverse = 1.0 / jnp.sum(exponent, axis=0, keepdims=True)
        probability = exponent * inverse
        rounded = probability.astype(jnp.bfloat16)
        attended = jnp.dot(value_t[:, 0:hi], rounded, preferred_element_type=jnp.float32)
        weighted = inner_rows(values, grad) * probability
        delta = jnp.sum(weighted, axis=0, keepdims=True)
        grad_score = (weighted - probability * delta).astype(jnp.bfloat16)
        query_grad = jnp.dot(key_t[:, 0:hi], grad_score, preferred_element_type=jnp.float32) * score_scale
        dk_part = jnp.dot(grad_score, query, preferred_element_type=jnp.float32)
        dv_part = jnp.dot(rounded, grad, preferred_element_type=jnp.float32)
        if zone == KV_HEADS - 1:
            dk_s[0:hi, :] = dk_part
            dv_s[0:hi, :] = dv_part
        else:
            dk_s[0:hi, :] += dk_part
            dv_s[0:hi, :] += dv_part
        for head in range(heads):
            part = slice(head * rows, (head + 1) * rows)
            out_s[zone, :, head * HEAD_DIM : (head + 1) * HEAD_DIM] = attended[:, part].T.astype(jnp.bfloat16)
            out_s[zone, :, width + head * HEAD_DIM : width + (head + 1) * HEAD_DIM] = (
                query_grad[:, part].T.astype(jnp.bfloat16)
            )
    for e in range(KV_HEADS):
        outs[e][...] = out_s[jnp.bitwise_xor(group, e)]

    @pl.when(which == 0)
    def _():
        keep_ref[...] = dk_s[...] * score_scale
        send_ref[...] = dv_s[...].astype(send_ref.dtype)

    @pl.when(which != 0)
    def _():
        keep_ref[...] = dv_s[...]
        send_ref[...] = (dk_s[...] * score_scale).astype(send_ref.dtype)


def attend(dp, index, qkv, kv, grads, documents):
    rows, width = grads[0].shape
    heads = width // HEAD_DIM
    length = KV_HEADS * SIDES * rows
    pairs = heads * length * length // 4
    return pl.pallas_call(
        functools.partial(attend_kernel, dp),
        in_specs=[pl.BlockSpec(memory_space=SMEM)] + vmem_specs(KV_HEADS + 3),
        out_specs=vmem_specs(KV_HEADS + 2),
        out_shape=[struct((rows, 2 * width))] * KV_HEADS
        + [struct((length, HEAD_DIM), jnp.float32), struct((length, HEAD_DIM))],
        scratch_shapes=[
            VMEM((length, HEAD_DIM), jnp.bfloat16),
            VMEM((length, HEAD_DIM), jnp.bfloat16),
            VMEM((HEAD_DIM, length), jnp.bfloat16),
            VMEM((HEAD_DIM, length), jnp.bfloat16),
            VMEM((KV_HEADS, heads * rows, HEAD_DIM), jnp.bfloat16),
            VMEM((KV_HEADS, heads * rows, HEAD_DIM), jnp.bfloat16),
            VMEM((length, HEAD_DIM), jnp.float32),
            VMEM((length, HEAD_DIM), jnp.float32),
            VMEM((KV_HEADS, rows, 2 * width), jnp.bfloat16),
            VMEM((length, rows), jnp.float32),
        ],
        cost_estimate=cost(10 * pairs * HEAD_DIM, 2 * (kv.size + 4 * qkv.size), pairs),
        name="attend",
    )(index, qkv, kv, *grads, documents.reshape(KV_HEADS * SIDES, 1, rows))


def combine_kernel(dp, index_ref, keep_ref, recv_any, cos_ref, sin_ref, out_ref, recv_ref, sems):
    side = index_ref[2]
    finish(begin([(recv_any, recv_ref)], sems))
    length = keep_ref.shape[0]
    ctx = KV_HEADS * SIDES
    send = length // (dp * ctx)
    total = (keep_ref[...] + recv_ref[...].astype(jnp.float32)).astype(jnp.bfloat16).astype(jnp.float32)
    back = total * cos_ref[...] + pltpu.roll(total, HEAD_DIM // 2, 1) * sin_ref[...]
    back = back.astype(jnp.bfloat16)
    for c in range(ctx):
        for s in range(dp):
            at = (c * dp + s) * send
            half = jnp.bitwise_xor(side, c % SIDES) * (length // SIDES)
            to = pl.multiple_of(half + (s * KV_HEADS + c // SIDES) * send, send)
            out_ref[pl.ds(to, send), :] = back[at : at + send]


def combine(dp, index, keep, recv, cosine, sine):
    return pl.pallas_call(
        functools.partial(combine_kernel, dp),
        in_specs=[pl.BlockSpec(memory_space=SMEM)] + vmem_specs(1) + any_specs(1) + vmem_specs(2),
        out_specs=pl.BlockSpec(memory_space=VMEM),
        out_shape=struct(keep.shape),
        scratch_shapes=[VMEM(recv.shape, recv.dtype), pltpu.SemaphoreType.DMA((1,))],
        compiler_params=kernel_params(12),
        cost_estimate=cost(4 * keep.size, 16 * keep.size),
        name="combine",
    )(index, keep, recv, cosine, sine)


def product_kernel(dp, index_ref, *refs):
    group, side, high = index_ref[1], index_ref[2], index_ref[3]
    grads = refs[:KV_HEADS]
    hid_any = refs[KV_HEADS : KV_HEADS + SIDES]
    out_refs = refs[KV_HEADS + SIDES : KV_HEADS + SIDES + dp]
    own_ref, other_ref, heads_s, own_s, other_s, sems = refs[KV_HEADS + SIDES + dp :]
    hid_refs = (own_s, other_s)
    ctx = KV_HEADS * SIDES
    length = grads[0].shape[0]
    send = length // (dp * ctx)
    pairs = [(grads[e], heads_s.at[jnp.bitwise_xor(group, e)]) for e in range(KV_HEADS)]
    copies = begin(pairs + list(zip(hid_any, hid_refs)), sems)
    finish(copies[:KV_HEADS])
    part = length // SIDES
    columns = hid_refs[0].shape[1] // SIDES
    for s in range(dp):
        at = pl.multiple_of((s * KV_HEADS + group) * send, send)
        own, other = pl.ds(at, send), pl.ds(part + at, send)
        for head in range(KV_HEADS):
            cols = slice(head * HEAD_DIM, (head + 1) * HEAD_DIM)
            own_ref[s * send : (s + 1) * send, cols] = heads_s[head, own, :]
            other_ref[s * send : (s + 1) * send, cols] = heads_s[head, other, :]
    finish(copies[KV_HEADS:])
    halves = dp // SIDES
    per = KV_HEADS // halves
    for ek in range(halves):
        first = jnp.bitwise_xor(high, ek) * per
        for t in range(per):
            left = heads_s[first + t]
            for ey in range(SIDES):
                window = pl.ds(pl.multiple_of(jnp.bitwise_xor(side, ey) * columns, columns), columns)
                total = outer_rows(left[:part], hid_refs[0][:, window]) + outer_rows(left[part:], hid_refs[1][:, window])
                out_refs[ek * SIDES + ey][t * HEAD_DIM : (t + 1) * HEAD_DIM, :] = total.astype(jnp.bfloat16)


def product(dp, index, grads, hid_own, hid_other):
    length = grads[0].shape[0]
    columns = hid_own.shape[1] // SIDES
    rows = length // (KV_HEADS * SIDES)
    block = (2 * KV_HEADS * HEAD_DIM // dp, columns)
    return pl.pallas_call(
        functools.partial(product_kernel, dp),
        in_specs=[pl.BlockSpec(memory_space=SMEM)] + any_specs(KV_HEADS + SIDES),
        out_specs=vmem_specs(dp + 2),
        out_shape=[struct(block)] * dp + [struct((rows, KV_HEADS * HEAD_DIM))] * 2,
        scratch_shapes=[
            VMEM((KV_HEADS, length, HEAD_DIM), jnp.bfloat16),
            VMEM(hid_own.shape, jnp.bfloat16),
            VMEM(hid_other.shape, jnp.bfloat16),
            pltpu.SemaphoreType.DMA((KV_HEADS + SIDES,)),
        ],
        compiler_params=kernel_params(20),
        cost_estimate=cost(
            4 * length * KV_HEADS * HEAD_DIM * columns,
            2 * (2 * length * columns + length * KV_HEADS * HEAD_DIM + 4 * columns * HEAD_DIM * KV_HEADS),
        ),
        name="weight_product",
    )(index, *grads, hid_own, hid_other)


def hidden_kernel(which_ref, own_ref, other_ref, own_proj_ref, other_proj_ref, out_ref):
    total = jnp.dot(own_ref[...], own_proj_ref[0], preferred_element_type=jnp.float32)
    total += jnp.dot(other_ref[...], other_proj_ref[0], preferred_element_type=jnp.float32)
    out_ref[...] = total.astype(out_ref.dtype)


def hidden_product(which, own, other, projection):
    rows, half = own.shape
    width = projection.shape[1]
    columns = math.gcd(width, 1024)
    halves = projection.reshape(2, half, width)
    spec = pltpu.PrefetchScalarGridSpec(
        num_scalar_prefetch=1,
        grid=(width // columns,),
        in_specs=[
            pl.BlockSpec((rows, half), lambda i, w: (0, 0)),
            pl.BlockSpec((rows, half), lambda i, w: (0, 0)),
            pl.BlockSpec((1, half, columns), lambda i, w: (w[0], 0, i)),
            pl.BlockSpec((1, half, columns), lambda i, w: (1 - w[0], 0, i)),
        ],
        out_specs=pl.BlockSpec((rows, columns), lambda i, w: (0, i)),
    )
    return pl.pallas_call(
        hidden_kernel,
        grid_spec=spec,
        out_shape=struct((rows, width)),
        compiler_params=kernel_params(16),
        cost_estimate=cost(4 * rows * half * width, 2 * projection.size + 4 * rows * width),
        name="hidden_product",
    )(which, own, other, halves, halves)


AXES = ("dp", "group", "side")


def paired_body(hidden_rows, query_rows, out_grad, projection, packing_plan, document_ids):
    rows, width = hidden_rows.shape
    dp = lax.axis_size("dp")
    ctx = KV_HEADS * SIDES
    a, group, side = (lax.axis_index(name) for name in AXES)
    block_id = group * SIDES + side
    send = rows // dp
    length = rows * ctx
    which = jnp.bitwise_xor(side, a % SIDES)
    index = jnp.stack([which, group, side, a // SIDES]).astype(jnp.int32)
    group_index = group.reshape(1)

    def move(value, target):
        flat = lambda i, g, p: (i * KV_HEADS + g) * SIDES + p
        moves = [
            (flat(i, g, p), flat(*target(i, g, p)))
            for i in range(dp)
            for g in range(KV_HEADS)
            for p in range(SIDES)
        ]
        return lax.ppermute(value, AXES, moves)

    def spread(pieces):
        return [pieces[0]] + [move(pieces[e], lambda i, g, p, e=e: (i, g ^ e, p)) for e in range(1, KV_HEADS)]

    other_side = lambda i, g, p: (i, g, 1 - p)
    scatter = lambda value, axes: lax.all_to_all(value, axes, split_axis=0, concat_axis=0, tiled=True)

    grads_in = split_columns(group_index, out_grad)
    packing_plan, grads_in = lax.optimization_barrier((packing_plan, grads_in))
    grads_in = spread(grads_in)
    slot = block_id * rows + a * send + jnp.arange(send, dtype=jnp.int32)
    cosine, sine = rotary_tables(slot, HEAD_DIM)
    qkv_pieces, hid_pieces = pack_rows(dp, packing_plan, query_rows, hidden_rows, cosine, sine, projection)
    qkv = scatter(qkv_pieces, AXES[:2])
    kv_other = move(qkv[:, :, query_rows.shape[1] // KV_HEADS :], other_side)
    qkv, hid_pieces = lax.optimization_barrier((qkv, hid_pieces))
    hid = scatter(hid_pieces, AXES[:2])

    *outputs, keep, give = attend(dp, index, qkv, kv_other, grads_in, document_ids)
    recv = move(give, other_side)
    cosine, sine = rotary_tables(jnp.arange(length, dtype=jnp.int32), HEAD_DIM)
    cosine = jnp.where(which == 0, jnp.concatenate([cosine, cosine], axis=1), 1.0)
    sine = jnp.where(which == 0, jnp.concatenate([sine, -sine], axis=1), 0.0)
    piece = combine(dp, index, keep, recv, cosine, sine)
    hid_own = hid.reshape(length // SIDES, width // KV_HEADS)
    hid_other = move(hid_own, other_side)
    shift = lambda value, e: move(value, lambda i, g, p: (i, g ^ e, p))
    grads = [piece, shift(piece, 1), shift(piece, 2)]
    grads.append(shift(grads[2], 1))

    outputs, *early = lax.optimization_barrier((outputs, *grads[:3]))
    grads = [*early, grads[3]]
    back = spread(outputs)
    products = product(dp, index, grads, hid_own, hid_other)
    own_rows, other_rows = products[dp], products[dp + 1]
    other_half = move(other_rows, other_side)
    half = dp // SIDES
    blocks = [
        move(
            products[ek * SIDES + ey],
            lambda i, g, p, ek=ek, ey=ey: ((p ^ (i % SIDES)) * half + ((i // SIDES) ^ ek), g, p ^ ey),
        )
        for ek in range(half)
        for ey in range(SIDES)
    ]

    hidden_grad = hidden_product(which.reshape(1), own_rows, other_half, projection)
    weight_grad = functools.reduce(jnp.add, [b.astype(jnp.float32) for b in blocks]) / dp

    back, hidden_grad = lax.optimization_barrier((back, hidden_grad))
    attended, query_grad = join_columns(group_index, back, 2)
    return (attended, query_grad, hidden_grad, weight_grad)


def paired(mesh):
    dp, ctx = mesh.shape["dp"], mesh.shape["ctx"]
    return ctx == KV_HEADS * SIDES and dp in (2, 4, 8)


def solution(mesh):
    if paired(mesh):
        body = paired_body
        inner = Mesh(mesh.devices.reshape(mesh.shape["dp"], KV_HEADS, SIDES), AXES)
        ctx = AXES[1:]
    else:
        body = general_body
        inner = mesh
        ctx = ("ctx",)
    rows = P(("dp", *ctx), None)
    step = jax.shard_map(
        body,
        mesh=inner,
        in_specs=(rows, rows, rows, P(), rows, P("dp", None)),
        out_specs=(rows, rows, rows, P("dp", ctx)),
        check_vma=False,
    )
    if body is general_body:
        return step

    return step
```

```python
import functools
import math

import jax
import jax.numpy as jnp
from jax import lax
from jax.experimental import pallas as pl
from jax.experimental.pallas import tpu as pltpu
from jax.sharding import Mesh, PartitionSpec as P

KV_HEADS = 4
HEAD_DIM = 128


ROPE_BASE = 500000.0
MASK_VALUE = -1e30


def rotary_tables(positions, head_width):
    half_width = head_width // 2
    exponent = jnp.arange(half_width, dtype=jnp.float32) * (-2.0 * math.log(ROPE_BASE) / head_width)
    angles = positions.astype(jnp.float32)[:, None] * jnp.exp(exponent)[None, :]
    return (jnp.cos(angles), jnp.sin(angles))


def rotate_forward(head_rows, cosine_table, sine_table):
    half_width = head_rows.shape[-1] // 2
    first_half = head_rows[..., :half_width]
    second_half = head_rows[..., half_width:]
    cosine_part = cosine_table[:, None, :]
    sine_part = sine_table[:, None, :]
    return jnp.concatenate(
        [
            first_half * cosine_part - second_half * sine_part,
            second_half * cosine_part + first_half * sine_part,
        ],
        axis=-1,
    )


def rotate_adjoint(head_grads, cosine_table, sine_table):
    half_width = head_grads.shape[-1] // 2
    first_half = head_grads[..., :half_width]
    second_half = head_grads[..., half_width:]
    cosine_part = cosine_table[:, None, :]
    sine_part = sine_table[:, None, :]
    return jnp.concatenate(
        [
            first_half * cosine_part + second_half * sine_part,
            second_half * cosine_part - first_half * sine_part,
        ],
        axis=-1,
    )


def inner_rows(left_side, right_side):
    return lax.dot_general(
        left_side, right_side, (((1,), (1,)), ((), ())), preferred_element_type=jnp.float32
    )


def outer_rows(left_side, right_side):
    return lax.dot_general(
        left_side, right_side, (((0,), (0,)), ((), ())), preferred_element_type=jnp.float32
    )


def block_terms(
    query_block, grad_block, key_rows, value_rows, query_index, query_document, key_document
):
    score_scale = key_rows.shape[1] ** (-0.5)
    scores = inner_rows(query_block, key_rows) * score_scale
    key_index = jnp.arange(key_rows.shape[0], dtype=jnp.int32)
    allowed = (key_index[None, :] <= query_index[:, None]) & (
        key_document[None, :] == query_document[:, None]
    )
    scores = jnp.where(allowed, scores, MASK_VALUE)
    row_max = jnp.max(scores, axis=1, keepdims=True)
    exponent = jnp.exp(scores - row_max)
    probability = exponent / jnp.sum(exponent, axis=1, keepdims=True)
    rounded = probability.astype(jnp.bfloat16)
    attended = jnp.dot(rounded, value_rows, preferred_element_type=jnp.float32).astype(jnp.bfloat16)
    grad_prob = inner_rows(grad_block, value_rows)
    delta_sum = jnp.sum(probability * grad_prob, axis=1, keepdims=True)
    grad_score = (probability * (grad_prob - delta_sum)).astype(jnp.bfloat16)
    query_grad = (
        jnp.dot(grad_score, key_rows, preferred_element_type=jnp.float32) * score_scale
    ).astype(jnp.bfloat16)
    key_part = outer_rows(grad_score, query_block) * score_scale
    value_part = outer_rows(rounded, grad_block)
    return (attended, query_grad, key_part, value_part)


def general_body(hidden_rows, query_rows, out_grad, projection, packing_plan, document_ids):
    row_count = hidden_rows.shape[0]
    split_size = lax.axis_size("ctx")
    part_index = lax.axis_index("ctx")
    sequences = lax.axis_size("dp")
    order_rows = jnp.argsort(packing_plan[0])
    send_hidden = jnp.take(hidden_rows, order_rows, axis=0)
    send_query = jnp.take(query_rows, order_rows, axis=0)
    packed_hidden, packed_query = (
        lax.all_to_all(send_hidden, "dp", split_axis=0, concat_axis=0, tiled=True),
        lax.all_to_all(send_query, "dp", split_axis=0, concat_axis=0, tiled=True),
    )
    projected = inner_rows(packed_hidden, projection)
    positions = part_index * row_count + jnp.arange(row_count, dtype=jnp.int32)
    cosine_table, sine_table = rotary_tables(positions, HEAD_DIM)
    key_width = KV_HEADS * HEAD_DIM
    key_heads = rotate_forward(
        projected[:, :key_width].reshape(row_count, KV_HEADS, HEAD_DIM), cosine_table, sine_table
    ).astype(jnp.bfloat16)
    values = projected[:, key_width:].reshape(row_count, KV_HEADS, HEAD_DIM).astype(jnp.bfloat16)
    repeats = split_size // KV_HEADS
    key_slots = jnp.repeat(key_heads, repeats, axis=1).reshape(row_count, split_size * HEAD_DIM)
    value_slots = jnp.repeat(values, repeats, axis=1).reshape(row_count, split_size * HEAD_DIM)
    local_query, local_keys, local_values = (
        lax.all_to_all(packed_query, "ctx", split_axis=1, concat_axis=0, tiled=True),
        lax.all_to_all(key_slots, "ctx", split_axis=1, concat_axis=0, tiled=True),
        lax.all_to_all(value_slots, "ctx", split_axis=1, concat_axis=0, tiled=True),
    )
    local_grad = lax.all_to_all(out_grad, "ctx", split_axis=1, concat_axis=0, tiled=True)
    length = local_query.shape[0]
    block_rows = math.gcd(length, 512)
    block_count = length // block_rows
    documents = document_ids[0]
    head_count = local_query.shape[1] // HEAD_DIM
    starts = jnp.arange(block_count, dtype=jnp.int32) * block_rows
    key_total = jnp.zeros((length, HEAD_DIM), jnp.float32)
    value_total = jnp.zeros((length, HEAD_DIM), jnp.float32)
    attended_parts = []
    query_parts = []
    for head_index in range(head_count):
        query_blocks = local_query[:, head_index * HEAD_DIM : (head_index + 1) * HEAD_DIM].reshape(
            block_count, block_rows, HEAD_DIM
        )
        grad_blocks = local_grad[:, head_index * HEAD_DIM : (head_index + 1) * HEAD_DIM].reshape(
            block_count, block_rows, HEAD_DIM
        )

        def block_step(carry_pair, inputs):
            query_block, grad_block, block_start = inputs
            query_index = block_start + jnp.arange(block_rows, dtype=jnp.int32)
            query_document = lax.dynamic_slice_in_dim(documents, block_start, block_rows)
            attended_block, query_block_grad, key_part, value_part = block_terms(
                query_block,
                grad_block,
                local_keys,
                local_values,
                query_index,
                query_document,
                documents,
            )
            return (
                (carry_pair[0] + key_part, carry_pair[1] + value_part),
                (attended_block, query_block_grad),
            )

        (key_total, value_total), (attended_blocks, query_grad_blocks) = lax.scan(
            block_step, (key_total, value_total), (query_blocks, grad_blocks, starts)
        )
        attended_parts.append(attended_blocks.reshape(length, HEAD_DIM))
        query_parts.append(query_grad_blocks.reshape(length, HEAD_DIM))
    local_attended = jnp.concatenate(attended_parts, axis=1)
    local_query_grad = jnp.concatenate(query_parts, axis=1)
    attended = lax.all_to_all(local_attended, "ctx", split_axis=0, concat_axis=1, tiled=True)
    query_grad = lax.all_to_all(local_query_grad, "ctx", split_axis=0, concat_axis=1, tiled=True)
    key_slots_grad, value_slots_grad = (
        lax.all_to_all(key_total, "ctx", split_axis=0, concat_axis=1, tiled=True),
        lax.all_to_all(value_total, "ctx", split_axis=0, concat_axis=1, tiled=True),
    )
    key_grad = (
        key_slots_grad.reshape(row_count, KV_HEADS, repeats, HEAD_DIM)
        .sum(axis=2)
        .astype(jnp.bfloat16)
    )
    value_grad = (
        value_slots_grad.reshape(row_count, KV_HEADS, repeats, HEAD_DIM)
        .sum(axis=2)
        .astype(jnp.bfloat16)
    )
    key_back = rotate_adjoint(key_grad.astype(jnp.float32), cosine_table, sine_table).reshape(
        row_count, key_width
    )
    projected_grad = jnp.concatenate(
        [key_back, value_grad.reshape(row_count, key_width).astype(jnp.float32)], axis=1
    ).astype(jnp.bfloat16)
    hidden_grad = jnp.dot(projected_grad, projection, preferred_element_type=jnp.float32).astype(
        jnp.bfloat16
    )
    block_term = outer_rows(projected_grad, packed_hidden)
    partial_sum = lax.psum_scatter(
        block_term.astype(jnp.bfloat16), "ctx", scatter_dimension=1, tiled=True
    ).astype(jnp.float32)
    weight_grad = lax.psum_scatter(partial_sum, "dp", scatter_dimension=0, tiled=True)
    weight_grad = weight_grad / sequences
    return (attended, query_grad, hidden_grad, weight_grad)


VMEM = pltpu.VMEM
SMEM = pltpu.SMEM
SIDES = 2


def vmem_specs(count):
    return [pl.BlockSpec(memory_space=VMEM)] * count


def any_specs(count):
    return [pl.BlockSpec(memory_space=pl.ANY)] * count


def begin(pairs, semaphores):
    copies = [pltpu.make_async_copy(source, target, semaphores.at[i]) for i, (source, target) in enumerate(pairs)]
    for copy in copies:
        copy.start()
    return copies


def finish(copies):
    for copy in copies:
        copy.wait()


def kernel_params(mebibytes):
    return pltpu.CompilerParams(vmem_limit_bytes=mebibytes * 2**20)


def struct(shape, dtype=jnp.bfloat16):
    return jax.ShapeDtypeStruct(shape, dtype)


def cost(flops, count, transcendentals=0):
    return pl.CostEstimate(flops=flops, bytes_accessed=count, transcendentals=transcendentals)


def pack_kernel(dp, plan_ref, query_ref, hidden_ref, cos_ref, sin_ref, proj_ref, qkv_ref, *refs):
    hid_refs, (proj_s, sorted_s, sems) = refs[:SIDES], refs[SIDES:]
    steps = proj_s.shape[0]
    copies = begin([(proj_ref.at[i], proj_s.at[i]) for i in range(steps)], sems)
    rows, width = hidden_ref.shape
    send = rows // dp
    query_width = query_ref.shape[1] // KV_HEADS
    quarter = width // KV_HEADS
    slot = lax.broadcasted_iota(jnp.int32, (rows, rows), 0)
    select = (plan_ref[...] == slot).astype(jnp.bfloat16)
    for group in range(KV_HEADS):
        hidden = hidden_ref[:, group * quarter : (group + 1) * quarter]
        part = jnp.dot(select, hidden, preferred_element_type=jnp.float32)
        sorted_s[group * quarter : (group + 1) * quarter, :] = part.T.astype(jnp.bfloat16)
        part = part.astype(jnp.bfloat16)
        query = query_ref[:, group * query_width : (group + 1) * query_width]
        query = jnp.dot(select, query, preferred_element_type=jnp.float32).astype(jnp.bfloat16)
        for a in range(dp):
            for half, hid_ref in enumerate(hid_refs):
                columns = slice(half * hid_ref.shape[2], (half + 1) * hid_ref.shape[2])
                hid_ref[a * KV_HEADS + group] = part[a * send : (a + 1) * send, columns]
            qkv_ref[a * KV_HEADS + group, :, 0:query_width] = query[a * send : (a + 1) * send]
    cosine = jnp.concatenate([cos_ref[...]] * 2, axis=1)
    sine = jnp.concatenate([-sin_ref[...], sin_ref[...]], axis=1)
    heads = proj_s.shape[1] // HEAD_DIM
    for step in range(steps):
        copies[step].wait()
        block = jnp.dot(proj_s[step], sorted_s[...], preferred_element_type=jnp.float32)
        for t in range(heads):
            head = step * heads + t
            is_value, group = head // KV_HEADS, head % KV_HEADS
            start = query_width + is_value * HEAD_DIM
            head_rows = block[t * HEAD_DIM : (t + 1) * HEAD_DIM, :].T
            for a in range(dp):
                x = head_rows[a * send : (a + 1) * send]
                if not is_value:
                    x = x * cosine + pltpu.roll(x, HEAD_DIM // 2, 1) * sine
                qkv_ref[a * KV_HEADS + group, :, start : start + HEAD_DIM] = x.astype(jnp.bfloat16)


def pack_rows(dp, plan, query, hidden, cosine, sine, projection):
    rows, width = hidden.shape
    send = rows // dp
    proj_rows = 2 * HEAD_DIM
    steps = projection.shape[0] // proj_rows
    qkv_shape = (dp * KV_HEADS, send, query.shape[1] // KV_HEADS + 2 * HEAD_DIM)
    hid_shape = (dp * KV_HEADS, send, width // KV_HEADS // SIDES)
    return pl.pallas_call(
        functools.partial(pack_kernel, dp),
        in_specs=vmem_specs(5) + any_specs(1),
        out_specs=vmem_specs(1 + SIDES),
        out_shape=[struct(qkv_shape)] + [struct(hid_shape)] * SIDES,
        scratch_shapes=[
            VMEM((steps, proj_rows, width), jnp.bfloat16),
            VMEM((width, rows), jnp.bfloat16),
            pltpu.SemaphoreType.DMA((steps,)),
        ],
        cost_estimate=cost(2 * rows * width * projection.shape[0], 2 * (projection.size + 3 * hidden.size)),
        name="pack_rows",
    )(plan, query, hidden, cosine, sine, projection.reshape(steps, proj_rows, width))


def split_kernel(group_ref, in_ref, *out_refs):
    width = out_refs[0].shape[1]
    for e, out_ref in enumerate(out_refs):
        at = jnp.bitwise_xor(group_ref[0], e) * width
        out_ref[...] = in_ref[:, pl.ds(pl.multiple_of(at, width), width)]


def split_columns(group, array):
    rows, width = array.shape
    return pl.pallas_call(
        split_kernel,
        in_specs=[pl.BlockSpec(memory_space=SMEM)] + vmem_specs(1),
        out_specs=vmem_specs(KV_HEADS),
        out_shape=[struct((rows, width // KV_HEADS))] * KV_HEADS,
        cost_estimate=cost(0, 4 * array.size),
        name="split_columns",
    )(group, array)


def join_kernel(group_ref, *refs):
    pieces, outs, sems = refs[:KV_HEADS], refs[KV_HEADS:-1], refs[-1]
    width = pieces[0].shape[1] // len(outs)
    pairs = []
    for e, piece in enumerate(pieces):
        at = pl.multiple_of(jnp.bitwise_xor(group_ref[0], e) * width, width)
        for k, out_ref in enumerate(outs):
            pairs.append((piece.at[:, pl.ds(k * width, width)], out_ref.at[:, pl.ds(at, width)]))
    finish(begin(pairs, sems))


def join_columns(group, pieces, outs):
    rows, width = pieces[0].shape
    return pl.pallas_call(
        join_kernel,
        in_specs=[pl.BlockSpec(memory_space=SMEM)] + any_specs(KV_HEADS),
        out_specs=vmem_specs(outs),
        out_shape=[struct((rows, KV_HEADS * width // outs))] * outs,
        scratch_shapes=[pltpu.SemaphoreType.DMA((KV_HEADS * outs,))],
        compiler_params=kernel_params(8),
        cost_estimate=cost(0, 4 * KV_HEADS * rows * width),
        name="join_columns",
    )(group, *pieces)


def attend_kernel(dp, index_ref, qkv_ref, kv_ref, *refs):
    grads = refs[:KV_HEADS]
    doc_ref = refs[KV_HEADS]
    outs = refs[KV_HEADS + 1 : 2 * KV_HEADS + 1]
    keep_ref, send_ref, key_s, value_s, key_t, value_t, query_s, grad_s, dk_s, dv_s, out_s, doc_s = refs[2 * KV_HEADS + 1 :]
    which, group, side = index_ref[0], index_ref[1], index_ref[2]
    send = qkv_ref.shape[1]
    rows = dp * send
    width = qkv_ref.shape[2] - 2 * HEAD_DIM
    heads = width // HEAD_DIM
    ctx = KV_HEADS * SIDES
    score_scale = HEAD_DIM ** (-0.5)
    power = score_scale * math.log2(math.e)
    for e in range(KV_HEADS):
        zone = jnp.bitwise_xor(group, e)
        for head in range(heads):
            grad_s[zone, head * rows : (head + 1) * rows, :] = grads[e][:, head * HEAD_DIM : (head + 1) * HEAD_DIM]
            for s in range(dp):
                query_s[e, head * rows + s * send : head * rows + (s + 1) * send, :] = qkv_ref[
                    s * KV_HEADS + e, :, head * HEAD_DIM : (head + 1) * HEAD_DIM
                ]
    for s in range(dp):
        for zone in range(KV_HEADS):
            piece = s * KV_HEADS + zone
            own = pl.ds(pl.multiple_of((zone * SIDES + side) * rows + s * send, send), send)
            other = pl.ds(pl.multiple_of((zone * SIDES + 1 - side) * rows + s * send, send), send)
            key_s[own, :] = qkv_ref[piece, :, width : width + HEAD_DIM]
            value_s[own, :] = qkv_ref[piece, :, width + HEAD_DIM :]
            key_s[other, :] = kv_ref[piece, :, 0:HEAD_DIM]
            value_s[other, :] = kv_ref[piece, :, HEAD_DIM:]
    for c in range(ctx):
        part = slice(c * rows, (c + 1) * rows)
        key_t[:, part] = key_s[part, :].astype(jnp.float32).T.astype(jnp.bfloat16)
        value_t[:, part] = value_s[part, :].astype(jnp.float32).T.astype(jnp.bfloat16)
        doc_s[part, :] = jnp.broadcast_to(doc_ref[c].astype(jnp.float32), (rows, rows)).T
    for zone in reversed(range(KV_HEADS)):
        hi = (zone + 1) * SIDES * rows
        start = pl.multiple_of((zone * SIDES + side) * rows, rows)
        keys = key_s[0:hi, :]
        values = value_s[0:hi, :]
        key_index = lax.broadcasted_iota(jnp.int32, (hi, rows), 0)
        query_index = lax.broadcasted_iota(jnp.int32, (hi, rows), 1) + start
        allowed = (key_index <= query_index) & (doc_s[0:hi, :] == doc_ref[zone * SIDES + side].astype(jnp.float32))
        bias = jnp.where(allowed, 0.0, MASK_VALUE)
        query = query_s[zone]
        grad = grad_s[zone]
        scores = inner_rows(keys, query) + jnp.concatenate([bias] * heads, axis=1)
        row_max = jnp.max(scores, axis=0, keepdims=True)
        exponent = jnp.exp2((scores - row_max) * power)
        inverse = 1.0 / jnp.sum(exponent, axis=0, keepdims=True)
        probability = exponent * inverse
        rounded = probability.astype(jnp.bfloat16)
        attended = jnp.dot(value_t[:, 0:hi], rounded, preferred_element_type=jnp.float32)
        weighted = inner_rows(values, grad) * probability
        delta = jnp.sum(weighted, axis=0, keepdims=True)
        grad_score = (weighted - probability * delta).astype(jnp.bfloat16)
        query_grad = jnp.dot(key_t[:, 0:hi], grad_score, preferred_element_type=jnp.float32) * score_scale
        dk_part = jnp.dot(grad_score, query, preferred_element_type=jnp.float32)
        dv_part = jnp.dot(rounded, grad, preferred_element_type=jnp.float32)
        if zone == KV_HEADS - 1:
            dk_s[0:hi, :] = dk_part
            dv_s[0:hi, :] = dv_part
        else:
            dk_s[0:hi, :] += dk_part
            dv_s[0:hi, :] += dv_part
        for head in range(heads):
            part = slice(head * rows, (head + 1) * rows)
            out_s[zone, :, head * HEAD_DIM : (head + 1) * HEAD_DIM] = attended[:, part].T.astype(jnp.bfloat16)
            out_s[zone, :, width + head * HEAD_DIM : width + (head + 1) * HEAD_DIM] = (
                query_grad[:, part].T.astype(jnp.bfloat16)
            )
    for e in range(KV_HEADS):
        outs[e][...] = out_s[jnp.bitwise_xor(group, e)]

    @pl.when(which == 0)
    def _():
        keep_ref[...] = dk_s[...] * score_scale
        send_ref[...] = dv_s[...].astype(send_ref.dtype)

    @pl.when(which != 0)
    def _():
        keep_ref[...] = dv_s[...]
        send_ref[...] = (dk_s[...] * score_scale).astype(send_ref.dtype)


def attend(dp, index, qkv, kv, grads, documents):
    rows, width = grads[0].shape
    heads = width // HEAD_DIM
    length = KV_HEADS * SIDES * rows
    pairs = heads * length * length // 4
    return pl.pallas_call(
        functools.partial(attend_kernel, dp),
        in_specs=[pl.BlockSpec(memory_space=SMEM)] + vmem_specs(KV_HEADS + 3),
        out_specs=vmem_specs(KV_HEADS + 2),
        out_shape=[struct((rows, 2 * width))] * KV_HEADS
        + [struct((length, HEAD_DIM), jnp.float32), struct((length, HEAD_DIM))],
        scratch_shapes=[
            VMEM((length, HEAD_DIM), jnp.bfloat16),
            VMEM((length, HEAD_DIM), jnp.bfloat16),
            VMEM((HEAD_DIM, length), jnp.bfloat16),
            VMEM((HEAD_DIM, length), jnp.bfloat16),
            VMEM((KV_HEADS, heads * rows, HEAD_DIM), jnp.bfloat16),
            VMEM((KV_HEADS, heads * rows, HEAD_DIM), jnp.bfloat16),
            VMEM((length, HEAD_DIM), jnp.float32),
            VMEM((length, HEAD_DIM), jnp.float32),
            VMEM((KV_HEADS, rows, 2 * width), jnp.bfloat16),
            VMEM((length, rows), jnp.float32),
        ],
        cost_estimate=cost(10 * pairs * HEAD_DIM, 2 * (kv.size + 4 * qkv.size), pairs),
        name="attend",
    )(index, qkv, kv, *grads, documents.reshape(KV_HEADS * SIDES, 1, rows))


def combine_kernel(dp, index_ref, keep_ref, recv_any, cos_ref, sin_ref, out_ref, recv_ref, sems):
    side = index_ref[2]
    finish(begin([(recv_any, recv_ref)], sems))
    length = keep_ref.shape[0]
    ctx = KV_HEADS * SIDES
    send = length // (dp * ctx)
    total = (keep_ref[...] + recv_ref[...].astype(jnp.float32)).astype(jnp.bfloat16).astype(jnp.float32)
    back = total * cos_ref[...] + pltpu.roll(total, HEAD_DIM // 2, 1) * sin_ref[...]
    back = back.astype(jnp.bfloat16)
    for c in range(ctx):
        for s in range(dp):
            at = (c * dp + s) * send
            half = jnp.bitwise_xor(side, c % SIDES) * (length // SIDES)
            to = pl.multiple_of(half + (s * KV_HEADS + c // SIDES) * send, send)
            out_ref[pl.ds(to, send), :] = back[at : at + send]


def combine(dp, index, keep, recv, cosine, sine):
    return pl.pallas_call(
        functools.partial(combine_kernel, dp),
        in_specs=[pl.BlockSpec(memory_space=SMEM)] + vmem_specs(1) + any_specs(1) + vmem_specs(2),
        out_specs=pl.BlockSpec(memory_space=VMEM),
        out_shape=struct(keep.shape),
        scratch_shapes=[VMEM(recv.shape, recv.dtype), pltpu.SemaphoreType.DMA((1,))],
        compiler_params=kernel_params(12),
        cost_estimate=cost(4 * keep.size, 16 * keep.size),
        name="combine",
    )(index, keep, recv, cosine, sine)


def product_kernel(dp, index_ref, *refs):
    group, side, high = index_ref[1], index_ref[2], index_ref[3]
    grads = refs[:KV_HEADS]
    hid_any = refs[KV_HEADS : KV_HEADS + 2 * SIDES]
    out_refs = refs[KV_HEADS + 2 * SIDES : KV_HEADS + 2 * SIDES + dp]
    own_ref, other_ref, heads_s, own_s, other_s, sems = refs[KV_HEADS + 2 * SIDES + dp :]
    hid_refs = (own_s.at[0], own_s.at[1], other_s.at[0], other_s.at[1])
    ctx = KV_HEADS * SIDES
    length = grads[0].shape[0]
    send = length // (dp * ctx)
    pairs = [(grads[e], heads_s.at[jnp.bitwise_xor(group, e)]) for e in range(KV_HEADS)]
    copies = begin(pairs + list(zip(hid_any, hid_refs)), sems)
    finish(copies[:KV_HEADS])
    part = length // SIDES
    for s in range(dp):
        at = pl.multiple_of((s * KV_HEADS + group) * send, send)
        own, other = pl.ds(at, send), pl.ds(part + at, send)
        for head in range(KV_HEADS):
            cols = slice(head * HEAD_DIM, (head + 1) * HEAD_DIM)
            own_ref[s * send : (s + 1) * send, cols] = heads_s[head, own, :]
            other_ref[s * send : (s + 1) * send, cols] = heads_s[head, other, :]
    finish(copies[KV_HEADS:])
    halves = dp // SIDES
    per = KV_HEADS // halves
    for ek in range(halves):
        first = jnp.bitwise_xor(high, ek) * per
        for t in range(per):
            left = heads_s[first + t]
            for ey in range(SIDES):
                half = jnp.bitwise_xor(side, ey)
                total = outer_rows(left[:part], own_s[half]) + outer_rows(left[part:], other_s[half])
                out_refs[ek * SIDES + ey][t * HEAD_DIM : (t + 1) * HEAD_DIM, :] = total.astype(jnp.bfloat16)


def product(dp, index, grads, hid_own, hid_other):
    length = grads[0].shape[0]
    columns = hid_own[0].shape[1]
    rows = length // (KV_HEADS * SIDES)
    block = (2 * KV_HEADS * HEAD_DIM // dp, columns)
    return pl.pallas_call(
        functools.partial(product_kernel, dp),
        in_specs=[pl.BlockSpec(memory_space=SMEM)] + any_specs(KV_HEADS + 2 * SIDES),
        out_specs=vmem_specs(dp + 2),
        out_shape=[struct(block)] * dp + [struct((rows, KV_HEADS * HEAD_DIM))] * 2,
        scratch_shapes=[
            VMEM((KV_HEADS, length, HEAD_DIM), jnp.bfloat16),
            VMEM((SIDES, *hid_own[0].shape), jnp.bfloat16),
            VMEM((SIDES, *hid_own[0].shape), jnp.bfloat16),
            pltpu.SemaphoreType.DMA((KV_HEADS + 2 * SIDES,)),
        ],
        compiler_params=kernel_params(20),
        cost_estimate=cost(
            4 * length * KV_HEADS * HEAD_DIM * columns,
            2 * (2 * length * columns + length * KV_HEADS * HEAD_DIM + 4 * columns * HEAD_DIM * KV_HEADS),
        ),
        name="weight_product",
    )(index, *grads, *hid_own, *hid_other)


def hidden_kernel(which_ref, own_ref, other_ref, own_proj_ref, other_proj_ref, out_ref):
    total = jnp.dot(own_ref[...], own_proj_ref[0], preferred_element_type=jnp.float32)
    total += jnp.dot(other_ref[...], other_proj_ref[0], preferred_element_type=jnp.float32)
    out_ref[...] = total.astype(out_ref.dtype)


def hidden_product(which, own, other, projection):
    rows, half = own.shape
    width = projection.shape[1]
    columns = math.gcd(width, 1024)
    halves = projection.reshape(2, half, width)
    spec = pltpu.PrefetchScalarGridSpec(
        num_scalar_prefetch=1,
        grid=(width // columns,),
        in_specs=[
            pl.BlockSpec((rows, half), lambda i, w: (0, 0)),
            pl.BlockSpec((rows, half), lambda i, w: (0, 0)),
            pl.BlockSpec((1, half, columns), lambda i, w: (w[0], 0, i)),
            pl.BlockSpec((1, half, columns), lambda i, w: (1 - w[0], 0, i)),
        ],
        out_specs=pl.BlockSpec((rows, columns), lambda i, w: (0, i)),
    )
    return pl.pallas_call(
        hidden_kernel,
        grid_spec=spec,
        out_shape=struct((rows, width)),
        compiler_params=kernel_params(16),
        cost_estimate=cost(4 * rows * half * width, 2 * projection.size + 4 * rows * width),
        name="hidden_product",
    )(which, own, other, halves, halves)


AXES = ("dp", "group", "side")


def paired_body(hidden_rows, query_rows, out_grad, projection, packing_plan, document_ids):
    rows, _ = hidden_rows.shape
    dp = lax.axis_size("dp")
    ctx = KV_HEADS * SIDES
    a, group, side = (lax.axis_index(name) for name in AXES)
    block_id = group * SIDES + side
    send = rows // dp
    length = rows * ctx
    which = jnp.bitwise_xor(side, a % SIDES)
    index = jnp.stack([which, group, side, a // SIDES]).astype(jnp.int32)
    group_index = group.reshape(1)

    def move(value, target):
        flat = lambda i, g, p: (i * KV_HEADS + g) * SIDES + p
        moves = [
            (flat(i, g, p), flat(*target(i, g, p)))
            for i in range(dp)
            for g in range(KV_HEADS)
            for p in range(SIDES)
        ]
        return lax.ppermute(value, AXES, moves)

    def spread(pieces):
        return [pieces[0]] + [move(pieces[e], lambda i, g, p, e=e: (i, g ^ e, p)) for e in range(1, KV_HEADS)]

    other_side = lambda i, g, p: (i, g, 1 - p)
    scatter = lambda value, axes: lax.all_to_all(value, axes, split_axis=0, concat_axis=0, tiled=True)

    grads_in = split_columns(group_index, out_grad)
    packing_plan, grads_in = lax.optimization_barrier((packing_plan, grads_in))
    grads_in = spread(grads_in)
    slot = block_id * rows + a * send + jnp.arange(send, dtype=jnp.int32)
    cosine, sine = rotary_tables(slot, HEAD_DIM)
    qkv_pieces, *hid_pieces = pack_rows(dp, packing_plan, query_rows, hidden_rows, cosine, sine, projection)
    qkv = scatter(qkv_pieces, AXES[:2])
    kv_other = move(qkv[:, :, query_rows.shape[1] // KV_HEADS :], other_side)
    flat_rows = lambda value: value.reshape(length // SIDES, value.shape[2])
    qkv, first_half = lax.optimization_barrier((qkv, hid_pieces[0]))
    hid_own = [flat_rows(scatter(first_half, AXES[:2]))]

    *outputs, keep, give = attend(dp, index, qkv, kv_other, grads_in, document_ids)
    give, second_half = lax.optimization_barrier((give, hid_pieces[1]))
    recv = move(give, other_side)
    hid_own.append(flat_rows(scatter(second_half, AXES[:2])))
    cosine, sine = rotary_tables(jnp.arange(length, dtype=jnp.int32), HEAD_DIM)
    cosine = jnp.where(which == 0, jnp.concatenate([cosine, cosine], axis=1), 1.0)
    sine = jnp.where(which == 0, jnp.concatenate([sine, -sine], axis=1), 0.0)
    piece = combine(dp, index, keep, recv, cosine, sine)
    piece, hid_own[0] = lax.optimization_barrier((piece, hid_own[0]))
    hid_other = [move(hid_own[0], other_side)]
    hid_other.append(move(hid_own[1], other_side))
    shift = lambda value, e: move(value, lambda i, g, p: (i, g ^ e, p))
    grads = [piece, shift(piece, 1), shift(piece, 2)]
    grads.append(shift(grads[2], 1))

    outputs, *early = lax.optimization_barrier((outputs, *grads[:3]))
    grads = [*early, grads[3]]
    back = spread(outputs)
    products = product(dp, index, grads, hid_own, hid_other)
    own_rows, other_rows = products[dp], products[dp + 1]
    other_half = move(other_rows, other_side)
    half = dp // SIDES
    blocks = [
        move(
            products[ek * SIDES + ey],
            lambda i, g, p, ek=ek, ey=ey: ((p ^ (i % SIDES)) * half + ((i // SIDES) ^ ek), g, p ^ ey),
        )
        for ek in range(half)
        for ey in range(SIDES)
    ]

    hidden_grad = hidden_product(which.reshape(1), own_rows, other_half, projection)
    weight_grad = functools.reduce(jnp.add, [b.astype(jnp.float32) for b in blocks]) / dp

    back, hidden_grad = lax.optimization_barrier((back, hidden_grad))
    attended, query_grad = join_columns(group_index, back, 2)
    return (attended, query_grad, hidden_grad, weight_grad)


def paired(mesh):
    dp, ctx = mesh.shape["dp"], mesh.shape["ctx"]
    return ctx == KV_HEADS * SIDES and dp in (2, 4, 8)


def solution(mesh):
    if paired(mesh):
        body = paired_body
        inner = Mesh(mesh.devices.reshape(mesh.shape["dp"], KV_HEADS, SIDES), AXES)
        ctx = AXES[1:]
    else:
        body = general_body
        inner = mesh
        ctx = ("ctx",)
    rows = P(("dp", *ctx), None)
    step = jax.shard_map(
        body,
        mesh=inner,
        in_specs=(rows, rows, rows, P(), rows, P("dp", None)),
        out_specs=(rows, rows, rows, P("dp", ctx)),
        check_vma=False,
    )
    if body is general_body:
        return step

    return step
```

```python
import functools
import math

import jax
import jax.numpy as jnp
from jax import lax
from jax.experimental import pallas as pl
from jax.experimental.pallas import tpu as pltpu
from jax.sharding import Mesh, PartitionSpec as P

KV_HEADS = 4
HEAD_DIM = 128


ROPE_BASE = 500000.0
MASK_VALUE = -1e30


def rotary_tables(positions, head_width):
    half_width = head_width // 2
    exponent = jnp.arange(half_width, dtype=jnp.float32) * (-2.0 * math.log(ROPE_BASE) / head_width)
    angles = positions.astype(jnp.float32)[:, None] * jnp.exp(exponent)[None, :]
    return (jnp.cos(angles), jnp.sin(angles))


def rotate_forward(head_rows, cosine_table, sine_table):
    half_width = head_rows.shape[-1] // 2
    first_half = head_rows[..., :half_width]
    second_half = head_rows[..., half_width:]
    cosine_part = cosine_table[:, None, :]
    sine_part = sine_table[:, None, :]
    return jnp.concatenate(
        [
            first_half * cosine_part - second_half * sine_part,
            second_half * cosine_part + first_half * sine_part,
        ],
        axis=-1,
    )


def rotate_adjoint(head_grads, cosine_table, sine_table):
    half_width = head_grads.shape[-1] // 2
    first_half = head_grads[..., :half_width]
    second_half = head_grads[..., half_width:]
    cosine_part = cosine_table[:, None, :]
    sine_part = sine_table[:, None, :]
    return jnp.concatenate(
        [
            first_half * cosine_part + second_half * sine_part,
            second_half * cosine_part - first_half * sine_part,
        ],
        axis=-1,
    )


def inner_rows(left_side, right_side):
    return lax.dot_general(
        left_side, right_side, (((1,), (1,)), ((), ())), preferred_element_type=jnp.float32
    )


def outer_rows(left_side, right_side):
    return lax.dot_general(
        left_side, right_side, (((0,), (0,)), ((), ())), preferred_element_type=jnp.float32
    )


def block_terms(
    query_block, grad_block, key_rows, value_rows, query_index, query_document, key_document
):
    score_scale = key_rows.shape[1] ** (-0.5)
    scores = inner_rows(query_block, key_rows) * score_scale
    key_index = jnp.arange(key_rows.shape[0], dtype=jnp.int32)
    allowed = (key_index[None, :] <= query_index[:, None]) & (
        key_document[None, :] == query_document[:, None]
    )
    scores = jnp.where(allowed, scores, MASK_VALUE)
    row_max = jnp.max(scores, axis=1, keepdims=True)
    exponent = jnp.exp(scores - row_max)
    probability = exponent / jnp.sum(exponent, axis=1, keepdims=True)
    rounded = probability.astype(jnp.bfloat16)
    attended = jnp.dot(rounded, value_rows, preferred_element_type=jnp.float32).astype(jnp.bfloat16)
    grad_prob = inner_rows(grad_block, value_rows)
    delta_sum = jnp.sum(probability * grad_prob, axis=1, keepdims=True)
    grad_score = (probability * (grad_prob - delta_sum)).astype(jnp.bfloat16)
    query_grad = (
        jnp.dot(grad_score, key_rows, preferred_element_type=jnp.float32) * score_scale
    ).astype(jnp.bfloat16)
    key_part = outer_rows(grad_score, query_block) * score_scale
    value_part = outer_rows(rounded, grad_block)
    return (attended, query_grad, key_part, value_part)


def general_body(hidden_rows, query_rows, out_grad, projection, packing_plan, document_ids):
    row_count = hidden_rows.shape[0]
    split_size = lax.axis_size("ctx")
    part_index = lax.axis_index("ctx")
    sequences = lax.axis_size("dp")
    order_rows = jnp.argsort(packing_plan[0])
    send_hidden = jnp.take(hidden_rows, order_rows, axis=0)
    send_query = jnp.take(query_rows, order_rows, axis=0)
    packed_hidden, packed_query = (
        lax.all_to_all(send_hidden, "dp", split_axis=0, concat_axis=0, tiled=True),
        lax.all_to_all(send_query, "dp", split_axis=0, concat_axis=0, tiled=True),
    )
    projected = inner_rows(packed_hidden, projection)
    positions = part_index * row_count + jnp.arange(row_count, dtype=jnp.int32)
    cosine_table, sine_table = rotary_tables(positions, HEAD_DIM)
    key_width = KV_HEADS * HEAD_DIM
    key_heads = rotate_forward(
        projected[:, :key_width].reshape(row_count, KV_HEADS, HEAD_DIM), cosine_table, sine_table
    ).astype(jnp.bfloat16)
    values = projected[:, key_width:].reshape(row_count, KV_HEADS, HEAD_DIM).astype(jnp.bfloat16)
    repeats = split_size // KV_HEADS
    key_slots = jnp.repeat(key_heads, repeats, axis=1).reshape(row_count, split_size * HEAD_DIM)
    value_slots = jnp.repeat(values, repeats, axis=1).reshape(row_count, split_size * HEAD_DIM)
    local_query, local_keys, local_values = (
        lax.all_to_all(packed_query, "ctx", split_axis=1, concat_axis=0, tiled=True),
        lax.all_to_all(key_slots, "ctx", split_axis=1, concat_axis=0, tiled=True),
        lax.all_to_all(value_slots, "ctx", split_axis=1, concat_axis=0, tiled=True),
    )
    local_grad = lax.all_to_all(out_grad, "ctx", split_axis=1, concat_axis=0, tiled=True)
    length = local_query.shape[0]
    block_rows = math.gcd(length, 512)
    block_count = length // block_rows
    documents = document_ids[0]
    head_count = local_query.shape[1] // HEAD_DIM
    starts = jnp.arange(block_count, dtype=jnp.int32) * block_rows
    key_total = jnp.zeros((length, HEAD_DIM), jnp.float32)
    value_total = jnp.zeros((length, HEAD_DIM), jnp.float32)
    attended_parts = []
    query_parts = []
    for head_index in range(head_count):
        query_blocks = local_query[:, head_index * HEAD_DIM : (head_index + 1) * HEAD_DIM].reshape(
            block_count, block_rows, HEAD_DIM
        )
        grad_blocks = local_grad[:, head_index * HEAD_DIM : (head_index + 1) * HEAD_DIM].reshape(
            block_count, block_rows, HEAD_DIM
        )

        def block_step(carry_pair, inputs):
            query_block, grad_block, block_start = inputs
            query_index = block_start + jnp.arange(block_rows, dtype=jnp.int32)
            query_document = lax.dynamic_slice_in_dim(documents, block_start, block_rows)
            attended_block, query_block_grad, key_part, value_part = block_terms(
                query_block,
                grad_block,
                local_keys,
                local_values,
                query_index,
                query_document,
                documents,
            )
            return (
                (carry_pair[0] + key_part, carry_pair[1] + value_part),
                (attended_block, query_block_grad),
            )

        (key_total, value_total), (attended_blocks, query_grad_blocks) = lax.scan(
            block_step, (key_total, value_total), (query_blocks, grad_blocks, starts)
        )
        attended_parts.append(attended_blocks.reshape(length, HEAD_DIM))
        query_parts.append(query_grad_blocks.reshape(length, HEAD_DIM))
    local_attended = jnp.concatenate(attended_parts, axis=1)
    local_query_grad = jnp.concatenate(query_parts, axis=1)
    attended = lax.all_to_all(local_attended, "ctx", split_axis=0, concat_axis=1, tiled=True)
    query_grad = lax.all_to_all(local_query_grad, "ctx", split_axis=0, concat_axis=1, tiled=True)
    key_slots_grad, value_slots_grad = (
        lax.all_to_all(key_total, "ctx", split_axis=0, concat_axis=1, tiled=True),
        lax.all_to_all(value_total, "ctx", split_axis=0, concat_axis=1, tiled=True),
    )
    key_grad = (
        key_slots_grad.reshape(row_count, KV_HEADS, repeats, HEAD_DIM)
        .sum(axis=2)
        .astype(jnp.bfloat16)
    )
    value_grad = (
        value_slots_grad.reshape(row_count, KV_HEADS, repeats, HEAD_DIM)
        .sum(axis=2)
        .astype(jnp.bfloat16)
    )
    key_back = rotate_adjoint(key_grad.astype(jnp.float32), cosine_table, sine_table).reshape(
        row_count, key_width
    )
    projected_grad = jnp.concatenate(
        [key_back, value_grad.reshape(row_count, key_width).astype(jnp.float32)], axis=1
    ).astype(jnp.bfloat16)
    hidden_grad = jnp.dot(projected_grad, projection, preferred_element_type=jnp.float32).astype(
        jnp.bfloat16
    )
    block_term = outer_rows(projected_grad, packed_hidden)
    partial_sum = lax.psum_scatter(
        block_term.astype(jnp.bfloat16), "ctx", scatter_dimension=1, tiled=True
    ).astype(jnp.float32)
    weight_grad = lax.psum_scatter(partial_sum, "dp", scatter_dimension=0, tiled=True)
    weight_grad = weight_grad / sequences
    return (attended, query_grad, hidden_grad, weight_grad)


VMEM = pltpu.VMEM
SMEM = pltpu.SMEM
SIDES = 2


def vmem_specs(count):
    return [pl.BlockSpec(memory_space=VMEM)] * count


def any_specs(count):
    return [pl.BlockSpec(memory_space=pl.ANY)] * count


def begin(pairs, semaphores):
    copies = [pltpu.make_async_copy(source, target, semaphores.at[i]) for i, (source, target) in enumerate(pairs)]
    for copy in copies:
        copy.start()
    return copies


def finish(copies):
    for copy in copies:
        copy.wait()


def kernel_params(mebibytes):
    return pltpu.CompilerParams(vmem_limit_bytes=mebibytes * 2**20)


def struct(shape, dtype=jnp.bfloat16):
    return jax.ShapeDtypeStruct(shape, dtype)


def cost(flops, count, transcendentals=0):
    return pl.CostEstimate(flops=flops, bytes_accessed=count, transcendentals=transcendentals)


def pack_kernel(
    dp, plan_ref, query_any, hidden_any, cos_ref, sin_ref, proj_ref, qkv_ref, hid_ref,
    query_ref, hidden_ref, proj_s, sorted_s, sems,
):
    steps = proj_s.shape[0]
    copies = begin(
        [(hidden_any, hidden_ref), (query_any, query_ref)] + [(proj_ref.at[i], proj_s.at[i]) for i in range(steps)], sems
    )
    rows, width = hidden_ref.shape
    send = rows // dp
    query_width = query_ref.shape[1] // KV_HEADS
    quarter = width // KV_HEADS
    slot = lax.broadcasted_iota(jnp.int32, (rows, rows), 0)
    select = (plan_ref[...] == slot).astype(jnp.bfloat16)
    finish(copies[:2])
    for group in range(KV_HEADS):
        hidden = hidden_ref[:, group * quarter : (group + 1) * quarter]
        part = jnp.dot(select, hidden, preferred_element_type=jnp.float32)
        sorted_s[group * quarter : (group + 1) * quarter, :] = part.T.astype(jnp.bfloat16)
        part = part.astype(jnp.bfloat16)
        query = query_ref[:, group * query_width : (group + 1) * query_width]
        query = jnp.dot(select, query, preferred_element_type=jnp.float32).astype(jnp.bfloat16)
        for a in range(dp):
            hid_ref[a * KV_HEADS + group] = part[a * send : (a + 1) * send]
            qkv_ref[a * KV_HEADS + group, :, 0:query_width] = query[a * send : (a + 1) * send]
    cosine = jnp.concatenate([cos_ref[...]] * 2, axis=1)
    sine = jnp.concatenate([-sin_ref[...], sin_ref[...]], axis=1)
    heads = proj_s.shape[1] // HEAD_DIM
    for step in range(steps):
        copies[2 + step].wait()
        block = jnp.dot(proj_s[step], sorted_s[...], preferred_element_type=jnp.float32)
        for t in range(heads):
            head = step * heads + t
            is_value, group = head // KV_HEADS, head % KV_HEADS
            start = query_width + is_value * HEAD_DIM
            head_rows = block[t * HEAD_DIM : (t + 1) * HEAD_DIM, :].T
            for a in range(dp):
                x = head_rows[a * send : (a + 1) * send]
                if not is_value:
                    x = x * cosine + pltpu.roll(x, HEAD_DIM // 2, 1) * sine
                qkv_ref[a * KV_HEADS + group, :, start : start + HEAD_DIM] = x.astype(jnp.bfloat16)


def pack_rows(dp, plan, query, hidden, cosine, sine, projection):
    rows, width = hidden.shape
    send = rows // dp
    proj_rows = 2 * HEAD_DIM
    steps = projection.shape[0] // proj_rows
    qkv_shape = (dp * KV_HEADS, send, query.shape[1] // KV_HEADS + 2 * HEAD_DIM)
    hid_shape = (dp * KV_HEADS, send, width // KV_HEADS)
    return pl.pallas_call(
        functools.partial(pack_kernel, dp),
        in_specs=vmem_specs(1) + any_specs(2) + vmem_specs(2) + any_specs(1),
        out_specs=vmem_specs(2),
        out_shape=[struct(qkv_shape), struct(hid_shape)],
        scratch_shapes=[
            VMEM(query.shape, jnp.bfloat16),
            VMEM(hidden.shape, jnp.bfloat16),
            VMEM((steps, proj_rows, width), jnp.bfloat16),
            VMEM((width, rows), jnp.bfloat16),
            pltpu.SemaphoreType.DMA((2 + steps,)),
        ],
        cost_estimate=cost(2 * rows * width * projection.shape[0], 2 * (projection.size + 3 * hidden.size)),
        name="pack_rows",
    )(plan, query, hidden, cosine, sine, projection.reshape(steps, proj_rows, width))


def split_kernel(group_ref, in_ref, *out_refs):
    width = out_refs[0].shape[1]
    for e, out_ref in enumerate(out_refs):
        at = jnp.bitwise_xor(group_ref[0], e) * width
        out_ref[...] = in_ref[:, pl.ds(pl.multiple_of(at, width), width)]


def split_columns(group, array):
    rows, width = array.shape
    return pl.pallas_call(
        split_kernel,
        in_specs=[pl.BlockSpec(memory_space=SMEM)] + vmem_specs(1),
        out_specs=vmem_specs(KV_HEADS),
        out_shape=[struct((rows, width // KV_HEADS))] * KV_HEADS,
        cost_estimate=cost(0, 4 * array.size),
        name="split_columns",
    )(group, array)


def join_kernel(group_ref, *refs):
    pieces, outs, sems = refs[:KV_HEADS], refs[KV_HEADS:-1], refs[-1]
    width = pieces[0].shape[1] // len(outs)
    pairs = []
    for e, piece in enumerate(pieces):
        at = pl.multiple_of(jnp.bitwise_xor(group_ref[0], e) * width, width)
        for k, out_ref in enumerate(outs):
            pairs.append((piece.at[:, pl.ds(k * width, width)], out_ref.at[:, pl.ds(at, width)]))
    finish(begin(pairs, sems))


def join_columns(group, pieces, outs):
    rows, width = pieces[0].shape
    return pl.pallas_call(
        join_kernel,
        in_specs=[pl.BlockSpec(memory_space=SMEM)] + any_specs(KV_HEADS),
        out_specs=vmem_specs(outs),
        out_shape=[struct((rows, KV_HEADS * width // outs))] * outs,
        scratch_shapes=[pltpu.SemaphoreType.DMA((KV_HEADS * outs,))],
        compiler_params=kernel_params(8),
        cost_estimate=cost(0, 4 * KV_HEADS * rows * width),
        name="join_columns",
    )(group, *pieces)


def attend_kernel(dp, index_ref, qkv_ref, kv_ref, *refs):
    grads = refs[:KV_HEADS]
    doc_ref = refs[KV_HEADS]
    outs = refs[KV_HEADS + 1 : 2 * KV_HEADS + 1]
    keep_ref, send_ref, key_s, value_s, key_t, value_t, query_s, grad_s, dk_s, dv_s, out_s, doc_s = refs[2 * KV_HEADS + 1 :]
    which, group, side = index_ref[0], index_ref[1], index_ref[2]
    send = qkv_ref.shape[1]
    rows = dp * send
    width = qkv_ref.shape[2] - 2 * HEAD_DIM
    heads = width // HEAD_DIM
    ctx = KV_HEADS * SIDES
    score_scale = HEAD_DIM ** (-0.5)
    power = score_scale * math.log2(math.e)
    for e in range(KV_HEADS):
        zone = jnp.bitwise_xor(group, e)
        for head in range(heads):
            grad_s[zone, head * rows : (head + 1) * rows, :] = grads[e][:, head * HEAD_DIM : (head + 1) * HEAD_DIM]
            for s in range(dp):
                query_s[e, head * rows + s * send : head * rows + (s + 1) * send, :] = qkv_ref[
                    s * KV_HEADS + e, :, head * HEAD_DIM : (head + 1) * HEAD_DIM
                ]
    for s in range(dp):
        for zone in range(KV_HEADS):
            piece = s * KV_HEADS + zone
            own = pl.ds(pl.multiple_of((zone * SIDES + side) * rows + s * send, send), send)
            other = pl.ds(pl.multiple_of((zone * SIDES + 1 - side) * rows + s * send, send), send)
            key_s[own, :] = qkv_ref[piece, :, width : width + HEAD_DIM]
            value_s[own, :] = qkv_ref[piece, :, width + HEAD_DIM :]
            key_s[other, :] = kv_ref[piece, :, 0:HEAD_DIM]
            value_s[other, :] = kv_ref[piece, :, HEAD_DIM:]
    for c in range(ctx):
        part = slice(c * rows, (c + 1) * rows)
        key_t[:, part] = key_s[part, :].astype(jnp.float32).T.astype(jnp.bfloat16)
        value_t[:, part] = value_s[part, :].astype(jnp.float32).T.astype(jnp.bfloat16)
        doc_s[part, :] = jnp.broadcast_to(doc_ref[c].astype(jnp.float32), (rows, rows)).T
    for zone in reversed(range(KV_HEADS)):
        hi = (zone + 1) * SIDES * rows
        start = pl.multiple_of((zone * SIDES + side) * rows, rows)
        keys = key_s[0:hi, :]
        values = value_s[0:hi, :]
        key_index = lax.broadcasted_iota(jnp.int32, (hi, rows), 0)
        query_index = lax.broadcasted_iota(jnp.int32, (hi, rows), 1) + start
        allowed = (key_index <= query_index) & (doc_s[0:hi, :] == doc_ref[zone * SIDES + side].astype(jnp.float32))
        bias = jnp.where(allowed, 0.0, MASK_VALUE)
        query = query_s[zone]
        grad = grad_s[zone]
        scores = inner_rows(keys, query) + jnp.concatenate([bias] * heads, axis=1)
        row_max = jnp.max(scores, axis=0, keepdims=True)
        exponent = jnp.exp2((scores - row_max) * power)
        inverse = 1.0 / jnp.sum(exponent, axis=0, keepdims=True)
        probability = exponent * inverse
        rounded = probability.astype(jnp.bfloat16)
        attended = jnp.dot(value_t[:, 0:hi], rounded, preferred_element_type=jnp.float32)
        weighted = inner_rows(values, grad) * probability
        delta = jnp.sum(weighted, axis=0, keepdims=True)
        grad_score = (weighted - probability * delta).astype(jnp.bfloat16)
        query_grad = jnp.dot(key_t[:, 0:hi], grad_score, preferred_element_type=jnp.float32) * score_scale
        dk_part = jnp.dot(grad_score, query, preferred_element_type=jnp.float32)
        dv_part = jnp.dot(rounded, grad, preferred_element_type=jnp.float32)
        if zone == KV_HEADS - 1:
            dk_s[0:hi, :] = dk_part
            dv_s[0:hi, :] = dv_part
        else:
            dk_s[0:hi, :] += dk_part
            dv_s[0:hi, :] += dv_part
        for head in range(heads):
            part = slice(head * rows, (head + 1) * rows)
            out_s[zone, :, head * HEAD_DIM : (head + 1) * HEAD_DIM] = attended[:, part].T.astype(jnp.bfloat16)
            out_s[zone, :, width + head * HEAD_DIM : width + (head + 1) * HEAD_DIM] = (
                query_grad[:, part].T.astype(jnp.bfloat16)
            )
    for e in range(KV_HEADS):
        outs[e][...] = out_s[jnp.bitwise_xor(group, e)]

    @pl.when(which == 0)
    def _():
        keep_ref[...] = dk_s[...] * score_scale
        send_ref[...] = dv_s[...].astype(send_ref.dtype)

    @pl.when(which != 0)
    def _():
        keep_ref[...] = dv_s[...]
        send_ref[...] = (dk_s[...] * score_scale).astype(send_ref.dtype)


def attend(dp, index, qkv, kv, grads, documents):
    rows, width = grads[0].shape
    heads = width // HEAD_DIM
    length = KV_HEADS * SIDES * rows
    pairs = heads * length * length // 4
    return pl.pallas_call(
        functools.partial(attend_kernel, dp),
        in_specs=[pl.BlockSpec(memory_space=SMEM)] + vmem_specs(KV_HEADS + 3),
        out_specs=vmem_specs(KV_HEADS + 2),
        out_shape=[struct((rows, 2 * width))] * KV_HEADS
        + [struct((length, HEAD_DIM), jnp.float32), struct((length, HEAD_DIM))],
        scratch_shapes=[
            VMEM((length, HEAD_DIM), jnp.bfloat16),
            VMEM((length, HEAD_DIM), jnp.bfloat16),
            VMEM((HEAD_DIM, length), jnp.bfloat16),
            VMEM((HEAD_DIM, length), jnp.bfloat16),
            VMEM((KV_HEADS, heads * rows, HEAD_DIM), jnp.bfloat16),
            VMEM((KV_HEADS, heads * rows, HEAD_DIM), jnp.bfloat16),
            VMEM((length, HEAD_DIM), jnp.float32),
            VMEM((length, HEAD_DIM), jnp.float32),
            VMEM((KV_HEADS, rows, 2 * width), jnp.bfloat16),
            VMEM((length, rows), jnp.float32),
        ],
        cost_estimate=cost(10 * pairs * HEAD_DIM, 2 * (kv.size + 4 * qkv.size), pairs),
        name="attend",
    )(index, qkv, kv, *grads, documents.reshape(KV_HEADS * SIDES, 1, rows))


def combine_kernel(dp, index_ref, keep_ref, recv_any, cos_ref, sin_ref, out_ref, recv_ref, sems):
    side = index_ref[2]
    finish(begin([(recv_any, recv_ref)], sems))
    length = keep_ref.shape[0]
    ctx = KV_HEADS * SIDES
    send = length // (dp * ctx)
    total = (keep_ref[...] + recv_ref[...].astype(jnp.float32)).astype(jnp.bfloat16).astype(jnp.float32)
    back = total * cos_ref[...] + pltpu.roll(total, HEAD_DIM // 2, 1) * sin_ref[...]
    back = back.astype(jnp.bfloat16)
    for c in range(ctx):
        for s in range(dp):
            at = (c * dp + s) * send
            half = jnp.bitwise_xor(side, c % SIDES) * (length // SIDES)
            to = pl.multiple_of(half + (s * KV_HEADS + c // SIDES) * send, send)
            out_ref[pl.ds(to, send), :] = back[at : at + send]


def combine(dp, index, keep, recv, cosine, sine):
    return pl.pallas_call(
        functools.partial(combine_kernel, dp),
        in_specs=[pl.BlockSpec(memory_space=SMEM)] + vmem_specs(1) + any_specs(1) + vmem_specs(2),
        out_specs=pl.BlockSpec(memory_space=VMEM),
        out_shape=struct(keep.shape),
        scratch_shapes=[VMEM(recv.shape, recv.dtype), pltpu.SemaphoreType.DMA((1,))],
        compiler_params=kernel_params(12),
        cost_estimate=cost(4 * keep.size, 16 * keep.size),
        name="combine",
    )(index, keep, recv, cosine, sine)


def product_kernel(dp, index_ref, *refs):
    group, side, high = index_ref[1], index_ref[2], index_ref[3]
    grads = refs[:KV_HEADS]
    hid_any = refs[KV_HEADS : KV_HEADS + SIDES]
    out_refs = refs[KV_HEADS + SIDES : KV_HEADS + SIDES + dp]
    own_ref, other_ref, heads_s, own_s, other_s, sems = refs[KV_HEADS + SIDES + dp :]
    hid_refs = (own_s, other_s)
    ctx = KV_HEADS * SIDES
    length = grads[0].shape[0]
    send = length // (dp * ctx)
    pairs = [(grads[e], heads_s.at[jnp.bitwise_xor(group, e)]) for e in range(KV_HEADS)]
    copies = begin(pairs + list(zip(hid_any, hid_refs)), sems)
    finish(copies[:KV_HEADS])
    part = length // SIDES
    columns = hid_refs[0].shape[1] // SIDES
    for s in range(dp):
        at = pl.multiple_of((s * KV_HEADS + group) * send, send)
        own, other = pl.ds(at, send), pl.ds(part + at, send)
        for head in range(KV_HEADS):
            cols = slice(head * HEAD_DIM, (head + 1) * HEAD_DIM)
            own_ref[s * send : (s + 1) * send, cols] = heads_s[head, own, :]
            other_ref[s * send : (s + 1) * send, cols] = heads_s[head, other, :]
    finish(copies[KV_HEADS:])
    halves = dp // SIDES
    per = KV_HEADS // halves
    for ek in range(halves):
        first = jnp.bitwise_xor(high, ek) * per
        for t in range(per):
            left = heads_s[first + t]
            for ey in range(SIDES):
                window = pl.ds(pl.multiple_of(jnp.bitwise_xor(side, ey) * columns, columns), columns)
                total = outer_rows(left[:part], hid_refs[0][:, window]) + outer_rows(left[part:], hid_refs[1][:, window])
                out_refs[ek * SIDES + ey][t * HEAD_DIM : (t + 1) * HEAD_DIM, :] = total.astype(jnp.bfloat16)


def product(dp, index, grads, hid_own, hid_other):
    length = grads[0].shape[0]
    columns = hid_own.shape[1] // SIDES
    rows = length // (KV_HEADS * SIDES)
    block = (2 * KV_HEADS * HEAD_DIM // dp, columns)
    return pl.pallas_call(
        functools.partial(product_kernel, dp),
        in_specs=[pl.BlockSpec(memory_space=SMEM)] + any_specs(KV_HEADS + SIDES),
        out_specs=vmem_specs(dp + 2),
        out_shape=[struct(block)] * dp + [struct((rows, KV_HEADS * HEAD_DIM))] * 2,
        scratch_shapes=[
            VMEM((KV_HEADS, length, HEAD_DIM), jnp.bfloat16),
            VMEM(hid_own.shape, jnp.bfloat16),
            VMEM(hid_other.shape, jnp.bfloat16),
            pltpu.SemaphoreType.DMA((KV_HEADS + SIDES,)),
        ],
        compiler_params=kernel_params(20),
        cost_estimate=cost(
            4 * length * KV_HEADS * HEAD_DIM * columns,
            2 * (2 * length * columns + length * KV_HEADS * HEAD_DIM + 4 * columns * HEAD_DIM * KV_HEADS),
        ),
        name="weight_product",
    )(index, *grads, hid_own, hid_other)


def hidden_kernel(which_ref, own_ref, other_ref, own_proj_ref, other_proj_ref, out_ref):
    total = jnp.dot(own_ref[...], own_proj_ref[0], preferred_element_type=jnp.float32)
    total += jnp.dot(other_ref[...], other_proj_ref[0], preferred_element_type=jnp.float32)
    out_ref[...] = total.astype(out_ref.dtype)


def hidden_product(which, own, other, projection):
    rows, half = own.shape
    width = projection.shape[1]
    columns = math.gcd(width, 1024)
    halves = projection.reshape(2, half, width)
    spec = pltpu.PrefetchScalarGridSpec(
        num_scalar_prefetch=1,
        grid=(width // columns,),
        in_specs=[
            pl.BlockSpec((rows, half), lambda i, w: (0, 0)),
            pl.BlockSpec((rows, half), lambda i, w: (0, 0)),
            pl.BlockSpec((1, half, columns), lambda i, w: (w[0], 0, i)),
            pl.BlockSpec((1, half, columns), lambda i, w: (1 - w[0], 0, i)),
        ],
        out_specs=pl.BlockSpec((rows, columns), lambda i, w: (0, i)),
    )
    return pl.pallas_call(
        hidden_kernel,
        grid_spec=spec,
        out_shape=struct((rows, width)),
        compiler_params=kernel_params(16),
        cost_estimate=cost(4 * rows * half * width, 2 * projection.size + 4 * rows * width),
        name="hidden_product",
    )(which, own, other, halves, halves)


AXES = ("dp", "group", "side")


def paired_body(hidden_rows, query_rows, out_grad, projection, packing_plan, document_ids):
    rows, width = hidden_rows.shape
    dp = lax.axis_size("dp")
    ctx = KV_HEADS * SIDES
    a, group, side = (lax.axis_index(name) for name in AXES)
    block_id = group * SIDES + side
    send = rows // dp
    length = rows * ctx
    which = jnp.bitwise_xor(side, a % SIDES)
    index = jnp.stack([which, group, side, a // SIDES]).astype(jnp.int32)
    group_index = group.reshape(1)

    def move(value, target):
        flat = lambda i, g, p: (i * KV_HEADS + g) * SIDES + p
        moves = [
            (flat(i, g, p), flat(*target(i, g, p)))
            for i in range(dp)
            for g in range(KV_HEADS)
            for p in range(SIDES)
        ]
        return lax.ppermute(value, AXES, moves)

    def spread(pieces):
        return [pieces[0]] + [move(pieces[e], lambda i, g, p, e=e: (i, g ^ e, p)) for e in range(1, KV_HEADS)]

    other_side = lambda i, g, p: (i, g, 1 - p)
    scatter = lambda value, axes: lax.all_to_all(value, axes, split_axis=0, concat_axis=0, tiled=True)

    grads_in = split_columns(group_index, out_grad)
    packing_plan, grads_in = lax.optimization_barrier((packing_plan, grads_in))
    grads_in = spread(grads_in)
    slot = block_id * rows + a * send + jnp.arange(send, dtype=jnp.int32)
    cosine, sine = rotary_tables(slot, HEAD_DIM)
    qkv_pieces, hid_pieces = pack_rows(dp, packing_plan, query_rows, hidden_rows, cosine, sine, projection)
    qkv = scatter(qkv_pieces, AXES[:2])
    kv_other = move(qkv[:, :, query_rows.shape[1] // KV_HEADS :], other_side)
    qkv, hid_pieces = lax.optimization_barrier((qkv, hid_pieces))
    hid = scatter(hid_pieces, AXES[:2])

    *outputs, keep, give = attend(dp, index, qkv, kv_other, grads_in, document_ids)
    recv = move(give, other_side)
    cosine, sine = rotary_tables(jnp.arange(length, dtype=jnp.int32), HEAD_DIM)
    cosine = jnp.where(which == 0, jnp.concatenate([cosine, cosine], axis=1), 1.0)
    sine = jnp.where(which == 0, jnp.concatenate([sine, -sine], axis=1), 0.0)
    piece = combine(dp, index, keep, recv, cosine, sine)
    shift = lambda value, e: move(value, lambda i, g, p: (i, g ^ e, p))
    near = shift(piece, 1)
    far_piece, hid = lax.optimization_barrier((piece, hid))
    hid_own = hid.reshape(length // SIDES, width // KV_HEADS)
    hid_other = move(hid_own, other_side)
    grads = [piece, near, shift(far_piece, 2)]
    grads.append(shift(grads[2], 1))

    outputs, *early = lax.optimization_barrier((outputs, *grads[:3]))
    grads = [*early, grads[3]]
    back = spread(outputs)
    products = product(dp, index, grads, hid_own, hid_other)
    own_rows, other_rows = products[dp], products[dp + 1]
    other_half = move(other_rows, other_side)
    half = dp // SIDES
    blocks = [
        move(
            products[ek * SIDES + ey],
            lambda i, g, p, ek=ek, ey=ey: ((p ^ (i % SIDES)) * half + ((i // SIDES) ^ ek), g, p ^ ey),
        )
        for ek in range(half)
        for ey in range(SIDES)
    ]

    hidden_grad = hidden_product(which.reshape(1), own_rows, other_half, projection)
    weight_grad = functools.reduce(jnp.add, [b.astype(jnp.float32) for b in blocks]) / dp

    back, hidden_grad = lax.optimization_barrier((back, hidden_grad))
    attended, query_grad = join_columns(group_index, back, 2)
    return (attended, query_grad, hidden_grad, weight_grad)


def paired(mesh):
    dp, ctx = mesh.shape["dp"], mesh.shape["ctx"]
    return ctx == KV_HEADS * SIDES and dp in (2, 4, 8)


def solution(mesh):
    if paired(mesh):
        body = paired_body
        inner = Mesh(mesh.devices.reshape(mesh.shape["dp"], KV_HEADS, SIDES), AXES)
        ctx = AXES[1:]
    else:
        body = general_body
        inner = mesh
        ctx = ("ctx",)
    rows = P(("dp", *ctx), None)
    step = jax.shard_map(
        body,
        mesh=inner,
        in_specs=(rows, rows, rows, P(), rows, P("dp", None)),
        out_specs=(rows, rows, rows, P("dp", ctx)),
        check_vma=False,
    )
    if body is general_body:
        return step

    return step
```

```python
import functools
import math

import jax
import jax.numpy as jnp
from jax import lax
from jax.experimental import pallas as pl
from jax.experimental.pallas import tpu as pltpu
from jax.sharding import Mesh, PartitionSpec as P

KV_HEADS = 4
HEAD_DIM = 128


ROPE_BASE = 500000.0
MASK_VALUE = -1e30


def rotary_tables(positions, head_width):
    half_width = head_width // 2
    exponent = jnp.arange(half_width, dtype=jnp.float32) * (-2.0 * math.log(ROPE_BASE) / head_width)
    angles = positions.astype(jnp.float32)[:, None] * jnp.exp(exponent)[None, :]
    return (jnp.cos(angles), jnp.sin(angles))


def rotate_forward(head_rows, cosine_table, sine_table):
    half_width = head_rows.shape[-1] // 2
    first_half = head_rows[..., :half_width]
    second_half = head_rows[..., half_width:]
    cosine_part = cosine_table[:, None, :]
    sine_part = sine_table[:, None, :]
    return jnp.concatenate(
        [
            first_half * cosine_part - second_half * sine_part,
            second_half * cosine_part + first_half * sine_part,
        ],
        axis=-1,
    )


def rotate_adjoint(head_grads, cosine_table, sine_table):
    half_width = head_grads.shape[-1] // 2
    first_half = head_grads[..., :half_width]
    second_half = head_grads[..., half_width:]
    cosine_part = cosine_table[:, None, :]
    sine_part = sine_table[:, None, :]
    return jnp.concatenate(
        [
            first_half * cosine_part + second_half * sine_part,
            second_half * cosine_part - first_half * sine_part,
        ],
        axis=-1,
    )


def inner_rows(left_side, right_side):
    return lax.dot_general(
        left_side, right_side, (((1,), (1,)), ((), ())), preferred_element_type=jnp.float32
    )


def outer_rows(left_side, right_side):
    return lax.dot_general(
        left_side, right_side, (((0,), (0,)), ((), ())), preferred_element_type=jnp.float32
    )


def block_terms(
    query_block, grad_block, key_rows, value_rows, query_index, query_document, key_document
):
    score_scale = key_rows.shape[1] ** (-0.5)
    scores = inner_rows(query_block, key_rows) * score_scale
    key_index = jnp.arange(key_rows.shape[0], dtype=jnp.int32)
    allowed = (key_index[None, :] <= query_index[:, None]) & (
        key_document[None, :] == query_document[:, None]
    )
    scores = jnp.where(allowed, scores, MASK_VALUE)
    row_max = jnp.max(scores, axis=1, keepdims=True)
    exponent = jnp.exp(scores - row_max)
    probability = exponent / jnp.sum(exponent, axis=1, keepdims=True)
    rounded = probability.astype(jnp.bfloat16)
    attended = jnp.dot(rounded, value_rows, preferred_element_type=jnp.float32).astype(jnp.bfloat16)
    grad_prob = inner_rows(grad_block, value_rows)
    delta_sum = jnp.sum(probability * grad_prob, axis=1, keepdims=True)
    grad_score = (probability * (grad_prob - delta_sum)).astype(jnp.bfloat16)
    query_grad = (
        jnp.dot(grad_score, key_rows, preferred_element_type=jnp.float32) * score_scale
    ).astype(jnp.bfloat16)
    key_part = outer_rows(grad_score, query_block) * score_scale
    value_part = outer_rows(rounded, grad_block)
    return (attended, query_grad, key_part, value_part)


def general_body(hidden_rows, query_rows, out_grad, projection, packing_plan, document_ids):
    row_count = hidden_rows.shape[0]
    split_size = lax.axis_size("ctx")
    part_index = lax.axis_index("ctx")
    sequences = lax.axis_size("dp")
    order_rows = jnp.argsort(packing_plan[0])
    send_hidden = jnp.take(hidden_rows, order_rows, axis=0)
    send_query = jnp.take(query_rows, order_rows, axis=0)
    packed_hidden, packed_query = (
        lax.all_to_all(send_hidden, "dp", split_axis=0, concat_axis=0, tiled=True),
        lax.all_to_all(send_query, "dp", split_axis=0, concat_axis=0, tiled=True),
    )
    projected = inner_rows(packed_hidden, projection)
    positions = part_index * row_count + jnp.arange(row_count, dtype=jnp.int32)
    cosine_table, sine_table = rotary_tables(positions, HEAD_DIM)
    key_width = KV_HEADS * HEAD_DIM
    key_heads = rotate_forward(
        projected[:, :key_width].reshape(row_count, KV_HEADS, HEAD_DIM), cosine_table, sine_table
    ).astype(jnp.bfloat16)
    values = projected[:, key_width:].reshape(row_count, KV_HEADS, HEAD_DIM).astype(jnp.bfloat16)
    repeats = split_size // KV_HEADS
    key_slots = jnp.repeat(key_heads, repeats, axis=1).reshape(row_count, split_size * HEAD_DIM)
    value_slots = jnp.repeat(values, repeats, axis=1).reshape(row_count, split_size * HEAD_DIM)
    local_query, local_keys, local_values = (
        lax.all_to_all(packed_query, "ctx", split_axis=1, concat_axis=0, tiled=True),
        lax.all_to_all(key_slots, "ctx", split_axis=1, concat_axis=0, tiled=True),
        lax.all_to_all(value_slots, "ctx", split_axis=1, concat_axis=0, tiled=True),
    )
    local_grad = lax.all_to_all(out_grad, "ctx", split_axis=1, concat_axis=0, tiled=True)
    length = local_query.shape[0]
    block_rows = math.gcd(length, 512)
    block_count = length // block_rows
    documents = document_ids[0]
    head_count = local_query.shape[1] // HEAD_DIM
    starts = jnp.arange(block_count, dtype=jnp.int32) * block_rows
    key_total = jnp.zeros((length, HEAD_DIM), jnp.float32)
    value_total = jnp.zeros((length, HEAD_DIM), jnp.float32)
    attended_parts = []
    query_parts = []
    for head_index in range(head_count):
        query_blocks = local_query[:, head_index * HEAD_DIM : (head_index + 1) * HEAD_DIM].reshape(
            block_count, block_rows, HEAD_DIM
        )
        grad_blocks = local_grad[:, head_index * HEAD_DIM : (head_index + 1) * HEAD_DIM].reshape(
            block_count, block_rows, HEAD_DIM
        )

        def block_step(carry_pair, inputs):
            query_block, grad_block, block_start = inputs
            query_index = block_start + jnp.arange(block_rows, dtype=jnp.int32)
            query_document = lax.dynamic_slice_in_dim(documents, block_start, block_rows)
            attended_block, query_block_grad, key_part, value_part = block_terms(
                query_block,
                grad_block,
                local_keys,
                local_values,
                query_index,
                query_document,
                documents,
            )
            return (
                (carry_pair[0] + key_part, carry_pair[1] + value_part),
                (attended_block, query_block_grad),
            )

        (key_total, value_total), (attended_blocks, query_grad_blocks) = lax.scan(
            block_step, (key_total, value_total), (query_blocks, grad_blocks, starts)
        )
        attended_parts.append(attended_blocks.reshape(length, HEAD_DIM))
        query_parts.append(query_grad_blocks.reshape(length, HEAD_DIM))
    local_attended = jnp.concatenate(attended_parts, axis=1)
    local_query_grad = jnp.concatenate(query_parts, axis=1)
    attended = lax.all_to_all(local_attended, "ctx", split_axis=0, concat_axis=1, tiled=True)
    query_grad = lax.all_to_all(local_query_grad, "ctx", split_axis=0, concat_axis=1, tiled=True)
    key_slots_grad, value_slots_grad = (
        lax.all_to_all(key_total, "ctx", split_axis=0, concat_axis=1, tiled=True),
        lax.all_to_all(value_total, "ctx", split_axis=0, concat_axis=1, tiled=True),
    )
    key_grad = (
        key_slots_grad.reshape(row_count, KV_HEADS, repeats, HEAD_DIM)
        .sum(axis=2)
        .astype(jnp.bfloat16)
    )
    value_grad = (
        value_slots_grad.reshape(row_count, KV_HEADS, repeats, HEAD_DIM)
        .sum(axis=2)
        .astype(jnp.bfloat16)
    )
    key_back = rotate_adjoint(key_grad.astype(jnp.float32), cosine_table, sine_table).reshape(
        row_count, key_width
    )
    projected_grad = jnp.concatenate(
        [key_back, value_grad.reshape(row_count, key_width).astype(jnp.float32)], axis=1
    ).astype(jnp.bfloat16)
    hidden_grad = jnp.dot(projected_grad, projection, preferred_element_type=jnp.float32).astype(
        jnp.bfloat16
    )
    block_term = outer_rows(projected_grad, packed_hidden)
    partial_sum = lax.psum_scatter(
        block_term.astype(jnp.bfloat16), "ctx", scatter_dimension=1, tiled=True
    ).astype(jnp.float32)
    weight_grad = lax.psum_scatter(partial_sum, "dp", scatter_dimension=0, tiled=True)
    weight_grad = weight_grad / sequences
    return (attended, query_grad, hidden_grad, weight_grad)


VMEM = pltpu.VMEM
SMEM = pltpu.SMEM
SIDES = 2


def vmem_specs(count):
    return [pl.BlockSpec(memory_space=VMEM)] * count


def any_specs(count):
    return [pl.BlockSpec(memory_space=pl.ANY)] * count


def begin(pairs, semaphores):
    copies = [pltpu.make_async_copy(source, target, semaphores.at[i]) for i, (source, target) in enumerate(pairs)]
    for copy in copies:
        copy.start()
    return copies


def finish(copies):
    for copy in copies:
        copy.wait()


def kernel_params(mebibytes):
    return pltpu.CompilerParams(vmem_limit_bytes=mebibytes * 2**20)


def struct(shape, dtype=jnp.bfloat16):
    return jax.ShapeDtypeStruct(shape, dtype)


def cost(flops, count, transcendentals=0):
    return pl.CostEstimate(flops=flops, bytes_accessed=count, transcendentals=transcendentals)


def pack_kernel(
    dp, plan_ref, query_any, hidden_any, cos_ref, sin_ref, proj_ref, qkv_ref, hid_ref,
    query_ref, hidden_ref, proj_s, sorted_s, sems,
):
    steps = proj_s.shape[0]
    copies = begin(
        [(hidden_any, hidden_ref), (query_any, query_ref)] + [(proj_ref.at[i], proj_s.at[i]) for i in range(steps)], sems
    )
    rows, width = hidden_ref.shape
    send = rows // dp
    query_width = query_ref.shape[1] // KV_HEADS
    quarter = width // KV_HEADS
    slot = lax.broadcasted_iota(jnp.int32, (rows, rows), 0)
    select = (plan_ref[...] == slot).astype(jnp.bfloat16)
    finish(copies[:2])
    for group in range(KV_HEADS):
        hidden = hidden_ref[:, group * quarter : (group + 1) * quarter]
        part = jnp.dot(select, hidden, preferred_element_type=jnp.float32)
        sorted_s[group * quarter : (group + 1) * quarter, :] = part.T.astype(jnp.bfloat16)
        part = part.astype(jnp.bfloat16)
        query = query_ref[:, group * query_width : (group + 1) * query_width]
        query = jnp.dot(select, query, preferred_element_type=jnp.float32).astype(jnp.bfloat16)
        for a in range(dp):
            hid_ref[a * KV_HEADS + group] = part[a * send : (a + 1) * send]
            qkv_ref[a * KV_HEADS + group, :, 0:query_width] = query[a * send : (a + 1) * send]
    cosine = jnp.concatenate([cos_ref[...]] * 2, axis=1)
    sine = jnp.concatenate([-sin_ref[...], sin_ref[...]], axis=1)
    heads = proj_s.shape[1] // HEAD_DIM
    for step in range(steps):
        copies[2 + step].wait()
        block = jnp.dot(proj_s[step], sorted_s[...], preferred_element_type=jnp.float32)
        for t in range(heads):
            head = step * heads + t
            is_value, group = head // KV_HEADS, head % KV_HEADS
            start = query_width + is_value * HEAD_DIM
            head_rows = block[t * HEAD_DIM : (t + 1) * HEAD_DIM, :].T
            for a in range(dp):
                x = head_rows[a * send : (a + 1) * send]
                if not is_value:
                    x = x * cosine + pltpu.roll(x, HEAD_DIM // 2, 1) * sine
                qkv_ref[a * KV_HEADS + group, :, start : start + HEAD_DIM] = x.astype(jnp.bfloat16)


def pack_rows(dp, plan, query, hidden, cosine, sine, projection):
    rows, width = hidden.shape
    send = rows // dp
    proj_rows = 2 * HEAD_DIM
    steps = projection.shape[0] // proj_rows
    qkv_shape = (dp * KV_HEADS, send, query.shape[1] // KV_HEADS + 2 * HEAD_DIM)
    hid_shape = (dp * KV_HEADS, send, width // KV_HEADS)
    return pl.pallas_call(
        functools.partial(pack_kernel, dp),
        in_specs=vmem_specs(1) + any_specs(2) + vmem_specs(2) + any_specs(1),
        out_specs=vmem_specs(2),
        out_shape=[struct(qkv_shape), struct(hid_shape)],
        scratch_shapes=[
            VMEM(query.shape, jnp.bfloat16),
            VMEM(hidden.shape, jnp.bfloat16),
            VMEM((steps, proj_rows, width), jnp.bfloat16),
            VMEM((width, rows), jnp.bfloat16),
            pltpu.SemaphoreType.DMA((2 + steps,)),
        ],
        cost_estimate=cost(2 * rows * width * projection.shape[0], 2 * (projection.size + 3 * hidden.size)),
        name="pack_rows",
    )(plan, query, hidden, cosine, sine, projection.reshape(steps, proj_rows, width))


def split_kernel(group_ref, in_ref, *out_refs):
    width = out_refs[0].shape[1]
    for e, out_ref in enumerate(out_refs):
        at = jnp.bitwise_xor(group_ref[0], e) * width
        out_ref[...] = in_ref[:, pl.ds(pl.multiple_of(at, width), width)]


def split_columns(group, array):
    rows, width = array.shape
    return pl.pallas_call(
        split_kernel,
        in_specs=[pl.BlockSpec(memory_space=SMEM)] + vmem_specs(1),
        out_specs=vmem_specs(KV_HEADS),
        out_shape=[struct((rows, width // KV_HEADS))] * KV_HEADS,
        cost_estimate=cost(0, 4 * array.size),
        name="split_columns",
    )(group, array)


def join_kernel(group_ref, *refs):
    pieces, outs, sems = refs[:KV_HEADS], refs[KV_HEADS:-1], refs[-1]
    width = pieces[0].shape[1] // len(outs)
    pairs = []
    for e, piece in enumerate(pieces):
        at = pl.multiple_of(jnp.bitwise_xor(group_ref[0], e) * width, width)
        for k, out_ref in enumerate(outs):
            pairs.append((piece.at[:, pl.ds(k * width, width)], out_ref.at[:, pl.ds(at, width)]))
    finish(begin(pairs, sems))


def join_columns(group, pieces, outs):
    rows, width = pieces[0].shape
    return pl.pallas_call(
        join_kernel,
        in_specs=[pl.BlockSpec(memory_space=SMEM)] + any_specs(KV_HEADS),
        out_specs=vmem_specs(outs),
        out_shape=[struct((rows, KV_HEADS * width // outs))] * outs,
        scratch_shapes=[pltpu.SemaphoreType.DMA((KV_HEADS * outs,))],
        compiler_params=kernel_params(8),
        cost_estimate=cost(0, 4 * KV_HEADS * rows * width),
        name="join_columns",
    )(group, *pieces)


def attend_kernel(dp, index_ref, qkv_ref, kv_ref, *refs):
    grads = refs[:KV_HEADS]
    doc_ref = refs[KV_HEADS]
    outs = refs[KV_HEADS + 1 : 2 * KV_HEADS + 1]
    keep_ref, send_ref, key_s, value_s, key_t, value_t, query_s, grad_s, dk_s, dv_s, out_s, doc_s = refs[2 * KV_HEADS + 1 :]
    which, group, side = index_ref[0], index_ref[1], index_ref[2]
    send = qkv_ref.shape[1]
    rows = dp * send
    width = qkv_ref.shape[2] - 2 * HEAD_DIM
    heads = width // HEAD_DIM
    ctx = KV_HEADS * SIDES
    score_scale = HEAD_DIM ** (-0.5)
    power = score_scale * math.log2(math.e)
    for e in range(KV_HEADS):
        zone = jnp.bitwise_xor(group, e)
        for head in range(heads):
            grad_s[zone, head * rows : (head + 1) * rows, :] = grads[e][:, head * HEAD_DIM : (head + 1) * HEAD_DIM]
            for s in range(dp):
                query_s[e, head * rows + s * send : head * rows + (s + 1) * send, :] = qkv_ref[
                    s * KV_HEADS + e, :, head * HEAD_DIM : (head + 1) * HEAD_DIM
                ]
    for s in range(dp):
        for zone in range(KV_HEADS):
            piece = s * KV_HEADS + zone
            own = pl.ds(pl.multiple_of((zone * SIDES + side) * rows + s * send, send), send)
            other = pl.ds(pl.multiple_of((zone * SIDES + 1 - side) * rows + s * send, send), send)
            key_s[own, :] = qkv_ref[piece, :, width : width + HEAD_DIM]
            value_s[own, :] = qkv_ref[piece, :, width + HEAD_DIM :]
            key_s[other, :] = kv_ref[piece, :, 0:HEAD_DIM]
            value_s[other, :] = kv_ref[piece, :, HEAD_DIM:]
    for c in range(ctx):
        part = slice(c * rows, (c + 1) * rows)
        key_t[:, part] = key_s[part, :].astype(jnp.float32).T.astype(jnp.bfloat16)
        value_t[:, part] = value_s[part, :].astype(jnp.float32).T.astype(jnp.bfloat16)
        doc_s[part, :] = jnp.broadcast_to(doc_ref[c].astype(jnp.float32), (rows, rows)).T
    for zone in reversed(range(KV_HEADS)):
        hi = (zone + 1) * SIDES * rows
        start = pl.multiple_of((zone * SIDES + side) * rows, rows)
        keys = key_s[0:hi, :]
        values = value_s[0:hi, :]
        key_index = lax.broadcasted_iota(jnp.int32, (hi, rows), 0)
        query_index = lax.broadcasted_iota(jnp.int32, (hi, rows), 1) + start
        allowed = (key_index <= query_index) & (doc_s[0:hi, :] == doc_ref[zone * SIDES + side].astype(jnp.float32))
        bias = jnp.where(allowed, 0.0, MASK_VALUE)
        query = query_s[zone]
        grad = grad_s[zone]
        scores = inner_rows(keys, query) + jnp.concatenate([bias] * heads, axis=1)
        row_max = jnp.max(scores, axis=0, keepdims=True)
        exponent = jnp.exp2((scores - row_max) * power)
        inverse = 1.0 / jnp.sum(exponent, axis=0, keepdims=True)
        probability = exponent * inverse
        rounded = probability.astype(jnp.bfloat16)
        attended = jnp.dot(value_t[:, 0:hi], rounded, preferred_element_type=jnp.float32)
        weighted = inner_rows(values, grad) * probability
        delta = jnp.sum(weighted, axis=0, keepdims=True)
        grad_score = (weighted - probability * delta).astype(jnp.bfloat16)
        query_grad = jnp.dot(key_t[:, 0:hi], grad_score, preferred_element_type=jnp.float32) * score_scale
        dk_part = jnp.dot(grad_score, query, preferred_element_type=jnp.float32)
        dv_part = jnp.dot(rounded, grad, preferred_element_type=jnp.float32)
        if zone == KV_HEADS - 1:
            dk_s[0:hi, :] = dk_part
            dv_s[0:hi, :] = dv_part
        else:
            dk_s[0:hi, :] += dk_part
            dv_s[0:hi, :] += dv_part
        for head in range(heads):
            part = slice(head * rows, (head + 1) * rows)
            out_s[zone, :, head * HEAD_DIM : (head + 1) * HEAD_DIM] = attended[:, part].T.astype(jnp.bfloat16)
            out_s[zone, :, width + head * HEAD_DIM : width + (head + 1) * HEAD_DIM] = (
                query_grad[:, part].T.astype(jnp.bfloat16)
            )
    for e in range(KV_HEADS):
        outs[e][...] = out_s[jnp.bitwise_xor(group, e)]

    @pl.when(which == 0)
    def _():
        keep_ref[...] = dk_s[...] * score_scale
        send_ref[...] = dv_s[...].astype(send_ref.dtype)

    @pl.when(which != 0)
    def _():
        keep_ref[...] = dv_s[...]
        send_ref[...] = (dk_s[...] * score_scale).astype(send_ref.dtype)


def attend(dp, index, qkv, kv, grads, documents):
    rows, width = grads[0].shape
    heads = width // HEAD_DIM
    length = KV_HEADS * SIDES * rows
    pairs = heads * length * length // 4
    return pl.pallas_call(
        functools.partial(attend_kernel, dp),
        in_specs=[pl.BlockSpec(memory_space=SMEM)] + vmem_specs(KV_HEADS + 3),
        out_specs=vmem_specs(KV_HEADS + 2),
        out_shape=[struct((rows, 2 * width))] * KV_HEADS
        + [struct((length, HEAD_DIM), jnp.float32), struct((length, HEAD_DIM))],
        scratch_shapes=[
            VMEM((length, HEAD_DIM), jnp.bfloat16),
            VMEM((length, HEAD_DIM), jnp.bfloat16),
            VMEM((HEAD_DIM, length), jnp.bfloat16),
            VMEM((HEAD_DIM, length), jnp.bfloat16),
            VMEM((KV_HEADS, heads * rows, HEAD_DIM), jnp.bfloat16),
            VMEM((KV_HEADS, heads * rows, HEAD_DIM), jnp.bfloat16),
            VMEM((length, HEAD_DIM), jnp.float32),
            VMEM((length, HEAD_DIM), jnp.float32),
            VMEM((KV_HEADS, rows, 2 * width), jnp.bfloat16),
            VMEM((length, rows), jnp.float32),
        ],
        cost_estimate=cost(10 * pairs * HEAD_DIM, 2 * (kv.size + 4 * qkv.size), pairs),
        name="attend",
    )(index, qkv, kv, *grads, documents.reshape(KV_HEADS * SIDES, 1, rows))


def combine_kernel(dp, index_ref, keep_ref, recv_any, cos_ref, sin_ref, out_ref, recv_ref, sems):
    side = index_ref[2]
    finish(begin([(recv_any, recv_ref)], sems))
    length = keep_ref.shape[0]
    ctx = KV_HEADS * SIDES
    send = length // (dp * ctx)
    total = (keep_ref[...] + recv_ref[...].astype(jnp.float32)).astype(jnp.bfloat16).astype(jnp.float32)
    back = total * cos_ref[...] + pltpu.roll(total, HEAD_DIM // 2, 1) * sin_ref[...]
    back = back.astype(jnp.bfloat16)
    for c in range(ctx):
        for s in range(dp):
            at = (c * dp + s) * send
            half = jnp.bitwise_xor(side, c % SIDES) * (length // SIDES)
            to = pl.multiple_of(half + (s * KV_HEADS + c // SIDES) * send, send)
            out_ref[pl.ds(to, send), :] = back[at : at + send]


def combine(dp, index, keep, recv, cosine, sine):
    return pl.pallas_call(
        functools.partial(combine_kernel, dp),
        in_specs=[pl.BlockSpec(memory_space=SMEM)] + vmem_specs(1) + any_specs(1) + vmem_specs(2),
        out_specs=pl.BlockSpec(memory_space=VMEM),
        out_shape=struct(keep.shape),
        scratch_shapes=[VMEM(recv.shape, recv.dtype), pltpu.SemaphoreType.DMA((1,))],
        compiler_params=kernel_params(12),
        cost_estimate=cost(4 * keep.size, 16 * keep.size),
        name="combine",
    )(index, keep, recv, cosine, sine)


def product_kernel(dp, index_ref, *refs):
    group, side, high = index_ref[1], index_ref[2], index_ref[3]
    grads = refs[:KV_HEADS]
    hid_any = refs[KV_HEADS : KV_HEADS + SIDES]
    out_refs = refs[KV_HEADS + SIDES : KV_HEADS + SIDES + dp]
    own_ref, other_ref, heads_s, own_s, other_s, sems = refs[KV_HEADS + SIDES + dp :]
    hid_refs = (own_s, other_s)
    ctx = KV_HEADS * SIDES
    length = grads[0].shape[0]
    send = length // (dp * ctx)
    pairs = [(grads[e], heads_s.at[jnp.bitwise_xor(group, e)]) for e in range(KV_HEADS)]
    copies = begin(pairs + list(zip(hid_any, hid_refs)), sems)
    finish(copies[:KV_HEADS])
    part = length // SIDES
    columns = hid_refs[0].shape[1] // SIDES
    for s in range(dp):
        at = pl.multiple_of((s * KV_HEADS + group) * send, send)
        own, other = pl.ds(at, send), pl.ds(part + at, send)
        for head in range(KV_HEADS):
            cols = slice(head * HEAD_DIM, (head + 1) * HEAD_DIM)
            own_ref[s * send : (s + 1) * send, cols] = heads_s[head, own, :]
            other_ref[s * send : (s + 1) * send, cols] = heads_s[head, other, :]
    finish(copies[KV_HEADS:])
    halves = dp // SIDES
    per = KV_HEADS // halves
    for ek in range(halves):
        first = jnp.bitwise_xor(high, ek) * per
        for t in range(per):
            left = heads_s[first + t]
            for ey in range(SIDES):
                window = pl.ds(pl.multiple_of(jnp.bitwise_xor(side, ey) * columns, columns), columns)
                total = outer_rows(left[:part], hid_refs[0][:, window]) + outer_rows(left[part:], hid_refs[1][:, window])
                out_refs[ek * SIDES + ey][t * HEAD_DIM : (t + 1) * HEAD_DIM, :] = total.astype(jnp.bfloat16)


def product(dp, index, grads, hid_own, hid_other):
    length = grads[0].shape[0]
    columns = hid_own.shape[1] // SIDES
    rows = length // (KV_HEADS * SIDES)
    block = (2 * KV_HEADS * HEAD_DIM // dp, columns)
    return pl.pallas_call(
        functools.partial(product_kernel, dp),
        in_specs=[pl.BlockSpec(memory_space=SMEM)] + any_specs(KV_HEADS + SIDES),
        out_specs=vmem_specs(dp + 2),
        out_shape=[struct(block)] * dp + [struct((rows, KV_HEADS * HEAD_DIM))] * 2,
        scratch_shapes=[
            VMEM((KV_HEADS, length, HEAD_DIM), jnp.bfloat16),
            VMEM(hid_own.shape, jnp.bfloat16),
            VMEM(hid_other.shape, jnp.bfloat16),
            pltpu.SemaphoreType.DMA((KV_HEADS + SIDES,)),
        ],
        compiler_params=kernel_params(20),
        cost_estimate=cost(
            4 * length * KV_HEADS * HEAD_DIM * columns,
            2 * (2 * length * columns + length * KV_HEADS * HEAD_DIM + 4 * columns * HEAD_DIM * KV_HEADS),
        ),
        name="weight_product",
    )(index, *grads, hid_own, hid_other)


def hidden_kernel(which_ref, own_ref, other_ref, own_proj_ref, other_proj_ref, out_ref):
    total = jnp.dot(own_ref[...], own_proj_ref[0], preferred_element_type=jnp.float32)
    total += jnp.dot(other_ref[...], other_proj_ref[0], preferred_element_type=jnp.float32)
    out_ref[...] = total.astype(out_ref.dtype)


def hidden_product(which, own, other, projection):
    rows, half = own.shape
    width = projection.shape[1]
    columns = math.gcd(width, 1024)
    halves = projection.reshape(2, half, width)
    spec = pltpu.PrefetchScalarGridSpec(
        num_scalar_prefetch=1,
        grid=(width // columns,),
        in_specs=[
            pl.BlockSpec((rows, half), lambda i, w: (0, 0)),
            pl.BlockSpec((rows, half), lambda i, w: (0, 0)),
            pl.BlockSpec((1, half, columns), lambda i, w: (w[0], 0, i)),
            pl.BlockSpec((1, half, columns), lambda i, w: (1 - w[0], 0, i)),
        ],
        out_specs=pl.BlockSpec((rows, columns), lambda i, w: (0, i)),
    )
    return pl.pallas_call(
        hidden_kernel,
        grid_spec=spec,
        out_shape=struct((rows, width)),
        compiler_params=kernel_params(16),
        cost_estimate=cost(4 * rows * half * width, 2 * projection.size + 4 * rows * width),
        name="hidden_product",
    )(which, own, other, halves, halves)


AXES = ("dp", "group", "side")


def paired_body(hidden_rows, query_rows, out_grad, projection, packing_plan, document_ids):
    rows, width = hidden_rows.shape
    dp = lax.axis_size("dp")
    ctx = KV_HEADS * SIDES
    a, group, side = (lax.axis_index(name) for name in AXES)
    block_id = group * SIDES + side
    send = rows // dp
    length = rows * ctx
    which = jnp.bitwise_xor(side, a % SIDES)
    index = jnp.stack([which, group, side, a // SIDES]).astype(jnp.int32)
    group_index = group.reshape(1)

    def move(value, target):
        flat = lambda i, g, p: (i * KV_HEADS + g) * SIDES + p
        moves = [
            (flat(i, g, p), flat(*target(i, g, p)))
            for i in range(dp)
            for g in range(KV_HEADS)
            for p in range(SIDES)
        ]
        return lax.ppermute(value, AXES, moves)

    def spread(pieces):
        return [pieces[0]] + [move(pieces[e], lambda i, g, p, e=e: (i, g ^ e, p)) for e in range(1, KV_HEADS)]

    other_side = lambda i, g, p: (i, g, 1 - p)
    scatter = lambda value, axes: lax.all_to_all(value, axes, split_axis=0, concat_axis=0, tiled=True)

    grads_in = split_columns(group_index, out_grad)
    packing_plan, grads_in = lax.optimization_barrier((packing_plan, grads_in))
    grads_in = spread(grads_in)
    slot = block_id * rows + a * send + jnp.arange(send, dtype=jnp.int32)
    cosine, sine = rotary_tables(slot, HEAD_DIM)
    qkv_pieces, hid_pieces = pack_rows(dp, packing_plan, query_rows, hidden_rows, cosine, sine, projection)
    qkv = scatter(qkv_pieces, AXES[:2])
    kv_other = move(qkv[:, :, query_rows.shape[1] // KV_HEADS :], other_side)
    qkv, hid_pieces = lax.optimization_barrier((qkv, hid_pieces))
    hid = scatter(hid_pieces, AXES[:2])

    *outputs, keep, give = attend(dp, index, qkv, kv_other, grads_in, document_ids)
    recv = move(give, other_side)
    cosine, sine = rotary_tables(jnp.arange(length, dtype=jnp.int32), HEAD_DIM)
    cosine = jnp.where(which == 0, jnp.concatenate([cosine, cosine], axis=1), 1.0)
    sine = jnp.where(which == 0, jnp.concatenate([sine, -sine], axis=1), 0.0)
    piece = combine(dp, index, keep, recv, cosine, sine)
    shift = lambda value, e: move(value, lambda i, g, p: (i, g ^ e, p))
    near = shift(piece, 1)
    far_piece, hid = lax.optimization_barrier((piece, hid))
    hid_own = hid.reshape(length // SIDES, width // KV_HEADS)
    hid_other = move(hid_own, other_side)
    grads = [piece, near, shift(far_piece, 2)]
    grads.append(shift(grads[2], 1))

    outputs, *early = lax.optimization_barrier((outputs, *grads[:3]))
    grads = [*early, grads[3]]
    back = spread(outputs)
    products = product(dp, index, grads, hid_own, hid_other)
    own_rows, other_rows = products[dp], products[dp + 1]
    other_half = move(other_rows, other_side)
    half = dp // SIDES
    blocks = []
    for ey in (1, 0):
        for ek in range(half):
            target = lambda i, g, p, ek=ek, ey=ey: ((p ^ (i % SIDES)) * half + ((i // SIDES) ^ ek), g, p ^ ey)
            blocks.append(move(products[ek * SIDES + ey], target))

    hidden_grad = hidden_product(which.reshape(1), own_rows, other_half, projection)
    weight_grad = functools.reduce(jnp.add, [b.astype(jnp.float32) for b in blocks]) / dp

    back, hidden_grad = lax.optimization_barrier((back, hidden_grad))
    attended, query_grad = join_columns(group_index, back, 2)
    return (attended, query_grad, hidden_grad, weight_grad)


def paired(mesh):
    dp, ctx = mesh.shape["dp"], mesh.shape["ctx"]
    return ctx == KV_HEADS * SIDES and dp in (2, 4, 8)


def solution(mesh):
    if paired(mesh):
        body = paired_body
        inner = Mesh(mesh.devices.reshape(mesh.shape["dp"], KV_HEADS, SIDES), AXES)
        ctx = AXES[1:]
    else:
        body = general_body
        inner = mesh
        ctx = ("ctx",)
    rows = P(("dp", *ctx), None)
    step = jax.shard_map(
        body,
        mesh=inner,
        in_specs=(rows, rows, rows, P(), rows, P("dp", None)),
        out_specs=(rows, rows, rows, P("dp", ctx)),
        check_vma=False,
    )
    if body is general_body:
        return step

    return step
```
